256 devices in a mesh: outer: 16 (over z, core), inner: 16 (over y, x).
Axes of the slice: x: 4, y: 4, z: 8, core: 2. Of those that a mesh axis runs over, the one named last changes fastest.
Arguments:
- queries: bfloat16 [32768, 4096], P(('outer', 'inner')), may hold values from -48 to 48
- keys: bfloat16 [32768, 1024], P(('outer', 'inner')), may hold values from -20 to 20
- values: bfloat16 [32768, 1024], P(('outer', 'inner')), may hold values from -6 to 6
- ancestors: int32 [256, 8], replicated, may hold values from -1 to 255, as said below
- token_block: int32 [32768], replicated, may hold values from 0 to 255, as said below
- positions: int32 [32768], replicated, may hold values from 0 to 1023, as said below
Outputs:
- attended: bfloat16 [32768, 4096], P(('outer', 'inner'))
The draws below stay inside these ranges and needn't reach their ends.
Inputs may be any that keep to these rules, and one draw needn't show every extreme that they name: `ancestors`: row b lists the blocks on the path from the root block 0 to block b, root first and b last, then -1; a parent has a smaller number than its child; some row lists 8 blocks. `token_block`: each aligned span of 128 tokens belongs to one block, and every block fills exactly one span; apart from block 0, no two blocks of one root path lie in the same aligned group of 2048 tokens. `positions`: a token's position is 128 times (the number of blocks on its block's root path minus 1) plus its offset within its span.
All inputs are finite; a program needn't handle non-finite values.
Results may differ from the reference program's by a relative error of at most 0.0065.
Values may be sent and summed in bfloat16 or wider, within the bound.
No kernel may reach another device: no remote copies, remote signals or barrier semaphores. Data moves between devices by JAX's collectives and lax.ppermute only.
A program may use at most 128 MiB of HBM per device.

```python
import jax
import jax.numpy as jnp
from jax import lax

HEADS = 32
KV_HEADS = 8
HEAD_DIM = 128
BLOCK = 128
ANC_MAX = 8
TOKENS = 32768
BLOCKS = 256
N_OUTER = 16


def paired_rows(key):
    query_key = jax.random.fold_in(key, 101)
    keys_key = jax.random.fold_in(key, 202)
    query_rows = jnp.clip(jax.random.normal(query_key, (TOKENS, HEADS, HEAD_DIM), jnp.float32), -6.0, 6.0)
    key_rows = jnp.clip(jax.random.normal(keys_key, (TOKENS, KV_HEADS, HEAD_DIM), jnp.float32), -6.0, 6.0)
    return (query_rows.reshape(TOKENS, HEADS * HEAD_DIM), key_rows.reshape(TOKENS, KV_HEADS * HEAD_DIM))


def tree_layout(key):
    block_total = TOKENS // BLOCK
    group_spans = block_total // N_OUTER
    trunk_len = min(ANC_MAX, block_total)
    pick_key = jax.random.fold_in(key, 505)
    order_key = jax.random.fold_in(key, 606)
    block_ids = jnp.arange(block_total, dtype=jnp.int32)
    group_of = block_ids % N_OUTER
    local_of = block_ids // N_OUTER
    group_seeds = jax.random.split(order_key, N_OUTER)
    shuffles = jax.vmap(lambda one_seed: jax.random.permutation(one_seed, group_spans))(group_seeds).astype(jnp.int32)
    span_of_block = (group_of * group_spans + shuffles[group_of, local_of]).astype(jnp.int32)
    span_blocks = jnp.zeros((block_total,), jnp.int32).at[span_of_block].set(block_ids)
    group_bits = jnp.left_shift(jnp.ones((block_total,), jnp.int32), group_of)
    noise = jax.random.randint(pick_key, (block_total, block_total), 0, 8192, jnp.int32)

    def attach(carried, current):
        depths, parents, masks = carried
        own_bit = group_bits[current]
        eligible = (block_ids < current) & (depths < ANC_MAX) & (masks & own_bit == 0)
        ranked = jnp.where(eligible, (depths * 2048 + noise[current]) * block_total + block_ids, -1)
        parent = jnp.argmax(ranked).astype(jnp.int32)
        parent = jnp.where(current < trunk_len, current - 1, parent)
        safe_parent = jnp.maximum(parent, 0)
        own_depth = jnp.where(current == 0, 1, depths[safe_parent] + 1)
        own_mask = jnp.where(current == 0, 0, masks[safe_parent] | own_bit)
        return ((depths.at[current].set(own_depth), parents.at[current].set(parent), masks.at[current].set(own_mask)), None)
    start_state = (jnp.zeros((block_total,), jnp.int32), jnp.zeros((block_total,), jnp.int32), jnp.zeros((block_total,), jnp.int32))
    (depths, parents, masks), ignored = lax.scan(attach, start_state, block_ids)
    chain_list = [block_ids]
    for hop_index in range(ANC_MAX - 1):
        latest = chain_list[-1]
        chain_list.append(jnp.where(latest >= 0, parents[jnp.maximum(latest, 0)], -1))
    chained = jnp.stack(chain_list, axis=1)
    lookup = depths[:, None] - 1 - jnp.arange(ANC_MAX, dtype=jnp.int32)[None, :]
    ancestry = jnp.where(lookup >= 0, jnp.take_along_axis(chained, jnp.maximum(lookup, 0), axis=1), -1)
    token_ids = jnp.arange(TOKENS, dtype=jnp.int32)
    token_blocks = span_blocks[token_ids // BLOCK]
    places = (depths[token_blocks] - 1) * BLOCK + token_ids % BLOCK
    return (ancestry.astype(jnp.int32), token_blocks.astype(jnp.int32), places.astype(jnp.int32))


def draw_queries(key, part):
    return paired_rows(key)[0].astype(jnp.bfloat16)


def draw_keys(key, part):
    return paired_rows(key)[1].astype(jnp.bfloat16)


def draw_ancestors(key, part):
    return tree_layout(key)[0]


def draw_token_block(key, part):
    return tree_layout(key)[1]


def draw_positions(key, part):
    return tree_layout(key)[2]


def shard_levels(rng, shape, cuts, least, largest):
    level, own = 1.0, jax.random.fold_in(rng, 6)
    for dim, blocks in cuts:
        draws = jnp.exp(jax.random.uniform(jax.random.fold_in(own, dim), (blocks,), jnp.float32, least / len(cuts), largest / len(cuts)))
        level = level * jnp.repeat(draws, shape[dim] // blocks).reshape([-1 if axis == dim else 1 for axis in range(len(shape))])
    return level


def centred(stream_key, shape, width, bound, shards=(), kind=jnp.bfloat16):
    drawn = width * jax.random.normal(stream_key, shape, jnp.float32)
    if shards:
        drawn = drawn * shard_levels(stream_key, shape, shards, -0.22, 0.18)
    return jnp.clip(drawn, -bound, bound).astype(kind)


def setup_inputs(seed: int = 0) -> dict:
    streams_of = jax.random.split(jax.random.key(seed), 7)
    return {
        "queries": draw_queries(jax.random.fold_in(streams_of[6], 71), 0),
        "keys": draw_keys(jax.random.fold_in(streams_of[6], 71), 0),
        "values": centred(streams_of[2], (TOKENS, KV_HEADS * HEAD_DIM), 1.0, 6.0, ((0, 256),)),
        "ancestors": draw_ancestors(jax.random.fold_in(streams_of[6], 71), 0),
        "token_block": draw_token_block(jax.random.fold_in(streams_of[6], 71), 0),
        "positions": draw_positions(jax.random.fold_in(streams_of[6], 71), 0),
    }


ROTARY_BASE = 500000.0


def rotate(matrix, places, head_count):
    row_count = matrix.shape[0]
    head_width = matrix.shape[1] // head_count
    half_width = head_width // 2
    inverse = ROTARY_BASE ** (-2.0 * jnp.arange(half_width, dtype=jnp.float32) / head_width)
    angles = places.astype(jnp.float32)[:, None] * inverse[None, :]
    cosine = jnp.cos(angles)[:, None, :]
    sine_part = jnp.sin(angles)[:, None, :]
    unfolded = matrix.astype(jnp.float32).reshape(row_count, head_count, head_width)
    leading = unfolded[:, :, :half_width]
    trailing = unfolded[:, :, half_width:]
    turned = jnp.concatenate([leading * cosine - trailing * sine_part, trailing * cosine + leading * sine_part], axis=2)
    return turned.reshape(row_count, head_count * head_width).astype(jnp.bfloat16)


def reference(queries, keys, values, ancestors, token_block, positions):
    rot_q = rotate(queries, positions, HEADS)
    rot_k = rotate(keys, positions, KV_HEADS)
    group_size = HEADS // KV_HEADS
    block_ids = jnp.arange(BLOCKS, dtype=jnp.int32)
    span_blocks = token_block[::BLOCK]
    span_index = jnp.arange(BLOCKS, dtype=jnp.int32)
    span_of = jnp.sum(jnp.where(span_blocks[:, None] == block_ids[None, :], span_index[:, None], 0), axis=0).astype(jnp.int32)
    offsets = jnp.arange(BLOCK, dtype=jnp.int32)
    scaling = HEAD_DIM ** -0.5

    def one_span(span_id):
        lineage = ancestors[span_blocks[span_id]]
        living = lineage >= 0
        key_spans = span_of[jnp.maximum(lineage, 0)]
        key_index = (key_spans[:, None] * BLOCK + offsets[None, :]).reshape(-1).astype(jnp.int32)
        key_rows = rot_k[key_index].reshape(ANC_MAX * BLOCK, KV_HEADS, HEAD_DIM).astype(jnp.float32)
        value_rows = values[key_index].reshape(ANC_MAX * BLOCK, KV_HEADS, HEAD_DIM).astype(jnp.float32)
        key_places = positions[key_index]
        query_places = lax.dynamic_slice_in_dim(positions, (span_id * BLOCK).astype(jnp.int32), BLOCK)
        query_rows = lax.dynamic_slice_in_dim(rot_q, (span_id * BLOCK).astype(jnp.int32), BLOCK)
        query_rows = query_rows.reshape(BLOCK, KV_HEADS, group_size, HEAD_DIM).astype(jnp.float32)
        allowed = jnp.repeat(living, BLOCK)[None, :] & (key_places[None, :] <= query_places[:, None])
        scores = jnp.einsum("tkgd,ukd->tkgu", query_rows, key_rows) * scaling
        wide_mask = allowed[:, None, None, :]
        top_score = jnp.max(jnp.where(wide_mask, scores, -jnp.inf), axis=3)
        weights = jnp.where(wide_mask, jnp.exp(scores - top_score[..., None]), 0.0)
        totals = jnp.sum(weights, axis=3)
        rounded = lax.optimization_barrier(weights.astype(jnp.bfloat16)).astype(jnp.float32)
        mixed = jnp.einsum("tkgu,ukd->tkgd", rounded, value_rows)
        return (mixed / totals[..., None]).reshape(BLOCK, HEADS * HEAD_DIM).astype(jnp.bfloat16)

    spans_out = lax.map(one_span, jnp.arange(BLOCKS, dtype=jnp.int32))
    return spans_out.reshape(TOKENS, HEADS * HEAD_DIM)
```

```python
import functools

import jax
import jax.numpy as jnp
import numpy as np
from jax import lax
from jax.experimental import pallas as pl
from jax.experimental.pallas import tpu as pltpu
from jax.sharding import Mesh
from jax.sharding import PartitionSpec as P

HEADS = 32
KV_HEADS = 8
GROUP = HEADS // KV_HEADS
HEAD_DIM = 128
BLOCK = 128
ANC_MAX = 8
SLOTS = ANC_MAX - 1
DEVICES = 256
ROTARY_BASE = 500000.0
ALL_AXES = ("z", "c", "i")
NEG = -1e30
EXP2_SCALE = float(HEAD_DIM**-0.5 * np.log2(np.e))


def inverse_row():
    half = HEAD_DIM // 2
    inv = (ROTARY_BASE ** (-2.0 * np.arange(half, dtype=np.float64) / HEAD_DIM)).astype(np.float32)
    return np.concatenate([inv, inv])[None, :]


def turn(x, cosine, sine):
    return (x * cosine + pltpu.roll(x, HEAD_DIM // 2, 1) * sine).astype(jnp.bfloat16)


def spread_kernel(base_ref, inv_ref, k_ref, v_ref, send_ref, cos_ref, sin_ref, own_ref):
    rows = lax.broadcasted_iota(jnp.int32, (BLOCK, HEAD_DIM), 0) + base_ref[0]
    lanes = lax.broadcasted_iota(jnp.int32, (BLOCK, HEAD_DIM), 1)
    angles = rows.astype(jnp.float32) * inv_ref[...]
    cosine = jnp.cos(angles)
    sine = jnp.sin(angles)
    sine = jnp.where(lanes < HEAD_DIM // 2, -sine, sine)
    cos_ref[...] = cosine
    sin_ref[...] = sine
    for h in range(KV_HEADS):
        cols = slice(h * HEAD_DIM, (h + 1) * HEAD_DIM)
        turned = turn(k_ref[:, cols].astype(jnp.float32), cosine, sine)
        own_ref[:, cols] = turned
        plain = v_ref[:, cols]
        for high in range(2):
            for low in range(8):
                t = (high * 8 + low) * 8
                send_ref[low, h, 0, high] = turned[t : t + 8]
                send_ref[low, h, 1, high] = plain[t : t + 8]


def pick_kernel(count, idx_ref, src_ref, out_ref):
    def one(d, carry):
        for j in range(count):
            out_ref[d, j] = src_ref[idx_ref[d * count + j]]
        return carry

    lax.fori_loop(0, out_ref.shape[0], one, 0)


def attend_kernel(alive_ref, cos_ref, sin_ref, q_ref, ko_ref, vo_ref, ka_ref, va_ref, out_ref):
    cosine = cos_ref[...]
    sine = sin_ref[...]
    parts = [
        turn(q_ref[:, g * HEAD_DIM : (g + 1) * HEAD_DIM].astype(jnp.float32), cosine, sine)
        for g in range(GROUP)
    ]
    q = jnp.concatenate(parts, axis=0)
    dims = (((1,), (1,)), ((), ()))
    far = lax.dot_general(q, ka_ref[...], dims, preferred_element_type=jnp.float32)
    near = lax.dot_general(q, ko_ref[...], dims, preferred_element_type=jnp.float32)
    keys = ka_ref.shape[0]
    column = lax.broadcasted_iota(jnp.int32, (1, keys), 1)
    slot = (column // 64) % SLOTS
    far = far + jnp.where(slot < alive_ref[0], 0.0, NEG)
    row = lax.broadcasted_iota(jnp.int32, near.shape, 0) % BLOCK
    col = lax.broadcasted_iota(jnp.int32, near.shape, 1)
    near = jnp.where(col <= row, near, NEG)
    top = jnp.maximum(
        jnp.max(far, axis=1, keepdims=True), jnp.max(near, axis=1, keepdims=True)
    )
    far_w = jnp.exp2((far - top) * EXP2_SCALE)
    near_w = jnp.exp2((near - top) * EXP2_SCALE)
    total = jnp.sum(far_w, axis=1, keepdims=True) + jnp.sum(near_w, axis=1, keepdims=True)
    mixed = jnp.dot(far_w.astype(jnp.bfloat16), va_ref[...], preferred_element_type=jnp.float32)
    mixed += jnp.dot(near_w.astype(jnp.bfloat16), vo_ref[...], preferred_element_type=jnp.float32)
    done = (mixed / total).astype(jnp.bfloat16)
    for g in range(GROUP):
        out_ref[:, g * HEAD_DIM : (g + 1) * HEAD_DIM] = done[g * BLOCK : (g + 1) * BLOCK]


SMEM = pl.BlockSpec(memory_space=pltpu.SMEM)


def shards(queries, keys, values, ancestors, token_block, positions):
    bf = jnp.bfloat16
    me = lax.axis_index(ALL_AXES)
    base = lax.dynamic_slice_in_dim(positions, me * BLOCK, 1)
    span_blocks = token_block.reshape(DEVICES, BLOCK)[:, 0]
    ids = jnp.arange(DEVICES, dtype=jnp.int32)
    span_of = jnp.sum(jnp.where(span_blocks[:, None] == ids[None, :], ids[:, None], 0), axis=0)
    lineage = ancestors[span_blocks]
    depth = jnp.sum((lineage >= 0).astype(jnp.int32), axis=1)
    spans = span_of[jnp.maximum(lineage, 0)][:, :SLOTS]
    alive = lax.dynamic_slice_in_dim(depth - 1, me, 1)

    send, cosine, sine, own_k = pl.pallas_call(
        spread_kernel,
        out_shape=(
            jax.ShapeDtypeStruct((8, KV_HEADS, 2, 2, 8, HEAD_DIM), bf),
            jax.ShapeDtypeStruct((BLOCK, HEAD_DIM), jnp.float32),
            jax.ShapeDtypeStruct((BLOCK, HEAD_DIM), jnp.float32),
            jax.ShapeDtypeStruct((BLOCK, KV_HEADS * HEAD_DIM), bf),
        ),
        in_specs=[SMEM] + [pl.BlockSpec(memory_space=pltpu.VMEM)] * 3,
    )(base, jnp.asarray(inverse_row()), keys, values)
    chunks = lax.all_to_all(
        send.reshape(DEVICES, 8, HEAD_DIM), ALL_AXES, 0, 0, tiled=True
    )
    packed = pl.pallas_call(
        functools.partial(pick_kernel, SLOTS),
        out_shape=jax.ShapeDtypeStruct((DEVICES, SLOTS, 8, HEAD_DIM), bf),
        in_specs=[SMEM, pl.BlockSpec(memory_space=pltpu.VMEM)],
    )(spans.reshape(-1), chunks)
    got = lax.all_to_all(
        packed.reshape(DEVICES, SLOTS * 8, HEAD_DIM), ALL_AXES, 0, 0, tiled=True
    )
    got = got.reshape(8, KV_HEADS, 2, 2, SLOTS, 8, HEAD_DIM).transpose(2, 1, 3, 4, 0, 5, 6)
    got = got.reshape(2, KV_HEADS, SLOTS * BLOCK, HEAD_DIM)
    return attend(alive, cosine, sine, queries, own_k, values, got)


def attend(alive, cosine, sine, queries, own_k, values, got):
    table = pl.BlockSpec((BLOCK, HEAD_DIM), lambda h: (0, 0))
    head = pl.BlockSpec((BLOCK, HEAD_DIM), lambda h: (0, h))
    heads = pl.BlockSpec((BLOCK, GROUP * HEAD_DIM), lambda h: (0, h))
    far_k = pl.BlockSpec((None, None, SLOTS * BLOCK, HEAD_DIM), lambda h: (0, h, 0, 0))
    far_v = pl.BlockSpec((None, None, SLOTS * BLOCK, HEAD_DIM), lambda h: (1, h, 0, 0))
    return pl.pallas_call(
        attend_kernel,
        grid=(KV_HEADS,),
        out_shape=jax.ShapeDtypeStruct(queries.shape, jnp.bfloat16),
        in_specs=[SMEM, table, table, heads, head, head, far_k, far_v],
        out_specs=heads,
    )(alive, cosine, sine, queries, own_k, values, got, got)


def solution(mesh):
    fine = Mesh(mesh.devices.reshape(8, 2, 16), ALL_AXES)
    rows = P(ALL_AXES, None)
    return jax.shard_map(
        shards,
        mesh=fine,
        in_specs=(rows, rows, rows, P(), P(), P()),
        out_specs=rows,
        check_vma=False,
    )
```

```python
import functools

import jax
import jax.numpy as jnp
import numpy as np
from jax import lax
from jax.experimental import pallas as pl
from jax.experimental.pallas import tpu as pltpu
from jax.sharding import Mesh
from jax.sharding import PartitionSpec as P

HEADS = 32
KV_HEADS = 8
GROUP = HEADS // KV_HEADS
HEAD_DIM = 128
BLOCK = 128
ANC_MAX = 8
SLOTS = ANC_MAX - 1
DEVICES = 256
PLANES = 8
CAP = 40
HALF = BLOCK // 2
PACK = (GROUP + 2) * HEAD_DIM
ROTARY_BASE = 500000.0
AXES = ("z", "c", "y", "xh", "xl")
HEAD_AXES = ("y", "xl")
NEG = -1e30
EXP2_SCALE = float(HEAD_DIM**-0.5 * np.log2(np.e))

SMEM = pl.BlockSpec(memory_space=pltpu.SMEM)
VMEM = pl.BlockSpec(memory_space=pltpu.VMEM)


def inverse_row():
    half = HEAD_DIM // 2
    inv = (ROTARY_BASE ** (-2.0 * np.arange(half, dtype=np.float64) / HEAD_DIM)).astype(np.float32)
    return np.concatenate([inv, inv])[None, :]


def turn(x, cosine, sine):
    x = x.astype(jnp.float32)
    return (x * cosine + pltpu.roll(x, HEAD_DIM // 2, 1) * sine).astype(jnp.bfloat16)


def spread_kernel(base_ref, inv_ref, k_ref, v_ref, send_ref, cos_ref, sin_ref, own_ref):
    rows = lax.broadcasted_iota(jnp.int32, (BLOCK, HEAD_DIM), 0) + base_ref[0]
    lanes = lax.broadcasted_iota(jnp.int32, (BLOCK, HEAD_DIM), 1)
    angles = rows.astype(jnp.float32) * inv_ref[...]
    cosine = jnp.cos(angles)
    sine = jnp.sin(angles)
    sine = jnp.where(lanes < HEAD_DIM // 2, -sine, sine)
    cos_ref[...] = cosine
    sin_ref[...] = sine
    for h in range(KV_HEADS):
        cols = slice(h * HEAD_DIM, (h + 1) * HEAD_DIM)
        turned = turn(k_ref[:, cols], cosine, sine)
        own_ref[:, cols] = turned
        plain = v_ref[:, cols]
        for high in range(2):
            for low in range(8):
                t = (high * 8 + low) * 8
                send_ref[low, 0, h // 2, high, h % 2] = turned[t : t + 8]
                send_ref[low, 1, h // 2, high, h % 2] = plain[t : t + 8]


def bundle_kernel(cos_ref, sin_ref, q_ref, k_ref, v_ref, out_ref):
    for g in range(GROUP):
        cols = slice(g * HEAD_DIM, (g + 1) * HEAD_DIM)
        out_ref[:, cols] = turn(q_ref[:, cols], cos_ref[...], sin_ref[...])
    out_ref[:, GROUP * HEAD_DIM : (GROUP + 1) * HEAD_DIM] = k_ref[...]
    out_ref[:, (GROUP + 1) * HEAD_DIM :] = v_ref[...]


def plan_kernel(where_ref, row_ref, col_ref, anc_ref, picks_ref, slots_ref, count_ref):
    n = DEVICES
    f32, bf, i32 = jnp.float32, jnp.bfloat16, jnp.int32
    row = row_ref[...]
    anc = anc_ref[...]
    lane = lax.broadcasted_iota(i32, (n, n), 1)
    sub = lax.broadcasted_iota(i32, (n, n), 0)
    depth = jnp.sum((anc >= 0).astype(i32), axis=1, keepdims=True)
    holds = jnp.zeros((n, n), f32)
    for j in range(SLOTS):
        entry = jnp.where(j < depth - 1, anc[:, j : j + 1], -1)
        holds = jnp.where(entry == row, 1.0, holds)
    block_at = (col_ref[...] == lane).astype(f32).astype(bf)
    plane8 = lax.broadcasted_iota(i32, (PLANES, n), 0)
    lane8 = lax.broadcasted_iota(i32, (PLANES, n), 1)
    in_plane = (lane8 // (n // PLANES) == plane8).astype(f32).astype(bf)
    blocks = jnp.dot(in_plane, block_at, preferred_element_type=f32)
    need = jnp.dot(blocks.astype(bf), holds.astype(bf), preferred_element_type=f32) > 0.5
    needed = need.astype(f32)
    upto = (sub <= lane).astype(f32).astype(bf)
    ranks = jnp.dot(needed.astype(bf), upto, preferred_element_type=f32)
    count_ref[...] = jnp.max(ranks, axis=(0, 1), keepdims=True).astype(i32)
    ranks = ranks - 1.0
    wanted = lax.broadcasted_iota(i32, (CAP, n), 0).astype(f32)
    span = lax.broadcasted_iota(i32, (CAP, n), 1).astype(f32)
    for z in range(PLANES):
        hit = (ranks[z : z + 1] == wanted) & (needed[z : z + 1] > 0.5)
        picks_ref[:, z : z + 1] = jnp.sum(
            jnp.where(hit, span, 0.0), axis=1, keepdims=True
        ).astype(i32)
    z, c, xh = where_ref[0], where_ref[1], where_ref[2]
    member = plane8
    mine = z * 32 + c * 16 + (member // 2) * 4 + xh * 2 + member % 2
    own_block = jnp.dot(
        (lane8 == mine).astype(f32).astype(bf), block_at, preferred_element_type=f32
    )
    path = jnp.dot(
        own_block.astype(bf), anc.astype(f32).astype(bf), preferred_element_type=f32
    ).astype(i32)
    my_rank = jnp.sum(jnp.where(plane8 == z, ranks, 0.0), axis=0, keepdims=True)
    for j in range(SLOTS):
        slot = jnp.sum(
            jnp.where(path[:, j : j + 1] == row, my_rank, 0.0), axis=1, keepdims=True
        ).astype(i32)
        slots_ref[:, j : j + 1] = jnp.clip(slot, 0, CAP - 1)
    slots_ref[:, SLOTS:] = jnp.sum((path >= 0).astype(i32), axis=1, keepdims=True) - 1


def pack_kernel(where_ref, picks_ref, src_ref, *out_refs):
    z = where_ref[0]

    def one(k, carry):
        for d in range(PLANES):
            out_refs[d][k] = src_ref[picks_ref[k, (z + d) % PLANES]]
        return carry

    lax.fori_loop(0, CAP, one, 0)


def pick_kernel(idx_ref, src_ref, out_ref):
    def one(d, carry):
        for j in range(SLOTS):
            out_ref[d, j] = src_ref[idx_ref[d, j]]
        return carry

    lax.fori_loop(0, out_ref.shape[0], one, 0)


def attention(q, near_k, near_v, far_k, far_v, alive, period):
    dims = (((1,), (1,)), ((), ()))
    far = lax.dot_general(q, far_k, dims, preferred_element_type=jnp.float32)
    near = lax.dot_general(q, near_k, dims, preferred_element_type=jnp.float32)
    column = lax.broadcasted_iota(jnp.int32, (1, far_k.shape[0]), 1)
    slot = (column // period) % SLOTS
    far = far + jnp.where(slot < alive, 0.0, NEG)
    row = lax.broadcasted_iota(jnp.int32, near.shape, 0) % BLOCK
    col = lax.broadcasted_iota(jnp.int32, near.shape, 1)
    near = jnp.where(col <= row, near, NEG)
    top = jnp.maximum(
        jnp.max(far, axis=1, keepdims=True), jnp.max(near, axis=1, keepdims=True)
    )
    far_w = jnp.exp2((far - top) * EXP2_SCALE)
    near_w = jnp.exp2((near - top) * EXP2_SCALE)
    total = jnp.sum(far_w, axis=1, keepdims=True) + jnp.sum(near_w, axis=1, keepdims=True)
    mixed = jnp.dot(far_w.astype(jnp.bfloat16), far_v, preferred_element_type=jnp.float32)
    mixed += jnp.dot(near_w.astype(jnp.bfloat16), near_v, preferred_element_type=jnp.float32)
    return (mixed / total).astype(jnp.bfloat16)


def attend_one(x_ref, far_k, far_v, alive, period, out_ref):
    cols = [slice(g * HEAD_DIM, (g + 1) * HEAD_DIM) for g in range(GROUP + 2)]
    q = jnp.concatenate([x_ref[:, cols[g]] for g in range(GROUP)], axis=0)
    done = attention(q, x_ref[:, cols[GROUP]], x_ref[:, cols[GROUP + 1]], far_k, far_v, alive, period)
    for g in range(GROUP):
        out_ref[:, cols[g]] = done[g * BLOCK : (g + 1) * BLOCK]


def span_kernel(where_ref, slots_ref, x_ref, a0_ref, a1_ref, b0_ref, b1_ref, out_ref, k_ref, v_ref):
    m = pl.program_id(0)

    def fill(dst_ref, first_ref, second_ref):
        for j in range(SLOTS):
            slot = slots_ref[m, j]
            dst_ref[j * BLOCK : j * BLOCK + HALF] = first_ref[slot]
            dst_ref[j * BLOCK + HALF : (j + 1) * BLOCK] = second_ref[slot]

    @pl.when(where_ref[1] == 0)
    def _():
        fill(k_ref, a0_ref, a1_ref)
        fill(v_ref, b0_ref, b1_ref)

    @pl.when(where_ref[1] != 0)
    def _():
        fill(k_ref, b0_ref, b1_ref)
        fill(v_ref, a0_ref, a1_ref)

    attend_one(x_ref, k_ref[...], v_ref[...], slots_ref[m, SLOTS], BLOCK, out_ref)


def head_kernel(alive_ref, x_ref, k_ref, v_ref, out_ref):
    attend_one(x_ref, k_ref[...], v_ref[...], alive_ref[0], HALF, out_ref)


def quick(where, picks, slots, chunks, bundle, *unused):
    bf = jnp.bfloat16
    members = lax.all_to_all(bundle, HEAD_AXES, 0, 0, tiled=True)
    packs = pl.pallas_call(
        pack_kernel,
        out_shape=[jax.ShapeDtypeStruct((CAP, 8, HEAD_DIM), bf)] * PLANES,
        in_specs=[SMEM, SMEM, VMEM],
    )(where, picks, chunks)
    got = list(packs)
    for d in (4, 3, 5, 2, 6, 1, 7):
        got[d] = lax.ppermute(packs[d], "z", [(i, (i + d) % PLANES) for i in range(PLANES)])
    a0 = jnp.stack(got, axis=1).reshape(CAP, HALF, HEAD_DIM)
    swap = [(0, 1), (1, 0)]
    a1 = lax.ppermute(a0, "xh", swap)
    b0 = lax.ppermute(a0, "c", swap)
    b1 = lax.ppermute(a1, "c", swap)
    whole = pl.BlockSpec((CAP, HALF, HEAD_DIM), lambda m: (0, 0, 0))
    out = pl.pallas_call(
        span_kernel,
        grid=(KV_HEADS,),
        out_shape=jax.ShapeDtypeStruct((KV_HEADS, BLOCK, GROUP * HEAD_DIM), bf),
        in_specs=[SMEM, SMEM, pl.BlockSpec((None, BLOCK, PACK), lambda m: (m, 0, 0))] + [whole] * 4,
        out_specs=pl.BlockSpec((None, BLOCK, GROUP * HEAD_DIM), lambda m: (m, 0, 0)),
        scratch_shapes=[pltpu.VMEM((SLOTS * BLOCK, HEAD_DIM), bf)] * 2,
    )(where, slots, members, a0, a1, b0, b1)
    back = lax.all_to_all(out, HEAD_AXES, 0, 0, tiled=True)
    return back.transpose(1, 0, 2).reshape(BLOCK, HEADS * HEAD_DIM)


def general(where, picks, slots, chunks, bundle, span_blocks, ancestors):
    bf = jnp.bfloat16
    ids = jnp.arange(DEVICES, dtype=jnp.int32)
    span_of = jnp.sum(jnp.where(span_blocks[:, None] == ids[None, :], ids[:, None], 0), axis=0)
    lineage = ancestors[span_blocks]
    depth = jnp.sum((lineage >= 0).astype(jnp.int32), axis=1)
    spans = span_of[jnp.maximum(lineage, 0)]
    alive = lax.dynamic_slice_in_dim(depth - 1, lax.axis_index(AXES), 1)
    packed = pl.pallas_call(
        pick_kernel,
        out_shape=jax.ShapeDtypeStruct((DEVICES, SLOTS, 8, HEAD_DIM), bf),
        in_specs=[SMEM, VMEM],
    )(spans, chunks)
    got = lax.all_to_all(packed.reshape(DEVICES, SLOTS * 8, HEAD_DIM), AXES, 0, 0, tiled=True)
    got = got.reshape(8, 2, 4, 2, 2, SLOTS, 8, HEAD_DIM).transpose(1, 2, 4, 3, 5, 0, 6, 7)
    got = got.reshape(2, KV_HEADS, SLOTS * BLOCK, HEAD_DIM)
    far_k = pl.BlockSpec((None, None, SLOTS * BLOCK, HEAD_DIM), lambda h: (0, h, 0, 0))
    far_v = pl.BlockSpec((None, None, SLOTS * BLOCK, HEAD_DIM), lambda h: (1, h, 0, 0))
    return pl.pallas_call(
        head_kernel,
        grid=(KV_HEADS,),
        out_shape=jax.ShapeDtypeStruct((BLOCK, HEADS * HEAD_DIM), bf),
        in_specs=[SMEM, pl.BlockSpec((None, BLOCK, PACK), lambda h: (h, 0, 0)), far_k, far_v],
        out_specs=pl.BlockSpec((BLOCK, GROUP * HEAD_DIM), lambda h: (0, h)),
    )(alive, bundle, got, got)


def shards(queries, keys, values, ancestors, token_block, positions):
    bf, f32, i32 = jnp.bfloat16, jnp.float32, jnp.int32
    me = lax.axis_index(AXES)
    base = lax.dynamic_slice_in_dim(positions, me * BLOCK, 1)
    where = jnp.stack([lax.axis_index("z"), lax.axis_index("c"), lax.axis_index("xh")]).astype(i32)
    span_blocks = token_block.reshape(DEVICES, BLOCK)[:, 0]
    send, cosine, sine, own_k = pl.pallas_call(
        spread_kernel,
        out_shape=(
            jax.ShapeDtypeStruct((8, 2, 4, 2, 2, 8, HEAD_DIM), bf),
            jax.ShapeDtypeStruct((BLOCK, HEAD_DIM), f32),
            jax.ShapeDtypeStruct((BLOCK, HEAD_DIM), f32),
            jax.ShapeDtypeStruct((BLOCK, KV_HEADS * HEAD_DIM), bf),
        ),
        in_specs=[SMEM, VMEM, VMEM, VMEM],
    )(base, jnp.asarray(inverse_row()), keys, values)
    chunks = lax.all_to_all(send.reshape(DEVICES, 8, HEAD_DIM), AXES, 0, 0, tiled=True)
    table = pl.BlockSpec((BLOCK, HEAD_DIM), lambda h: (0, 0))
    head = pl.BlockSpec((BLOCK, HEAD_DIM), lambda h: (0, h))
    bundle = pl.pallas_call(
        bundle_kernel,
        grid=(KV_HEADS,),
        out_shape=jax.ShapeDtypeStruct((KV_HEADS, BLOCK, PACK), bf),
        in_specs=[table, table, pl.BlockSpec((BLOCK, GROUP * HEAD_DIM), lambda h: (0, h)), head, head],
        out_specs=pl.BlockSpec((None, BLOCK, PACK), lambda h: (h, 0, 0)),
        cost_estimate=pl.CostEstimate(flops=4 << 20, bytes_accessed=4 << 20, transcendentals=0),
    )(cosine, sine, queries, own_k, values)
    picks, slots, count = pl.pallas_call(
        plan_kernel,
        out_shape=(
            jax.ShapeDtypeStruct((CAP, PLANES), i32),
            jax.ShapeDtypeStruct((8, ANC_MAX), i32),
            jax.ShapeDtypeStruct((1, 1), i32),
        ),
        in_specs=[SMEM, VMEM, VMEM, VMEM],
        cost_estimate=pl.CostEstimate(flops=4 << 20, bytes_accessed=4 << 20, transcendentals=0),
    )(where, span_blocks[None, :], span_blocks[:, None], ancestors)
    fits = count[0, 0] <= CAP
    return lax.cond(
        fits, quick, general, where, picks, slots, chunks, bundle, span_blocks, ancestors
    )


def solution(mesh):
    fine = Mesh(mesh.devices.reshape(8, 2, 4, 2, 2), AXES)
    rows = P(AXES, None)
    return jax.shard_map(
        shards,
        mesh=fine,
        in_specs=(rows, rows, rows, P(), P(), P()),
        out_specs=rows,
        check_vma=False,
    )
```

```python
import functools

import jax
import jax.numpy as jnp
import numpy as np
from jax import lax
from jax.experimental import pallas as pl
from jax.experimental.pallas import tpu as pltpu
from jax.sharding import Mesh
from jax.sharding import PartitionSpec as P

HEADS = 32
KV_HEADS = 8
GROUP = HEADS // KV_HEADS
HEAD_DIM = 128
BLOCK = 128
ANC_MAX = 8
SLOTS = ANC_MAX - 1
DEVICES = 256
PLANES = 8
CAP = 40
HALF = BLOCK // 2
PARTS = 2
SHIFTS = ((0, 1, 7, 2), (6, 3, 5, 4))
GROUPS = len(SHIFTS)
PACK = (GROUP + 2) * HEAD_DIM
ROTARY_BASE = 500000.0
AXES = ("z", "c", "y", "xh", "xl")
HEAD_AXES = ("y", "xl")
NEG = -1e30
EXP2_SCALE = float(HEAD_DIM**-0.5 * np.log2(np.e))

SMEM = pl.BlockSpec(memory_space=pltpu.SMEM)
VMEM = pl.BlockSpec(memory_space=pltpu.VMEM)
VMEM_ONE = pl.BlockSpec((1, 1), lambda h: (0, 0))


def inverse_row():
    half = HEAD_DIM // 2
    inv = (ROTARY_BASE ** (-2.0 * np.arange(half, dtype=np.float64) / HEAD_DIM)).astype(np.float32)
    return np.concatenate([inv, inv])[None, :]


def turn(x, cosine, sine):
    x = x.astype(jnp.float32)
    return (x * cosine + pltpu.roll(x, HEAD_DIM // 2, 1) * sine).astype(jnp.bfloat16)


def spread_kernel(base_ref, inv_ref, k_ref, v_ref, send_ref, cos_ref, sin_ref, own_ref):
    rows = lax.broadcasted_iota(jnp.int32, (BLOCK, HEAD_DIM), 0) + base_ref[0]
    lanes = lax.broadcasted_iota(jnp.int32, (BLOCK, HEAD_DIM), 1)
    angles = rows.astype(jnp.float32) * inv_ref[...]
    cosine = jnp.cos(angles)
    sine = jnp.sin(angles)
    sine = jnp.where(lanes < HEAD_DIM // 2, -sine, sine)
    cos_ref[...] = cosine
    sin_ref[...] = sine
    for h in range(KV_HEADS):
        cols = slice(h * HEAD_DIM, (h + 1) * HEAD_DIM)
        turned = turn(k_ref[:, cols], cosine, sine)
        own_ref[:, cols] = turned
        plain = v_ref[:, cols]
        for high in range(2):
            for low in range(8):
                t = (high * 8 + low) * 8
                send_ref[low, 0, h // 2, high, h % 2] = turned[t : t + 8]
                send_ref[low, 1, h // 2, high, h % 2] = plain[t : t + 8]


def bundle_kernel(count_ref, cos_ref, sin_ref, q_ref, k_ref, v_ref, out_ref):
    for g in range(GROUP):
        cols = slice(g * HEAD_DIM, (g + 1) * HEAD_DIM)
        out_ref[:, cols] = turn(q_ref[:, cols], cos_ref[...], sin_ref[...])
    out_ref[:, GROUP * HEAD_DIM : (GROUP + 1) * HEAD_DIM] = k_ref[...]
    out_ref[:, (GROUP + 1) * HEAD_DIM :] = v_ref[...]


def plan_kernel(where_ref, row_ref, col_ref, anc_ref, picks_ref, slots_ref, count_ref):
    n = DEVICES
    f32, bf, i32 = jnp.float32, jnp.bfloat16, jnp.int32
    row = row_ref[...]
    anc = anc_ref[...]
    lane = lax.broadcasted_iota(i32, (n, n), 1)
    sub = lax.broadcasted_iota(i32, (n, n), 0)
    depth = jnp.sum((anc >= 0).astype(i32), axis=1, keepdims=True)
    holds = jnp.zeros((n, n), f32)
    for j in range(SLOTS):
        entry = jnp.where(j < depth - 1, anc[:, j : j + 1], -1)
        holds = jnp.where(entry == row, 1.0, holds)
    block_at = (col_ref[...] == lane).astype(f32).astype(bf)
    plane8 = lax.broadcasted_iota(i32, (PLANES, n), 0)
    lane8 = lax.broadcasted_iota(i32, (PLANES, n), 1)
    in_plane = (lane8 // (n // PLANES) == plane8).astype(f32).astype(bf)
    blocks = jnp.dot(in_plane, block_at, preferred_element_type=f32)
    need = jnp.dot(blocks.astype(bf), holds.astype(bf), preferred_element_type=f32) > 0.5
    needed = need.astype(f32)
    upto = (sub <= lane).astype(f32).astype(bf)
    ranks = jnp.dot(needed.astype(bf), upto, preferred_element_type=f32)
    count_ref[...] = jnp.max(ranks, axis=(0, 1), keepdims=True).astype(i32)
    ranks = ranks - 1.0
    wanted = lax.broadcasted_iota(i32, (CAP, n), 0).astype(f32)
    span = lax.broadcasted_iota(i32, (CAP, n), 1).astype(f32)
    for z in range(PLANES):
        hit = (ranks[z : z + 1] == wanted) & (needed[z : z + 1] > 0.5)
        picks_ref[:, z : z + 1] = jnp.sum(
            jnp.where(hit, span, 0.0), axis=1, keepdims=True
        ).astype(i32)
    z, c, xh = where_ref[0], where_ref[1], where_ref[2]
    member = plane8
    mine = z * 32 + c * 16 + (member // 2) * 4 + xh * 2 + member % 2
    own_block = jnp.dot(
        (lane8 == mine).astype(f32).astype(bf), block_at, preferred_element_type=f32
    )
    path = jnp.dot(
        own_block.astype(bf), anc.astype(f32).astype(bf), preferred_element_type=f32
    ).astype(i32)
    my_rank = jnp.sum(jnp.where(plane8 == z, ranks, 0.0), axis=0, keepdims=True)
    for j in range(SLOTS):
        slot = jnp.sum(
            jnp.where(path[:, j : j + 1] == row, my_rank, 0.0), axis=1, keepdims=True
        ).astype(i32)
        slots_ref[:, j : j + 1] = jnp.clip(slot, 0, CAP - 1)
    slots_ref[:, SLOTS:] = jnp.sum((path >= 0).astype(i32), axis=1, keepdims=True) - 1


def pack_kernel(where_ref, picks_ref, src_ref, *out_refs):
    z = where_ref[0]

    def one(k, carry):
        for d in range(PLANES):
            out_refs[d][k] = src_ref[picks_ref[k, (z + d) % PLANES]]
        return carry

    lax.fori_loop(0, CAP, one, 0)


def pick_kernel(idx_ref, src_ref, out_ref):
    def one(d, carry):
        for j in range(SLOTS):
            out_ref[d, j] = src_ref[idx_ref[d, j]]
        return carry

    lax.fori_loop(0, out_ref.shape[0], one, 0)


def attention(q, near_k, near_v, far_k, far_v, alive, period, first):
    dims = (((1,), (1,)), ((), ()))
    far = lax.dot_general(q, far_k, dims, preferred_element_type=jnp.float32)
    near = lax.dot_general(q, near_k, dims, preferred_element_type=jnp.float32)
    column = lax.broadcasted_iota(jnp.int32, (1, far_k.shape[0]), 1)
    slot = (column // period) % SLOTS
    far = far + jnp.where(slot < alive, 0.0, NEG)
    row = lax.broadcasted_iota(jnp.int32, near.shape, 0) % (q.shape[0] // GROUP) + first
    col = lax.broadcasted_iota(jnp.int32, near.shape, 1)
    near = jnp.where(col <= row, near, NEG)
    top = jnp.maximum(
        jnp.max(far, axis=1, keepdims=True), jnp.max(near, axis=1, keepdims=True)
    )
    far_w = jnp.exp2((far - top) * EXP2_SCALE)
    near_w = jnp.exp2((near - top) * EXP2_SCALE)
    total = jnp.sum(far_w, axis=1, keepdims=True) + jnp.sum(near_w, axis=1, keepdims=True)
    mixed = jnp.dot(far_w.astype(jnp.bfloat16), far_v, preferred_element_type=jnp.float32)
    mixed += jnp.dot(near_w.astype(jnp.bfloat16), near_v, preferred_element_type=jnp.float32)
    return (mixed / total).astype(jnp.bfloat16)


def attend_one(x_ref, far_k, far_v, alive, period, first, out_ref):
    rows = out_ref.shape[0]
    cols = [slice(g * HEAD_DIM, (g + 1) * HEAD_DIM) for g in range(GROUP + 2)]
    q = jnp.concatenate([x_ref[first : first + rows, cols[g]] for g in range(GROUP)], axis=0)
    near_k, near_v = x_ref[:, cols[GROUP]], x_ref[:, cols[GROUP + 1]]
    done = attention(q, near_k, near_v, far_k, far_v, alive, period, first)
    for g in range(GROUP):
        out_ref[:, cols[g]] = done[g * rows : (g + 1) * rows]


def span_kernel(first, where_ref, slots_ref, x_ref, *refs):
    far_refs, out_ref, k_ref, v_ref = refs[: 4 * GROUPS], refs[-3], refs[-2], refs[-1]
    m = pl.program_id(0)

    def fill(dst_ref, parts):
        for j in range(SLOTS):
            slot = slots_ref[m, j]
            at = j * BLOCK
            for part in parts:
                size = part.shape[1]
                dst_ref[at : at + size] = part[slot]
                at += size

    own, other = far_refs[: 2 * GROUPS], far_refs[2 * GROUPS :]

    @pl.when(where_ref[1] == 0)
    def _():
        fill(k_ref, own)
        fill(v_ref, other)

    @pl.when(where_ref[1] != 0)
    def _():
        fill(k_ref, other)
        fill(v_ref, own)

    attend_one(x_ref, k_ref[...], v_ref[...], slots_ref[m, SLOTS], BLOCK, first, out_ref)


def head_kernel(alive_ref, x_ref, k_ref, v_ref, out_ref):
    attend_one(x_ref, k_ref[...], v_ref[...], alive_ref[0], HALF, 0, out_ref)


def join_kernel(*refs):
    out_ref = refs[-1]
    rows = BLOCK // PARTS
    width = GROUP * HEAD_DIM
    for p in range(PARTS):
        for h in range(KV_HEADS):
            out_ref[p * rows : (p + 1) * rows, h * width : (h + 1) * width] = refs[p][h]


def quick(where, picks, slots, chunks, members):
    bf = jnp.bfloat16
    packs = pl.pallas_call(
        pack_kernel,
        out_shape=[jax.ShapeDtypeStruct((CAP, 8, HEAD_DIM), bf)] * PLANES,
        in_specs=[SMEM, SMEM, VMEM],
    )(where, picks, chunks)
    swap = [(0, 1), (1, 0)]
    got = {0: packs[0]}
    for shifts in SHIFTS:
        for d in shifts:
            if d:
                pairs = [(i, (i + d) % PLANES) for i in range(PLANES)]
                got[d] = lax.ppermute(packs[d], "z", pairs)
    own, other = [], []
    for shifts in SHIFTS:
        part = jnp.stack([got[d] for d in shifts], axis=1)
        own.append(part.reshape(CAP, 8 * len(shifts), HEAD_DIM))
    own += [lax.ppermute(part, "xh", swap) for part in own]
    other = [lax.ppermute(part, "c", swap) for part in own]
    outs = []
    rows = BLOCK // PARTS
    for p in range(PARTS):
        whole = [pl.BlockSpec(part.shape, lambda m: (0, 0, 0)) for part in own + other]
        out = pl.pallas_call(
            functools.partial(span_kernel, p * rows),
            grid=(KV_HEADS,),
            out_shape=jax.ShapeDtypeStruct((KV_HEADS, rows, GROUP * HEAD_DIM), bf),
            in_specs=[SMEM, SMEM, pl.BlockSpec((None, BLOCK, PACK), lambda m: (m, 0, 0))] + whole,
            out_specs=pl.BlockSpec((None, rows, GROUP * HEAD_DIM), lambda m: (m, 0, 0)),
            scratch_shapes=[pltpu.VMEM((SLOTS * BLOCK, HEAD_DIM), bf)] * 2,
            cost_estimate=pl.CostEstimate(
                flops=1 << 30, bytes_accessed=4 << 20, transcendentals=2 << 20
            ),
        )(where, slots, members, *own, *other)
        outs.append(lax.all_to_all(out, HEAD_AXES, 0, 0, tiled=True))
    return tuple(outs)


def join(outs, *unused):
    return pl.pallas_call(
        join_kernel,
        out_shape=jax.ShapeDtypeStruct((BLOCK, HEADS * HEAD_DIM), jnp.bfloat16),
        in_specs=[VMEM] * PARTS,
    )(*outs)


def general(outs, chunks, bundle, span_blocks, ancestors):
    bf = jnp.bfloat16
    ids = jnp.arange(DEVICES, dtype=jnp.int32)
    span_of = jnp.sum(jnp.where(span_blocks[:, None] == ids[None, :], ids[:, None], 0), axis=0)
    lineage = ancestors[span_blocks]
    depth = jnp.sum((lineage >= 0).astype(jnp.int32), axis=1)
    spans = span_of[jnp.maximum(lineage, 0)]
    alive = lax.dynamic_slice_in_dim(depth - 1, lax.axis_index(AXES), 1)
    packed = pl.pallas_call(
        pick_kernel,
        out_shape=jax.ShapeDtypeStruct((DEVICES, SLOTS, 8, HEAD_DIM), bf),
        in_specs=[SMEM, VMEM],
    )(spans, chunks)
    got = lax.all_to_all(packed.reshape(DEVICES, SLOTS * 8, HEAD_DIM), AXES, 0, 0, tiled=True)
    got = got.reshape(8, 2, 4, 2, 2, SLOTS, 8, HEAD_DIM).transpose(1, 2, 4, 3, 5, 0, 6, 7)
    got = got.reshape(2, KV_HEADS, SLOTS * BLOCK, HEAD_DIM)
    far_k = pl.BlockSpec((None, None, SLOTS * BLOCK, HEAD_DIM), lambda h: (0, h, 0, 0))
    far_v = pl.BlockSpec((None, None, SLOTS * BLOCK, HEAD_DIM), lambda h: (1, h, 0, 0))
    return pl.pallas_call(
        head_kernel,
        grid=(KV_HEADS,),
        out_shape=jax.ShapeDtypeStruct((BLOCK, HEADS * HEAD_DIM), bf),
        in_specs=[SMEM, pl.BlockSpec((None, BLOCK, PACK), lambda h: (h, 0, 0)), far_k, far_v],
        out_specs=pl.BlockSpec((BLOCK, GROUP * HEAD_DIM), lambda h: (0, h)),
    )(alive, bundle, got, got)


def shards(queries, keys, values, ancestors, token_block, positions):
    bf, f32, i32 = jnp.bfloat16, jnp.float32, jnp.int32
    me = lax.axis_index(AXES)
    base = lax.dynamic_slice_in_dim(positions, me * BLOCK, 1)
    where = jnp.stack([lax.axis_index("z"), lax.axis_index("c"), lax.axis_index("xh")]).astype(i32)
    span_blocks = token_block.reshape(DEVICES, BLOCK)[:, 0]
    send, cosine, sine, own_k = pl.pallas_call(
        spread_kernel,
        out_shape=(
            jax.ShapeDtypeStruct((8, 2, 4, 2, 2, 8, HEAD_DIM), bf),
            jax.ShapeDtypeStruct((BLOCK, HEAD_DIM), f32),
            jax.ShapeDtypeStruct((BLOCK, HEAD_DIM), f32),
            jax.ShapeDtypeStruct((BLOCK, KV_HEADS * HEAD_DIM), bf),
        ),
        in_specs=[SMEM, VMEM, VMEM, VMEM],
    )(base, jnp.asarray(inverse_row()), keys, values)
    chunks = lax.all_to_all(send.reshape(DEVICES, 8, HEAD_DIM), AXES, 0, 0, tiled=True)
    table = pl.BlockSpec((BLOCK, HEAD_DIM), lambda h: (0, 0))
    head = pl.BlockSpec((BLOCK, HEAD_DIM), lambda h: (0, h))
    picks, slots, count = pl.pallas_call(
        plan_kernel,
        out_shape=(
            jax.ShapeDtypeStruct((CAP, PLANES), i32),
            jax.ShapeDtypeStruct((8, ANC_MAX), i32),
            jax.ShapeDtypeStruct((1, 1), i32),
        ),
        in_specs=[SMEM, VMEM, VMEM, VMEM],
        cost_estimate=pl.CostEstimate(flops=4 << 20, bytes_accessed=4 << 20, transcendentals=0),
    )(where, span_blocks[None, :], span_blocks[:, None], ancestors)
    bundle = pl.pallas_call(
        bundle_kernel,
        grid=(KV_HEADS,),
        out_shape=jax.ShapeDtypeStruct((KV_HEADS, BLOCK, PACK), bf),
        in_specs=[VMEM_ONE, table, table, pl.BlockSpec((BLOCK, GROUP * HEAD_DIM), lambda h: (0, h)), head, head],
        out_specs=pl.BlockSpec((None, BLOCK, PACK), lambda h: (h, 0, 0)),
        cost_estimate=pl.CostEstimate(flops=4 << 20, bytes_accessed=4 << 20, transcendentals=0),
    )(count, cosine, sine, queries, own_k, values)
    members = lax.all_to_all(bundle, HEAD_AXES, 0, 0, tiled=True)
    fits = count[0, 0] <= CAP
    outs = quick(where, picks, slots, chunks, members)
    return lax.cond(fits, join, general, outs, chunks, bundle, span_blocks, ancestors)


def solution(mesh):
    fine = Mesh(mesh.devices.reshape(8, 2, 4, 2, 2), AXES)
    rows = P(AXES, None)
    return jax.shard_map(
        shards,
        mesh=fine,
        in_specs=(rows, rows, rows, P(), P(), P()),
        out_specs=rows,
        check_vma=False,
    )
```

```python
import functools

import jax
import jax.numpy as jnp
import numpy as np
from jax import lax
from jax.experimental import pallas as pl
from jax.experimental.pallas import tpu as pltpu
from jax.sharding import Mesh
from jax.sharding import PartitionSpec as P

HEADS = 32
KV_HEADS = 8
GROUP = HEADS // KV_HEADS
HEAD_DIM = 128
BLOCK = 128
ANC_MAX = 8
SLOTS = ANC_MAX - 1
DEVICES = 256
PLANES = 8
CAP = 40
HALF = BLOCK // 2
SHIFTS = ((0, 1, 7, 2), (6, 3, 5, 4))
GROUPS = len(SHIFTS)
PACK = (GROUP + 2) * HEAD_DIM
ROTARY_BASE = 500000.0
AXES = ("z", "c", "y", "xh", "xl")
HEAD_AXES = ("y", "xl")
NEG = -1e30
EXP2_SCALE = float(HEAD_DIM**-0.5 * np.log2(np.e))

SMEM = pl.BlockSpec(memory_space=pltpu.SMEM)
VMEM = pl.BlockSpec(memory_space=pltpu.VMEM)
VMEM_ONE = pl.BlockSpec((1, 1), lambda h: (0, 0))


def room(mib):
    return pltpu.CompilerParams(vmem_limit_bytes=mib << 20)


def inverse_row():
    half = HEAD_DIM // 2
    inv = (ROTARY_BASE ** (-2.0 * np.arange(half, dtype=np.float64) / HEAD_DIM)).astype(np.float32)
    return np.concatenate([inv, inv])[None, :]


def turn(x, cosine, sine):
    x = x.astype(jnp.float32)
    return (x * cosine + pltpu.roll(x, HEAD_DIM // 2, 1) * sine).astype(jnp.bfloat16)


def spread_kernel(base_ref, inv_ref, k_ref, v_ref, send_ref, cos_ref, sin_ref, own_ref):
    rows = lax.broadcasted_iota(jnp.int32, (BLOCK, HEAD_DIM), 0) + base_ref[0]
    lanes = lax.broadcasted_iota(jnp.int32, (BLOCK, HEAD_DIM), 1)
    angles = rows.astype(jnp.float32) * inv_ref[...]
    cosine = jnp.cos(angles)
    sine = jnp.sin(angles)
    sine = jnp.where(lanes < HEAD_DIM // 2, -sine, sine)
    cos_ref[...] = cosine
    sin_ref[...] = sine
    for h in range(KV_HEADS):
        cols = slice(h * HEAD_DIM, (h + 1) * HEAD_DIM)
        turned = turn(k_ref[:, cols], cosine, sine)
        own_ref[:, cols] = turned
        plain = v_ref[:, cols]
        for high in range(2):
            for low in range(8):
                t = (high * 8 + low) * 8
                send_ref[low, 0, h // 2, high, h % 2] = turned[t : t + 8]
                send_ref[low, 1, h // 2, high, h % 2] = plain[t : t + 8]


def bundle_kernel(count_ref, cos_ref, sin_ref, q_ref, k_ref, v_ref, out_ref):
    for g in range(GROUP):
        cols = slice(g * HEAD_DIM, (g + 1) * HEAD_DIM)
        out_ref[:, cols] = turn(q_ref[:, cols], cos_ref[...], sin_ref[...])
    out_ref[:, GROUP * HEAD_DIM : (GROUP + 1) * HEAD_DIM] = k_ref[...]
    out_ref[:, (GROUP + 1) * HEAD_DIM :] = v_ref[...]


def plan_kernel(where_ref, row_ref, col_ref, anc_ref, picks_ref, slots_ref, count_ref):
    n = DEVICES
    f32, bf, i32 = jnp.float32, jnp.bfloat16, jnp.int32
    row = row_ref[...]
    anc = anc_ref[...]
    lane = lax.broadcasted_iota(i32, (n, n), 1)
    sub = lax.broadcasted_iota(i32, (n, n), 0)
    depth = jnp.sum((anc >= 0).astype(i32), axis=1, keepdims=True)
    holds = jnp.zeros((n, n), f32)
    for j in range(SLOTS):
        entry = jnp.where(j < depth - 1, anc[:, j : j + 1], -1)
        holds = jnp.where(entry == row, 1.0, holds)
    block_at = (col_ref[...] == lane).astype(f32).astype(bf)
    plane8 = lax.broadcasted_iota(i32, (PLANES, n), 0)
    lane8 = lax.broadcasted_iota(i32, (PLANES, n), 1)
    in_plane = (lane8 // (n // PLANES) == plane8).astype(f32).astype(bf)
    blocks = jnp.dot(in_plane, block_at, preferred_element_type=f32)
    need = jnp.dot(blocks.astype(bf), holds.astype(bf), preferred_element_type=f32) > 0.5
    needed = need.astype(f32)
    upto = (sub <= lane).astype(f32).astype(bf)
    ranks = jnp.dot(needed.astype(bf), upto, preferred_element_type=f32)
    count_ref[...] = jnp.max(ranks, axis=(0, 1), keepdims=True).astype(i32)
    ranks = ranks - 1.0
    wanted = lax.broadcasted_iota(i32, (CAP, n), 0).astype(f32)
    span = lax.broadcasted_iota(i32, (CAP, n), 1).astype(f32)
    for z in range(PLANES):
        hit = (ranks[z : z + 1] == wanted) & (needed[z : z + 1] > 0.5)
        picks_ref[:, z : z + 1] = jnp.sum(
            jnp.where(hit, span, 0.0), axis=1, keepdims=True
        ).astype(i32)
    z, c, xh = where_ref[0], where_ref[1], where_ref[2]
    member = plane8
    mine = z * 32 + c * 16 + (member // 2) * 4 + xh * 2 + member % 2
    own_block = jnp.dot(
        (lane8 == mine).astype(f32).astype(bf), block_at, preferred_element_type=f32
    )
    path = jnp.dot(
        own_block.astype(bf), anc.astype(f32).astype(bf), preferred_element_type=f32
    ).astype(i32)
    my_rank = jnp.sum(jnp.where(plane8 == z, ranks, 0.0), axis=0, keepdims=True)
    for j in range(SLOTS):
        slot = jnp.sum(
            jnp.where(path[:, j : j + 1] == row, my_rank, 0.0), axis=1, keepdims=True
        ).astype(i32)
        slots_ref[:, j : j + 1] = jnp.clip(slot, 0, CAP - 1)
    slots_ref[:, SLOTS:] = jnp.sum((path >= 0).astype(i32), axis=1, keepdims=True) - 1


def pack_kernel(where_ref, picks_ref, src_ref, *out_refs):
    z = where_ref[0]

    def one(k, carry):
        for d in range(PLANES):
            out_refs[d][k] = src_ref[picks_ref[k, (z + d) % PLANES]]
        return carry

    lax.fori_loop(0, CAP, one, 0)


def pick_kernel(idx_ref, src_ref, out_ref):
    def one(d, carry):
        for j in range(SLOTS):
            out_ref[d, j] = src_ref[idx_ref[d, j]]
        return carry

    lax.fori_loop(0, out_ref.shape[0], one, 0)


def attention(q, near_k, near_v, far_k, far_v, alive, period):
    dims = (((1,), (1,)), ((), ()))
    far = lax.dot_general(q, far_k, dims, preferred_element_type=jnp.float32)
    near = lax.dot_general(q, near_k, dims, preferred_element_type=jnp.float32)
    column = lax.broadcasted_iota(jnp.int32, (1, far_k.shape[0]), 1)
    slot = (column // period) % SLOTS
    far = far + jnp.where(slot < alive, 0.0, NEG)
    row = lax.broadcasted_iota(jnp.int32, near.shape, 0) % BLOCK
    col = lax.broadcasted_iota(jnp.int32, near.shape, 1)
    near = jnp.where(col <= row, near, NEG)
    top = jnp.maximum(
        jnp.max(far, axis=1, keepdims=True), jnp.max(near, axis=1, keepdims=True)
    )
    far_w = jnp.exp2((far - top) * EXP2_SCALE)
    near_w = jnp.exp2((near - top) * EXP2_SCALE)
    total = jnp.sum(far_w, axis=1, keepdims=True) + jnp.sum(near_w, axis=1, keepdims=True)
    mixed = jnp.dot(far_w.astype(jnp.bfloat16), far_v, preferred_element_type=jnp.float32)
    mixed += jnp.dot(near_w.astype(jnp.bfloat16), near_v, preferred_element_type=jnp.float32)
    return (mixed / total).astype(jnp.bfloat16)


def attend_one(x_ref, far_k, far_v, alive, period):
    cols = [slice(g * HEAD_DIM, (g + 1) * HEAD_DIM) for g in range(GROUP + 2)]
    q = jnp.concatenate([x_ref[:, cols[g]] for g in range(GROUP)], axis=0)
    near_k, near_v = x_ref[:, cols[GROUP]], x_ref[:, cols[GROUP + 1]]
    return attention(q, near_k, near_v, far_k, far_v, alive, period)


def span_kernel(where_ref, slots_ref, x_ref, *refs):
    far_refs, out_ref, k_ref, v_ref = refs[: 4 * GROUPS], refs[-3], refs[-2], refs[-1]
    own, other = far_refs[: 2 * GROUPS], far_refs[2 * GROUPS :]

    def one(m, carry):
        def fill(dst_ref, parts):
            for j in range(SLOTS):
                slot = slots_ref[m, j]
                at = j * BLOCK
                for part in parts:
                    size = part.shape[1]
                    dst_ref[at : at + size] = part[slot]
                    at += size

        @pl.when(where_ref[1] == 0)
        def _():
            fill(k_ref, own)
            fill(v_ref, other)

        @pl.when(where_ref[1] != 0)
        def _():
            fill(k_ref, other)
            fill(v_ref, own)

        done = attend_one(x_ref.at[m], k_ref[...], v_ref[...], slots_ref[m, SLOTS], BLOCK)
        for g in range(GROUP):
            out_ref[m, :, g * HEAD_DIM : (g + 1) * HEAD_DIM] = done[g * BLOCK : (g + 1) * BLOCK]
        return carry

    lax.fori_loop(0, KV_HEADS, one, 0)


def head_kernel(alive_ref, x_ref, k_ref, v_ref, out_ref):
    done = attend_one(x_ref, k_ref[...], v_ref[...], alive_ref[0], HALF)
    for g in range(GROUP):
        out_ref[:, g * HEAD_DIM : (g + 1) * HEAD_DIM] = done[g * BLOCK : (g + 1) * BLOCK]


def join_kernel(in_ref, out_ref):
    width = GROUP * HEAD_DIM
    for h in range(KV_HEADS):
        out_ref[:, h * width : (h + 1) * width] = in_ref[h]


def quick(where, picks, slots, chunks, members):
    bf = jnp.bfloat16
    packs = pl.pallas_call(
        pack_kernel,
        out_shape=[jax.ShapeDtypeStruct((CAP, 8, HEAD_DIM), bf)] * PLANES,
        in_specs=[SMEM, SMEM, VMEM],
        compiler_params=room(8),
    )(where, picks, chunks)
    swap = [(0, 1), (1, 0)]
    got = {0: packs[0]}
    for shifts in SHIFTS:
        for d in shifts:
            if d:
                pairs = [(i, (i + d) % PLANES) for i in range(PLANES)]
                got[d] = lax.ppermute(packs[d], "z", pairs)
    own, other = [], []
    for shifts in SHIFTS:
        part = jnp.stack([got[d] for d in shifts], axis=1)
        own.append(part.reshape(CAP, 8 * len(shifts), HEAD_DIM))
    own += [lax.ppermute(part, "xh", swap) for part in own]
    other = [lax.ppermute(part, "c", swap) for part in own]
    out = pl.pallas_call(
        span_kernel,
        out_shape=jax.ShapeDtypeStruct((KV_HEADS, BLOCK, GROUP * HEAD_DIM), bf),
        in_specs=[SMEM, SMEM] + [VMEM] * (1 + 4 * GROUPS),
        out_specs=VMEM,
        scratch_shapes=[pltpu.VMEM((SLOTS * BLOCK, HEAD_DIM), bf)] * 2,
        compiler_params=room(24),
        cost_estimate=pl.CostEstimate(
            flops=1 << 31, bytes_accessed=4 << 20, transcendentals=4 << 20
        ),
    )(where, slots, members, *own, *other)
    return lax.all_to_all(out, HEAD_AXES, 0, 0, tiled=True)


def join(outs, *unused):
    return pl.pallas_call(
        join_kernel,
        out_shape=jax.ShapeDtypeStruct((BLOCK, HEADS * HEAD_DIM), jnp.bfloat16),
        in_specs=[VMEM],
        compiler_params=room(8),
    )(outs)


def general(outs, chunks, bundle, span_blocks, ancestors):
    bf = jnp.bfloat16
    ids = jnp.arange(DEVICES, dtype=jnp.int32)
    span_of = jnp.sum(jnp.where(span_blocks[:, None] == ids[None, :], ids[:, None], 0), axis=0)
    lineage = ancestors[span_blocks]
    depth = jnp.sum((lineage >= 0).astype(jnp.int32), axis=1)
    spans = span_of[jnp.maximum(lineage, 0)]
    alive = lax.dynamic_slice_in_dim(depth - 1, lax.axis_index(AXES), 1)
    packed = pl.pallas_call(
        pick_kernel,
        out_shape=jax.ShapeDtypeStruct((DEVICES, SLOTS, 8, HEAD_DIM), bf),
        in_specs=[SMEM, VMEM],
    )(spans, chunks)
    got = lax.all_to_all(packed.reshape(DEVICES, SLOTS * 8, HEAD_DIM), AXES, 0, 0, tiled=True)
    got = got.reshape(8, 2, 4, 2, 2, SLOTS, 8, HEAD_DIM).transpose(1, 2, 4, 3, 5, 0, 6, 7)
    got = got.reshape(2, KV_HEADS, SLOTS * BLOCK, HEAD_DIM)
    far_k = pl.BlockSpec((None, None, SLOTS * BLOCK, HEAD_DIM), lambda h: (0, h, 0, 0))
    far_v = pl.BlockSpec((None, None, SLOTS * BLOCK, HEAD_DIM), lambda h: (1, h, 0, 0))
    return pl.pallas_call(
        head_kernel,
        grid=(KV_HEADS,),
        out_shape=jax.ShapeDtypeStruct((BLOCK, HEADS * HEAD_DIM), bf),
        in_specs=[SMEM, pl.BlockSpec((None, BLOCK, PACK), lambda h: (h, 0, 0)), far_k, far_v],
        out_specs=pl.BlockSpec((BLOCK, GROUP * HEAD_DIM), lambda h: (0, h)),
    )(alive, bundle, got, got)


def shards(queries, keys, values, ancestors, token_block, positions):
    bf, f32, i32 = jnp.bfloat16, jnp.float32, jnp.int32
    me = lax.axis_index(AXES)
    base = lax.dynamic_slice_in_dim(positions, me * BLOCK, 1)
    where = jnp.stack([lax.axis_index("z"), lax.axis_index("c"), lax.axis_index("xh")]).astype(i32)
    span_blocks = token_block.reshape(DEVICES, BLOCK)[:, 0]
    send, cosine, sine, own_k = pl.pallas_call(
        spread_kernel,
        out_shape=(
            jax.ShapeDtypeStruct((8, 2, 4, 2, 2, 8, HEAD_DIM), bf),
            jax.ShapeDtypeStruct((BLOCK, HEAD_DIM), f32),
            jax.ShapeDtypeStruct((BLOCK, HEAD_DIM), f32),
            jax.ShapeDtypeStruct((BLOCK, KV_HEADS * HEAD_DIM), bf),
        ),
        in_specs=[SMEM, VMEM, VMEM, VMEM],
        compiler_params=room(8),
    )(base, jnp.asarray(inverse_row()), keys, values)
    chunks = lax.all_to_all(send.reshape(DEVICES, 8, HEAD_DIM), AXES, 0, 0, tiled=True)
    table = pl.BlockSpec((BLOCK, HEAD_DIM), lambda h: (0, 0))
    head = pl.BlockSpec((BLOCK, HEAD_DIM), lambda h: (0, h))
    picks, slots, count = pl.pallas_call(
        plan_kernel,
        out_shape=(
            jax.ShapeDtypeStruct((CAP, PLANES), i32),
            jax.ShapeDtypeStruct((8, ANC_MAX), i32),
            jax.ShapeDtypeStruct((1, 1), i32),
        ),
        in_specs=[SMEM, VMEM, VMEM, VMEM],
        compiler_params=room(8),
        cost_estimate=pl.CostEstimate(flops=4 << 20, bytes_accessed=4 << 20, transcendentals=0),
    )(where, span_blocks[None, :], span_blocks[:, None], ancestors)
    bundle = pl.pallas_call(
        bundle_kernel,
        grid=(KV_HEADS,),
        out_shape=jax.ShapeDtypeStruct((KV_HEADS, BLOCK, PACK), bf),
        in_specs=[VMEM_ONE, table, table, pl.BlockSpec((BLOCK, GROUP * HEAD_DIM), lambda h: (0, h)), head, head],
        out_specs=pl.BlockSpec((None, BLOCK, PACK), lambda h: (h, 0, 0)),
        compiler_params=room(8),
        cost_estimate=pl.CostEstimate(flops=4 << 20, bytes_accessed=4 << 20, transcendentals=0),
    )(count, cosine, sine, queries, own_k, values)
    members = lax.all_to_all(bundle, HEAD_AXES, 0, 0, tiled=True)
    fits = count[0, 0] <= CAP
    outs = quick(where, picks, slots, chunks, members)
    return lax.cond(fits, join, general, outs, chunks, bundle, span_blocks, ancestors)


def solution(mesh):
    fine = Mesh(mesh.devices.reshape(8, 2, 4, 2, 2), AXES)
    rows = P(AXES, None)
    return jax.shard_map(
        shards,
        mesh=fine,
        in_specs=(rows, rows, rows, P(), P(), P()),
        out_specs=rows,
        check_vma=False,
    )
```

```python
import functools

import jax
import jax.numpy as jnp
import numpy as np
from jax import lax
from jax.experimental import pallas as pl
from jax.experimental.pallas import tpu as pltpu
from jax.sharding import Mesh
from jax.sharding import PartitionSpec as P

HEADS = 32
KV_HEADS = 8
GROUP = HEADS // KV_HEADS
HEAD_DIM = 128
BLOCK = 128
ANC_MAX = 8
SLOTS = ANC_MAX - 1
DEVICES = 256
PLANES = 8
CAP = 34
HALF = BLOCK // 2
SHIFTS = ((0, 1, 7, 2), (6, 3, 5, 4))
GROUPS = len(SHIFTS)
STEPS = (5, 4, 7, 3, 6, 2, 1, 0)
KV_SCRATCH = [
    pltpu.VMEM((ANC_MAX * BLOCK, HEAD_DIM), jnp.bfloat16),
    pltpu.VMEM((ANC_MAX * BLOCK, 2 * HEAD_DIM), jnp.bfloat16),
]
PACK = (GROUP + 2) * HEAD_DIM
ROTARY_BASE = 500000.0
AXES = ("z", "c", "y", "xh", "xl")
HEAD_AXES = ("y", "xl")
NEG = -1e30
EXP2_SCALE = float(HEAD_DIM**-0.5 * np.log2(np.e))

HBM = pl.BlockSpec(memory_space=pltpu.HBM)
SMEM = pl.BlockSpec(memory_space=pltpu.SMEM)
VMEM = pl.BlockSpec(memory_space=pltpu.VMEM)
VMEM_ONE = pl.BlockSpec((1, 1), lambda h: (0, 0))


def room(mib):
    return pltpu.CompilerParams(vmem_limit_bytes=mib << 20)


def inverse_row():
    half = HEAD_DIM // 2
    inv = (ROTARY_BASE ** (-2.0 * np.arange(half, dtype=np.float64) / HEAD_DIM)).astype(np.float32)
    return np.concatenate([inv, inv])[None, :]


def turn(x, cosine, sine):
    x = x.astype(jnp.float32)
    return (x * cosine + pltpu.roll(x, HEAD_DIM // 2, 1) * sine).astype(jnp.bfloat16)


def device_index():
    z, c, y, xh, xl = [lax.axis_index(name) for name in AXES]
    return (((z * 2 + c) * 4 + y) * 2 + xh) * 2 + xl


def spread_kernel(
    pos_ref, inv_ref, k_hbm, v_hbm, send_ref, cos_ref, sin_ref, own_ref, v_ref, base_ref, sems
):
    start = pl.multiple_of(device_index() * BLOCK, BLOCK)
    loads = [
        pltpu.make_async_copy(pos_ref.at[pl.ds(start, BLOCK)], base_ref, sems.at[0]),
        pltpu.make_async_copy(k_hbm, own_ref, sems.at[1]),
        pltpu.make_async_copy(v_hbm, v_ref, sems.at[2]),
    ]
    for load in loads:
        load.start()
    loads[0].wait()
    rows = lax.broadcasted_iota(jnp.int32, (BLOCK, HEAD_DIM), 0) + base_ref[0]
    lanes = lax.broadcasted_iota(jnp.int32, (BLOCK, HEAD_DIM), 1)
    angles = rows.astype(jnp.float32) * inv_ref[...]
    cosine = jnp.cos(angles)
    sine = jnp.sin(angles)
    sine = jnp.where(lanes < HEAD_DIM // 2, -sine, sine)
    cos_ref[...] = cosine
    sin_ref[...] = sine
    loads[1].wait()
    loads[2].wait()
    for h in range(KV_HEADS):
        cols = slice(h * HEAD_DIM, (h + 1) * HEAD_DIM)
        turned = turn(own_ref[:, cols], cosine, sine)
        own_ref[:, cols] = turned
        plain = v_ref[:, cols]
        for high in range(2):
            for low in range(8):
                t = (high * 8 + low) * 8
                send_ref[low, 0, h // 2, high, h % 2] = turned[t : t + 8]
                send_ref[low, 1, h // 2, high, h % 2] = plain[t : t + 8]


def bundle_kernel(count_ref, cos_ref, sin_ref, q_ref, k_ref, v_ref, out_ref):
    for g in range(GROUP):
        cols = slice(g * HEAD_DIM, (g + 1) * HEAD_DIM)
        out_ref[:, cols] = turn(q_ref[:, cols], cos_ref[...], sin_ref[...])
    out_ref[:, GROUP * HEAD_DIM : (GROUP + 1) * HEAD_DIM] = k_ref[...]
    out_ref[:, (GROUP + 1) * HEAD_DIM :] = v_ref[...]


def plan_kernel(token_ref, anc_ref, picks_ref, slots_ref, count_ref):
    n = DEVICES
    f32, bf, i32 = jnp.float32, jnp.bfloat16, jnp.int32
    across = (((1,), (1,)), ((), ()))
    anc = anc_ref[...]
    col = token_ref[:, 0:1]
    lane = lax.broadcasted_iota(i32, (n, n), 1)
    sub = lax.broadcasted_iota(i32, (n, n), 0)
    row = jnp.sum(jnp.where(sub == lane, col, 0), axis=0, keepdims=True)
    depth = jnp.sum((anc >= 0).astype(i32), axis=0, keepdims=True)
    holds = jnp.zeros((n, n), f32)
    for j in range(SLOTS):
        entry = jnp.where(j < depth - 1, anc[j : j + 1], -1)
        holds = jnp.where(entry == col, 1.0, holds)
    block_at = (col == lane).astype(f32).astype(bf)
    plane8 = lax.broadcasted_iota(i32, (PLANES, n), 0)
    lane8 = lax.broadcasted_iota(i32, (PLANES, n), 1)
    in_plane = (lane8 // (n // PLANES) == plane8).astype(f32).astype(bf)
    blocks = jnp.dot(in_plane, block_at, preferred_element_type=f32)
    need = lax.dot_general(
        blocks.astype(bf), holds.astype(bf), across, preferred_element_type=f32
    )
    needed = (need > 0.5).astype(f32)
    upto = (sub <= lane).astype(f32).astype(bf)
    ranks = jnp.dot(needed.astype(bf), upto, preferred_element_type=f32)
    count_ref[...] = jnp.max(ranks, axis=(0, 1), keepdims=True).astype(i32)
    ranks = ranks - 1.0
    wanted = lax.broadcasted_iota(i32, (CAP, n), 0).astype(f32)
    span = lax.broadcasted_iota(i32, (CAP, n), 1).astype(f32)
    for z in range(PLANES):
        hit = (ranks[z : z + 1] == wanted) & (needed[z : z + 1] > 0.5)
        picks_ref[:, z : z + 1] = jnp.sum(
            jnp.where(hit, span, 0.0), axis=1, keepdims=True
        ).astype(i32)
    z, c, xh = lax.axis_index("z"), lax.axis_index("c"), lax.axis_index("xh")
    mine = z * 32 + c * 16 + (plane8 // 2) * 4 + xh * 2 + plane8 % 2
    own_block = jnp.dot(
        (lane8 == mine).astype(f32).astype(bf), block_at, preferred_element_type=f32
    )
    path = lax.dot_general(
        own_block.astype(bf), anc.astype(f32).astype(bf), across, preferred_element_type=f32
    ).astype(i32)
    my_rank = jnp.sum(jnp.where(plane8 == z, ranks, 0.0), axis=0, keepdims=True)
    for j in range(SLOTS):
        slot = jnp.sum(
            jnp.where(path[:, j : j + 1] == row, my_rank, 0.0), axis=1, keepdims=True
        ).astype(i32)
        slots_ref[:, j : j + 1] = jnp.clip(slot, 0, CAP - 1)
    slots_ref[:, SLOTS:] = jnp.sum((path >= 0).astype(i32), axis=1, keepdims=True) - 1


def pack_kernel(picks_ref, src_ref, *out_refs):
    z = lax.axis_index("z")
    for d in range(PLANES):
        plane = lax.rem(z + d, PLANES)

        def one(k, carry):
            out_refs[d][k] = src_ref[picks_ref[k, plane]]
            return carry

        lax.fori_loop(0, CAP, one, 0, unroll=True)


def pick_kernel(idx_ref, src_ref, out_ref):
    def one(d, carry):
        for j in range(SLOTS):
            out_ref[d, j] = src_ref[idx_ref[d, j]]
        return carry

    lax.fori_loop(0, out_ref.shape[0], one, 0)


def attention(x_ref, k_ref, v_ref, alive, period, out_ref):
    k_ref[0:BLOCK] = x_ref[:, GROUP * HEAD_DIM : (GROUP + 1) * HEAD_DIM]
    v_ref[0:BLOCK, 0:HEAD_DIM] = x_ref[:, (GROUP + 1) * HEAD_DIM :]
    v_ref[:, HEAD_DIM:] = jnp.ones((k_ref.shape[0], HEAD_DIM), jnp.bfloat16)
    column = lax.broadcasted_iota(jnp.int32, (1, SLOTS * BLOCK), 1)
    bias = jnp.where((column // period) % SLOTS < alive, 0.0, NEG)
    row = lax.broadcasted_iota(jnp.int32, (BLOCK, BLOCK), 0)
    col = lax.broadcasted_iota(jnp.int32, (BLOCK, BLOCK), 1)
    for g in range(GROUP):
        cols = slice(g * HEAD_DIM, (g + 1) * HEAD_DIM)
        scores = lax.dot_general(
            x_ref[:, cols], k_ref[...], (((1,), (1,)), ((), ())), preferred_element_type=jnp.float32
        )
        near = jnp.where(col <= row, scores[:, :BLOCK], NEG)
        scores = jnp.concatenate([near, scores[:, BLOCK:] + bias], axis=1)
        top = jnp.max(scores, axis=1, keepdims=True)
        weights = jnp.exp2((scores - top) * EXP2_SCALE).astype(jnp.bfloat16)
        mixed = jnp.dot(weights, v_ref[...], preferred_element_type=jnp.float32)
        out_ref[:, cols] = (mixed[:, :HEAD_DIM] / mixed[:, HEAD_DIM:]).astype(jnp.bfloat16)


def own_member():
    return lax.axis_index("y") * 2 + lax.axis_index("xl")


def span_kernel(step, slots_ref, x_ref, *refs):
    far_refs, out_ref, k_ref, v_ref = refs[: 4 * GROUPS], refs[-3], refs[-2], refs[-1]
    own, other = far_refs[: 2 * GROUPS], far_refs[2 * GROUPS :]
    m = own_member() ^ step
    core = lax.axis_index("c")

    def fill(dst_ref, parts):
        for j in range(SLOTS):
            slot = slots_ref[m, j]
            at = (j + 1) * BLOCK
            for part in parts:
                size = part.shape[1]
                dst_ref[at : at + size, 0:HEAD_DIM] = part[slot]
                at += size

    @pl.when(core == 0)
    def _():
        fill(k_ref, own)
        fill(v_ref, other)

    @pl.when(core != 0)
    def _():
        fill(k_ref, other)
        fill(v_ref, own)

    attention(x_ref.at[m], k_ref, v_ref, slots_ref[m, SLOTS], BLOCK, out_ref)


def head_kernel(alive_ref, x_ref, far_k_ref, far_v_ref, out_ref, k_ref, v_ref):
    k_ref[BLOCK:] = far_k_ref[...]
    v_ref[BLOCK:, 0:HEAD_DIM] = far_v_ref[...]
    attention(x_ref, k_ref, v_ref, alive_ref[0], HALF, out_ref)


def join_kernel(*refs):
    out_ref = refs[-1]
    width = GROUP * HEAD_DIM
    for step in range(KV_HEADS):
        at = pl.multiple_of((own_member() ^ step) * width, width)
        out_ref[:, pl.ds(at, width)] = refs[step][...]


def quick(picks, slots, chunks, members):
    bf = jnp.bfloat16
    packs = pl.pallas_call(
        pack_kernel,
        out_shape=[jax.ShapeDtypeStruct((CAP, 8, HEAD_DIM), bf)] * PLANES,
        in_specs=[SMEM, VMEM],
        compiler_params=room(8),
    )(picks, chunks)
    swap = [(0, 1), (1, 0)]
    got = {0: packs[0]}
    for shifts in SHIFTS:
        for d in shifts:
            if d:
                pairs = [(i, (i + d) % PLANES) for i in range(PLANES)]
                got[d] = lax.ppermute(packs[d], "z", pairs)
    own, other = [], []
    for shifts in SHIFTS:
        part = jnp.stack([got[d] for d in shifts], axis=1)
        own.append(part.reshape(CAP, 8 * len(shifts), HEAD_DIM))
    own += [lax.ppermute(part, "xh", swap) for part in own]
    other = [lax.ppermute(part, "c", swap) for part in own]
    outs = {}
    for step in STEPS:
        out = pl.pallas_call(
            functools.partial(span_kernel, step),
            out_shape=jax.ShapeDtypeStruct((BLOCK, GROUP * HEAD_DIM), bf),
            in_specs=[SMEM] + [VMEM] * (1 + 4 * GROUPS),
            out_specs=VMEM,
            scratch_shapes=KV_SCRATCH,
            compiler_params=room(16),
            cost_estimate=pl.CostEstimate(
                flops=1 << 29, bytes_accessed=1 << 20, transcendentals=1 << 19
            ),
        )(slots, members, *own, *other)
        pairs = [(m, m ^ step) for m in range(KV_HEADS)]
        outs[step] = lax.ppermute(out, HEAD_AXES, pairs) if step else out
    return [outs[step] for step in range(KV_HEADS)]


def join(outs, *unused):
    return pl.pallas_call(
        join_kernel,
        out_shape=jax.ShapeDtypeStruct((BLOCK, HEADS * HEAD_DIM), jnp.bfloat16),
        in_specs=[VMEM] * KV_HEADS,
        compiler_params=room(8),
    )(*outs)


def general(outs, chunks, bundle, token_block, ancestors):
    bf = jnp.bfloat16
    span_blocks = token_block.reshape(DEVICES, BLOCK)[:, 0]
    ids = jnp.arange(DEVICES, dtype=jnp.int32)
    span_of = jnp.sum(jnp.where(span_blocks[:, None] == ids[None, :], ids[:, None], 0), axis=0)
    lineage = ancestors[span_blocks]
    depth = jnp.sum((lineage >= 0).astype(jnp.int32), axis=1)
    spans = span_of[jnp.maximum(lineage, 0)]
    alive = lax.dynamic_slice_in_dim(depth - 1, lax.axis_index(AXES), 1)
    packed = pl.pallas_call(
        pick_kernel,
        out_shape=jax.ShapeDtypeStruct((DEVICES, SLOTS, 8, HEAD_DIM), bf),
        in_specs=[SMEM, VMEM],
    )(spans, chunks)
    got = lax.all_to_all(packed.reshape(DEVICES, SLOTS * 8, HEAD_DIM), AXES, 0, 0, tiled=True)
    got = got.reshape(8, 2, 4, 2, 2, SLOTS, 8, HEAD_DIM).transpose(1, 2, 4, 3, 5, 0, 6, 7)
    got = got.reshape(2, KV_HEADS, SLOTS * BLOCK, HEAD_DIM)
    far_k = pl.BlockSpec((None, None, SLOTS * BLOCK, HEAD_DIM), lambda h: (0, h, 0, 0))
    far_v = pl.BlockSpec((None, None, SLOTS * BLOCK, HEAD_DIM), lambda h: (1, h, 0, 0))
    return pl.pallas_call(
        head_kernel,
        grid=(KV_HEADS,),
        out_shape=jax.ShapeDtypeStruct((BLOCK, HEADS * HEAD_DIM), bf),
        in_specs=[SMEM, pl.BlockSpec((None, BLOCK, PACK), lambda h: (h, 0, 0)), far_k, far_v],
        out_specs=pl.BlockSpec((BLOCK, GROUP * HEAD_DIM), lambda h: (0, h)),
        scratch_shapes=KV_SCRATCH,
    )(alive, bundle, got, got)


def shards(queries, keys, values, ancestors, token_block, positions):
    bf, f32, i32 = jnp.bfloat16, jnp.float32, jnp.int32
    send, cosine, sine, own_k = pl.pallas_call(
        spread_kernel,
        out_shape=(
            jax.ShapeDtypeStruct((8, 2, 4, 2, 2, 8, HEAD_DIM), bf),
            jax.ShapeDtypeStruct((BLOCK, HEAD_DIM), f32),
            jax.ShapeDtypeStruct((BLOCK, HEAD_DIM), f32),
            jax.ShapeDtypeStruct((BLOCK, KV_HEADS * HEAD_DIM), bf),
        ),
        in_specs=[HBM, VMEM, HBM, HBM],
        scratch_shapes=[
            pltpu.VMEM((BLOCK, KV_HEADS * HEAD_DIM), bf),
            pltpu.SMEM((BLOCK,), i32),
            pltpu.SemaphoreType.DMA((3,)),
        ],
        compiler_params=room(8),
    )(positions, jnp.asarray(inverse_row()), keys, values)
    chunks = lax.all_to_all(send.reshape(DEVICES, 8, HEAD_DIM), AXES, 0, 0, tiled=True)
    table = pl.BlockSpec((BLOCK, HEAD_DIM), lambda h: (0, 0))
    head = pl.BlockSpec((BLOCK, HEAD_DIM), lambda h: (0, h))
    picks, slots, count = pl.pallas_call(
        plan_kernel,
        out_shape=(
            jax.ShapeDtypeStruct((CAP, PLANES), i32),
            jax.ShapeDtypeStruct((8, ANC_MAX), i32),
            jax.ShapeDtypeStruct((1, 1), i32),
        ),
        in_specs=[VMEM, VMEM],
        compiler_params=room(8),
        cost_estimate=pl.CostEstimate(flops=4 << 20, bytes_accessed=4 << 20, transcendentals=0),
    )(token_block.reshape(DEVICES, BLOCK), ancestors.T)
    bundle = pl.pallas_call(
        bundle_kernel,
        grid=(KV_HEADS,),
        out_shape=jax.ShapeDtypeStruct((KV_HEADS, BLOCK, PACK), bf),
        in_specs=[VMEM_ONE, table, table, pl.BlockSpec((BLOCK, GROUP * HEAD_DIM), lambda h: (0, h)), head, head],
        out_specs=pl.BlockSpec((None, BLOCK, PACK), lambda h: (h, 0, 0)),
        compiler_params=room(8),
        cost_estimate=pl.CostEstimate(flops=4 << 20, bytes_accessed=4 << 20, transcendentals=0),
    )(count, cosine, sine, queries, own_k, values)
    members = lax.all_to_all(bundle, HEAD_AXES, 0, 0, tiled=True)
    fits = count[0, 0] <= CAP
    outs = quick(picks, slots, chunks, members)
    return lax.cond(fits, join, general, outs, chunks, bundle, token_block, ancestors)


def solution(mesh):
    fine = Mesh(mesh.devices.reshape(8, 2, 4, 2, 2), AXES)
    rows = P(AXES, None)
    return jax.shard_map(
        shards,
        mesh=fine,
        in_specs=(rows, rows, rows, P(), P(), P()),
        out_specs=rows,
        check_vma=False,
    )
```

```python
import functools

import jax
import jax.numpy as jnp
import numpy as np
from jax import lax
from jax.experimental import pallas as pl
from jax.experimental.pallas import tpu as pltpu
from jax.sharding import Mesh
from jax.sharding import PartitionSpec as P


HEADS = 32
KV_HEADS = 8
GROUP = HEADS // KV_HEADS
HEAD_DIM = 128
BLOCK = 128
ANC_MAX = 8
SLOTS = ANC_MAX - 1
DEVICES = 256
PLANES = 8
CAP = 34
HALF = BLOCK // 2
SHIFTS = ((0, 1, 7, 2), (6, 3, 5, 4))
GROUPS = len(SHIFTS)
STEPS = ((5, 4), (7, 3), (6, 2), (1, 0))
KV_SCRATCH = [
    pltpu.VMEM((ANC_MAX * BLOCK, HEAD_DIM), jnp.bfloat16),
    pltpu.VMEM((ANC_MAX * BLOCK, 2 * HEAD_DIM), jnp.bfloat16),
]
PACK = (GROUP + 2) * HEAD_DIM
ROTARY_BASE = 500000.0
AXES = ("z", "c", "y", "xh", "xl")
HEAD_AXES = ("y", "xl")
NEG = -1e30
EXP2_SCALE = float(HEAD_DIM**-0.5 * np.log2(np.e))

HBM = pl.BlockSpec(memory_space=pltpu.HBM)
SMEM = pl.BlockSpec(memory_space=pltpu.SMEM)
VMEM = pl.BlockSpec(memory_space=pltpu.VMEM)
VMEM_ONE = pl.BlockSpec((1, 1), lambda h: (0, 0))


def room(mib):
    return pltpu.CompilerParams(vmem_limit_bytes=mib << 20)


def inverse_row():
    half = HEAD_DIM // 2
    inv = (ROTARY_BASE ** (-2.0 * np.arange(half, dtype=np.float64) / HEAD_DIM)).astype(np.float32)
    return np.concatenate([inv, inv])[None, :]


def turn(x, cosine, sine):
    x = x.astype(jnp.float32)
    return (x * cosine + pltpu.roll(x, HEAD_DIM // 2, 1) * sine).astype(jnp.bfloat16)


def device_index():
    z, c, y, xh, xl = [lax.axis_index(name) for name in AXES]
    return (((z * 2 + c) * 4 + y) * 2 + xh) * 2 + xl


def spread_kernel(
    pos_ref, inv_ref, k_hbm, v_hbm, send_ref, cos_ref, sin_ref, own_ref, v_ref, base_ref, sems
):
    start = pl.multiple_of(device_index() * BLOCK, BLOCK)
    loads = [
        pltpu.make_async_copy(pos_ref.at[pl.ds(start, BLOCK)], base_ref, sems.at[0]),
        pltpu.make_async_copy(k_hbm, own_ref, sems.at[1]),
        pltpu.make_async_copy(v_hbm, v_ref, sems.at[2]),
    ]
    for load in loads:
        load.start()
    loads[0].wait()
    rows = lax.broadcasted_iota(jnp.int32, (BLOCK, HEAD_DIM), 0) + base_ref[0]
    lanes = lax.broadcasted_iota(jnp.int32, (BLOCK, HEAD_DIM), 1)
    angles = rows.astype(jnp.float32) * inv_ref[...]
    cosine = jnp.cos(angles)
    sine = jnp.sin(angles)
    sine = jnp.where(lanes < HEAD_DIM // 2, -sine, sine)
    cos_ref[...] = cosine
    sin_ref[...] = sine
    loads[1].wait()
    loads[2].wait()
    for h in range(KV_HEADS):
        cols = slice(h * HEAD_DIM, (h + 1) * HEAD_DIM)
        turned = turn(own_ref[:, cols], cosine, sine)
        own_ref[:, cols] = turned
        plain = v_ref[:, cols]
        for high in range(2):
            for low in range(8):
                t = (high * 8 + low) * 8
                send_ref[low, 0, h // 2, high, h % 2] = turned[t : t + 8]
                send_ref[low, 1, h // 2, high, h % 2] = plain[t : t + 8]


def bundle_kernel(count_ref, cos_ref, sin_ref, q_ref, k_ref, v_ref, out_ref):
    for g in range(GROUP):
        cols = slice(g * HEAD_DIM, (g + 1) * HEAD_DIM)
        out_ref[:, cols] = turn(q_ref[:, cols], cos_ref[...], sin_ref[...])
    out_ref[:, GROUP * HEAD_DIM : (GROUP + 1) * HEAD_DIM] = k_ref[...]
    out_ref[:, (GROUP + 1) * HEAD_DIM :] = v_ref[...]


def plan_kernel(token_ref, anc_ref, picks_ref, slots_ref, count_ref):
    n = DEVICES
    f32, bf, i32 = jnp.float32, jnp.bfloat16, jnp.int32
    across = (((1,), (1,)), ((), ()))
    anc = anc_ref[...]
    col = token_ref[:, 0:1]
    lane = lax.broadcasted_iota(i32, (n, n), 1)
    sub = lax.broadcasted_iota(i32, (n, n), 0)
    row = jnp.sum(jnp.where(sub == lane, col, 0), axis=0, keepdims=True)
    depth = jnp.sum((anc >= 0).astype(i32), axis=0, keepdims=True)
    holds = jnp.zeros((n, n), f32)
    for j in range(SLOTS):
        entry = jnp.where(j < depth - 1, anc[j : j + 1], -1)
        holds = jnp.where(entry == col, 1.0, holds)
    block_at = (col == lane).astype(f32).astype(bf)
    plane8 = lax.broadcasted_iota(i32, (PLANES, n), 0)
    lane8 = lax.broadcasted_iota(i32, (PLANES, n), 1)
    in_plane = (lane8 // (n // PLANES) == plane8).astype(f32).astype(bf)
    blocks = jnp.dot(in_plane, block_at, preferred_element_type=f32)
    need = lax.dot_general(
        blocks.astype(bf), holds.astype(bf), across, preferred_element_type=f32
    )
    needed = (need > 0.5).astype(f32)
    upto = (sub <= lane).astype(f32).astype(bf)
    ranks = jnp.dot(needed.astype(bf), upto, preferred_element_type=f32)
    count_ref[...] = jnp.max(ranks, axis=(0, 1), keepdims=True).astype(i32)
    ranks = ranks - 1.0
    wanted = lax.broadcasted_iota(i32, (CAP, n), 0).astype(f32)
    span = lax.broadcasted_iota(i32, (CAP, n), 1).astype(f32)
    for z in range(PLANES):
        hit = (ranks[z : z + 1] == wanted) & (needed[z : z + 1] > 0.5)
        picks_ref[:, z : z + 1] = jnp.sum(
            jnp.where(hit, span, 0.0), axis=1, keepdims=True
        ).astype(i32)
    z, c, xh = lax.axis_index("z"), lax.axis_index("c"), lax.axis_index("xh")
    mine = z * 32 + c * 16 + (plane8 // 2) * 4 + xh * 2 + plane8 % 2
    own_block = jnp.dot(
        (lane8 == mine).astype(f32).astype(bf), block_at, preferred_element_type=f32
    )
    path = lax.dot_general(
        own_block.astype(bf), anc.astype(f32).astype(bf), across, preferred_element_type=f32
    ).astype(i32)
    my_rank = jnp.sum(jnp.where(plane8 == z, ranks, 0.0), axis=0, keepdims=True)
    for j in range(SLOTS):
        slot = jnp.sum(
            jnp.where(path[:, j : j + 1] == row, my_rank, 0.0), axis=1, keepdims=True
        ).astype(i32)
        slots_ref[:, j : j + 1] = jnp.clip(slot, 0, CAP - 1)
    slots_ref[:, SLOTS:] = jnp.sum((path >= 0).astype(i32), axis=1, keepdims=True) - 1


def pack_kernel(picks_ref, src_ref, *out_refs):
    z = lax.axis_index("z")
    for d in range(PLANES):
        plane = lax.rem(z + d, PLANES)

        def one(k, carry):
            out_refs[d][k] = src_ref[picks_ref[k, plane]]
            return carry

        lax.fori_loop(0, CAP, one, 0, unroll=True)


def pick_kernel(idx_ref, src_ref, out_ref):
    def one(d, carry):
        for j in range(SLOTS):
            out_ref[d, j] = src_ref[idx_ref[d, j]]
        return carry

    lax.fori_loop(0, out_ref.shape[0], one, 0)


def attention(x_ref, k_ref, v_ref, alive, period, out_ref):
    k_ref[0:BLOCK] = x_ref[:, GROUP * HEAD_DIM : (GROUP + 1) * HEAD_DIM]
    v_ref[0:BLOCK, 0:HEAD_DIM] = x_ref[:, (GROUP + 1) * HEAD_DIM :]
    v_ref[:, HEAD_DIM:] = jnp.ones((k_ref.shape[0], HEAD_DIM), jnp.bfloat16)
    column = lax.broadcasted_iota(jnp.int32, (1, SLOTS * BLOCK), 1)
    bias = jnp.where((column // period) % SLOTS < alive, 0.0, NEG)
    row = lax.broadcasted_iota(jnp.int32, (BLOCK, BLOCK), 0)
    col = lax.broadcasted_iota(jnp.int32, (BLOCK, BLOCK), 1)
    for g in range(GROUP):
        cols = slice(g * HEAD_DIM, (g + 1) * HEAD_DIM)
        scores = lax.dot_general(
            x_ref[:, cols], k_ref[...], (((1,), (1,)), ((), ())), preferred_element_type=jnp.float32
        )
        near = jnp.where(col <= row, scores[:, :BLOCK], NEG)
        scores = jnp.concatenate([near, scores[:, BLOCK:] + bias], axis=1)
        top = jnp.max(scores, axis=1, keepdims=True)
        weights = jnp.exp2((scores - top) * EXP2_SCALE).astype(jnp.bfloat16)
        mixed = jnp.dot(weights, v_ref[...], preferred_element_type=jnp.float32)
        out_ref[:, cols] = (mixed[:, :HEAD_DIM] / mixed[:, HEAD_DIM:]).astype(jnp.bfloat16)


def own_member():
    return lax.axis_index("y") * 2 + lax.axis_index("xl")


def fill(k_ref, v_ref, at, slots_ref, m, here, there):
    def copy(dst_ref, parts):
        for j in range(SLOTS):
            slot = slots_ref[m, j]
            place = at + j * HALF
            for part in parts:
                size = part.shape[1]
                dst_ref[place : place + size, 0:HEAD_DIM] = part[slot]
                place += size

    core = lax.axis_index("c")

    @pl.when(core == 0)
    def _():
        copy(k_ref, here)
        copy(v_ref, there)

    @pl.when(core != 0)
    def _():
        copy(k_ref, there)
        copy(v_ref, here)


def dead_slots(alive):
    column = lax.broadcasted_iota(jnp.int32, (1, SLOTS * HALF), 1)
    return jnp.where(column // HALF < alive, 0.0, NEG)


def scored(x_ref, g, k_ref):
    q = x_ref[:, g * HEAD_DIM : (g + 1) * HEAD_DIM]
    return lax.dot_general(
        q, k_ref[...], (((1,), (1,)), ((), ())), preferred_element_type=jnp.float32
    )


def first_kernel(slots_ref, x_ref, *refs):
    here, there = refs[:GROUPS], refs[GROUPS : 2 * GROUPS]
    mix_ref, top_ref, sum_ref, k_ref, v_ref = refs[2 * GROUPS :]
    v_ref[:, HEAD_DIM:] = jnp.ones((BLOCK + SLOTS * HALF, HEAD_DIM), jnp.bfloat16)
    row = lax.broadcasted_iota(jnp.int32, (BLOCK, BLOCK), 0)
    col = lax.broadcasted_iota(jnp.int32, (BLOCK, BLOCK), 1)
    causal = col <= row

    def one(m, carry):
        fill(k_ref, v_ref, BLOCK, slots_ref, m, here, there)
        k_ref[0:BLOCK] = x_ref[m, :, GROUP * HEAD_DIM : (GROUP + 1) * HEAD_DIM]
        v_ref[0:BLOCK, 0:HEAD_DIM] = x_ref[m, :, (GROUP + 1) * HEAD_DIM :]
        bias = dead_slots(slots_ref[m, SLOTS])
        for g in range(GROUP):
            scores = scored(x_ref.at[m], g, k_ref)
            near = jnp.where(causal, scores[:, :BLOCK], NEG)
            scores = jnp.concatenate([near, scores[:, BLOCK:] + bias], axis=1)
            top = jnp.max(scores, axis=1, keepdims=True)
            weights = jnp.exp2((scores - top) * EXP2_SCALE).astype(jnp.bfloat16)
            mixed = jnp.dot(weights, v_ref[...], preferred_element_type=jnp.float32)
            mix_ref[m, g] = mixed[:, :HEAD_DIM]
            sum_ref[m, g] = mixed[:, HEAD_DIM : HEAD_DIM + 1]
            top_ref[m, g] = top
        return carry

    lax.fori_loop(0, KV_HEADS, one, 0)


def second_kernel(steps, slots_ref, x_ref, mix_ref, top_ref, sum_ref, *refs):
    here, there = refs[:GROUPS], refs[GROUPS : 2 * GROUPS]
    out_refs = refs[2 * GROUPS : 2 * GROUPS + len(steps)]
    k_refs, v_refs = refs[-2], refs[-1]
    for n, step in enumerate(steps):
        m = own_member() ^ step
        k_ref, v_ref, out_ref = k_refs.at[n], v_refs.at[n], out_refs[n]
        v_ref[:, HEAD_DIM:] = jnp.ones((SLOTS * HALF, HEAD_DIM), jnp.bfloat16)
        fill(k_ref, v_ref, 0, slots_ref, m, here, there)
    for n, step in enumerate(steps):
        m = own_member() ^ step
        k_ref, v_ref, out_ref = k_refs.at[n], v_refs.at[n], out_refs[n]
        bias = dead_slots(slots_ref[m, SLOTS])
        for g in range(GROUP):
            scores = scored(x_ref.at[m], g, k_ref) + bias
            before = top_ref[m, g]
            top = jnp.maximum(before, jnp.max(scores, axis=1, keepdims=True))
            weights = jnp.exp2((scores - top) * EXP2_SCALE).astype(jnp.bfloat16)
            mixed = jnp.dot(weights, v_ref[...], preferred_element_type=jnp.float32)
            keep = jnp.exp2((before - top) * EXP2_SCALE)
            total = mixed[:, HEAD_DIM:] + keep * sum_ref[m, g]
            mixed = mixed[:, :HEAD_DIM] + keep * mix_ref[m, g]
            out_ref[:, g * HEAD_DIM : (g + 1) * HEAD_DIM] = (mixed / total).astype(jnp.bfloat16)


def head_kernel(alive_ref, x_ref, far_k_ref, far_v_ref, out_ref, k_ref, v_ref):
    k_ref[BLOCK:] = far_k_ref[...]
    v_ref[BLOCK:, 0:HEAD_DIM] = far_v_ref[...]
    attention(x_ref, k_ref, v_ref, alive_ref[0], HALF, out_ref)


def join_kernel(*refs):
    out_ref, sems = refs[-2], refs[-1]
    width = GROUP * HEAD_DIM
    copies = []
    for step in range(KV_HEADS):
        at = pl.multiple_of((own_member() ^ step) * width, width)
        copies.append(
            pltpu.make_async_copy(refs[step], out_ref.at[:, pl.ds(at, width)], sems.at[step])
        )
    for copy in copies:
        copy.start()
    for copy in copies:
        copy.wait()


def quick(picks, slots, chunks, members):
    bf = jnp.bfloat16
    packs = pl.pallas_call(
        pack_kernel,
        out_shape=[jax.ShapeDtypeStruct((CAP, 8, HEAD_DIM), bf)] * PLANES,
        in_specs=[SMEM, VMEM],
        compiler_params=room(8),
    )(picks, chunks)
    swap = [(0, 1), (1, 0)]
    got = {0: packs[0]}
    for shifts in SHIFTS:
        for d in shifts:
            if d:
                pairs = [(i, (i + d) % PLANES) for i in range(PLANES)]
                got[d] = lax.ppermute(packs[d], "z", pairs)
    f32 = jnp.float32
    near = [
        jnp.stack([got[d] for d in shifts], axis=1).reshape(CAP, 8 * len(shifts), HEAD_DIM)
        for shifts in SHIFTS
    ]
    far, near_there = [], []
    for part in near:
        far.append(lax.ppermute(part, "xh", swap))
        near_there.append(lax.ppermute(part, "c", swap))
    keys = BLOCK + SLOTS * HALF
    running = pl.pallas_call(
        first_kernel,
        out_shape=(
            jax.ShapeDtypeStruct((KV_HEADS, GROUP, BLOCK, HEAD_DIM), f32),
            jax.ShapeDtypeStruct((KV_HEADS, GROUP, BLOCK, 1), f32),
            jax.ShapeDtypeStruct((KV_HEADS, GROUP, BLOCK, 1), f32),
        ),
        in_specs=[SMEM] + [VMEM] * (1 + 2 * GROUPS),
        out_specs=[VMEM] * 3,
        scratch_shapes=[pltpu.VMEM((keys, HEAD_DIM), bf), pltpu.VMEM((keys, 2 * HEAD_DIM), bf)],
        compiler_params=room(24),
        cost_estimate=pl.CostEstimate(flops=1 << 31, bytes_accessed=4 << 20, transcendentals=2 << 20),
    )(slots, members, *near, *near_there)
    far, running = lax.optimization_barrier((far, running))
    far_there = [lax.ppermute(part, "c", swap) for part in far]
    outs = {}
    for steps in STEPS:
        count = len(steps)
        keys = SLOTS * HALF
        results = pl.pallas_call(
            functools.partial(second_kernel, steps),
            out_shape=[jax.ShapeDtypeStruct((BLOCK, GROUP * HEAD_DIM), bf)] * count,
            in_specs=[SMEM] + [VMEM] * (4 + 2 * GROUPS),
            out_specs=[VMEM] * count,
            scratch_shapes=[
                pltpu.VMEM((count, keys, HEAD_DIM), bf),
                pltpu.VMEM((count, keys, 2 * HEAD_DIM), bf),
            ],
            compiler_params=room(24),
            cost_estimate=pl.CostEstimate(
                flops=1 << 29, bytes_accessed=1 << 20, transcendentals=1 << 19
            ),
        )(slots, members, *running, *far, *far_there)
        for step, out in zip(steps, results):
            pairs = [(m, m ^ step) for m in range(KV_HEADS)]
            outs[step] = lax.ppermute(out, HEAD_AXES, pairs) if step else out
    return [outs[step] for step in range(KV_HEADS)]


def join(outs, *unused):
    return pl.pallas_call(
        join_kernel,
        out_shape=jax.ShapeDtypeStruct((BLOCK, HEADS * HEAD_DIM), jnp.bfloat16),
        in_specs=[VMEM] * KV_HEADS,
        out_specs=HBM,
        scratch_shapes=[pltpu.SemaphoreType.DMA((KV_HEADS,))],
        compiler_params=room(8),
    )(*outs)


def general(outs, chunks, bundle, token_block, ancestors):
    bf = jnp.bfloat16
    span_blocks = token_block.reshape(DEVICES, BLOCK)[:, 0]
    ids = jnp.arange(DEVICES, dtype=jnp.int32)
    span_of = jnp.sum(jnp.where(span_blocks[:, None] == ids[None, :], ids[:, None], 0), axis=0)
    lineage = ancestors[span_blocks]
    depth = jnp.sum((lineage >= 0).astype(jnp.int32), axis=1)
    spans = span_of[jnp.maximum(lineage, 0)]
    alive = lax.dynamic_slice_in_dim(depth - 1, lax.axis_index(AXES), 1)
    packed = pl.pallas_call(
        pick_kernel,
        out_shape=jax.ShapeDtypeStruct((DEVICES, SLOTS, 8, HEAD_DIM), bf),
        in_specs=[SMEM, VMEM],
    )(spans, chunks)
    got = lax.all_to_all(packed.reshape(DEVICES, SLOTS * 8, HEAD_DIM), AXES, 0, 0, tiled=True)
    got = got.reshape(8, 2, 4, 2, 2, SLOTS, 8, HEAD_DIM).transpose(1, 2, 4, 3, 5, 0, 6, 7)
    got = got.reshape(2, KV_HEADS, SLOTS * BLOCK, HEAD_DIM)
    far_k = pl.BlockSpec((None, None, SLOTS * BLOCK, HEAD_DIM), lambda h: (0, h, 0, 0))
    far_v = pl.BlockSpec((None, None, SLOTS * BLOCK, HEAD_DIM), lambda h: (1, h, 0, 0))
    return pl.pallas_call(
        head_kernel,
        grid=(KV_HEADS,),
        out_shape=jax.ShapeDtypeStruct((BLOCK, HEADS * HEAD_DIM), bf),
        in_specs=[SMEM, pl.BlockSpec((None, BLOCK, PACK), lambda h: (h, 0, 0)), far_k, far_v],
        out_specs=pl.BlockSpec((BLOCK, GROUP * HEAD_DIM), lambda h: (0, h)),
        scratch_shapes=KV_SCRATCH,
    )(alive, bundle, got, got)


def shards(queries, keys, values, ancestors, token_block, positions):
    bf, f32, i32 = jnp.bfloat16, jnp.float32, jnp.int32
    send, cosine, sine, own_k = pl.pallas_call(
        spread_kernel,
        out_shape=(
            jax.ShapeDtypeStruct((8, 2, 4, 2, 2, 8, HEAD_DIM), bf),
            jax.ShapeDtypeStruct((BLOCK, HEAD_DIM), f32),
            jax.ShapeDtypeStruct((BLOCK, HEAD_DIM), f32),
            jax.ShapeDtypeStruct((BLOCK, KV_HEADS * HEAD_DIM), bf),
        ),
        in_specs=[HBM, VMEM, HBM, HBM],
        scratch_shapes=[
            pltpu.VMEM((BLOCK, KV_HEADS * HEAD_DIM), bf),
            pltpu.SMEM((BLOCK,), i32),
            pltpu.SemaphoreType.DMA((3,)),
        ],
    )(positions, jnp.asarray(inverse_row()), keys, values)
    chunks = lax.all_to_all(send.reshape(DEVICES, 8, HEAD_DIM), AXES, 0, 0, tiled=True)
    table = pl.BlockSpec((BLOCK, HEAD_DIM), lambda h: (0, 0))
    head = pl.BlockSpec((BLOCK, HEAD_DIM), lambda h: (0, h))
    picks, slots, count = pl.pallas_call(
        plan_kernel,
        out_shape=(
            jax.ShapeDtypeStruct((CAP, PLANES), i32),
            jax.ShapeDtypeStruct((8, ANC_MAX), i32),
            jax.ShapeDtypeStruct((1, 1), i32),
        ),
        in_specs=[VMEM, VMEM],
        compiler_params=room(8),
        cost_estimate=pl.CostEstimate(flops=4 << 20, bytes_accessed=4 << 20, transcendentals=0),
    )(token_block.reshape(DEVICES, BLOCK), ancestors.T)
    bundle = pl.pallas_call(
        bundle_kernel,
        grid=(KV_HEADS,),
        out_shape=jax.ShapeDtypeStruct((KV_HEADS, BLOCK, PACK), bf),
        in_specs=[VMEM_ONE, table, table, pl.BlockSpec((BLOCK, GROUP * HEAD_DIM), lambda h: (0, h)), head, head],
        out_specs=pl.BlockSpec((None, BLOCK, PACK), lambda h: (h, 0, 0)),
        compiler_params=room(8),
        cost_estimate=pl.CostEstimate(flops=4 << 20, bytes_accessed=4 << 20, transcendentals=0),
    )(count, cosine, sine, queries, own_k, values)
    members = lax.all_to_all(bundle, HEAD_AXES, 0, 0, tiled=True)
    fits = count[0, 0] <= CAP
    outs = quick(picks, slots, chunks, members)
    return lax.cond(fits, join, general, outs, chunks, bundle, token_block, ancestors)


def solution(mesh):
    fine = Mesh(mesh.devices.reshape(8, 2, 4, 2, 2), AXES)
    rows = P(AXES, None)

    return jax.shard_map(
        shards,
        mesh=fine,
        in_specs=(rows, rows, rows, P(), P(), P()),
        out_specs=rows,
        check_vma=False,
    )
```

```python
import functools

import jax
import jax.numpy as jnp
import numpy as np
from jax import lax
from jax.experimental import pallas as pl
from jax.experimental.pallas import tpu as pltpu
from jax.sharding import Mesh
from jax.sharding import PartitionSpec as P


HEADS = 32
KV_HEADS = 8
GROUP = HEADS // KV_HEADS
HEAD_DIM = 128
BLOCK = 128
ANC_MAX = 8
SLOTS = ANC_MAX - 1
DEVICES = 256
PLANES = 8
CAP = 34
HALF = BLOCK // 2
SHIFTS = ((0, 1, 7, 2), (6, 3, 5, 4))
GROUPS = len(SHIFTS)
KV_SCRATCH = [
    pltpu.VMEM((ANC_MAX * BLOCK, HEAD_DIM), jnp.bfloat16),
    pltpu.VMEM((ANC_MAX * BLOCK, 2 * HEAD_DIM), jnp.bfloat16),
]
PACK = (GROUP + 2) * HEAD_DIM
ROTARY_BASE = 500000.0
AXES = ("z", "c", "y", "xh", "xl")
HEAD_AXES = ("y", "xl")
NEG = -1e30
EXP2_SCALE = float(HEAD_DIM**-0.5 * np.log2(np.e))

HBM = pl.BlockSpec(memory_space=pltpu.HBM)
SMEM = pl.BlockSpec(memory_space=pltpu.SMEM)
VMEM = pl.BlockSpec(memory_space=pltpu.VMEM)
VMEM_ONE = pl.BlockSpec((1, 1), lambda h: (0, 0))


def room(mib):
    return pltpu.CompilerParams(vmem_limit_bytes=mib << 20)


def inverse_row():
    half = HEAD_DIM // 2
    inv = (ROTARY_BASE ** (-2.0 * np.arange(half, dtype=np.float64) / HEAD_DIM)).astype(np.float32)
    return np.concatenate([inv, inv])[None, :]


def turn(x, cosine, sine):
    x = x.astype(jnp.float32)
    return (x * cosine + pltpu.roll(x, HEAD_DIM // 2, 1) * sine).astype(jnp.bfloat16)


def device_index():
    z, c, y, xh, xl = [lax.axis_index(name) for name in AXES]
    return (((z * 2 + c) * 4 + y) * 2 + xh) * 2 + xl


def spread_kernel(
    pos_ref, inv_ref, k_hbm, v_hbm, send_ref, cos_ref, sin_ref, own_ref, v_ref, base_ref, sems
):
    start = pl.multiple_of(device_index() * BLOCK, BLOCK)
    loads = [
        pltpu.make_async_copy(pos_ref.at[pl.ds(start, BLOCK)], base_ref, sems.at[0]),
        pltpu.make_async_copy(k_hbm, own_ref, sems.at[1]),
        pltpu.make_async_copy(v_hbm, v_ref, sems.at[2]),
    ]
    for load in loads:
        load.start()
    loads[0].wait()
    rows = lax.broadcasted_iota(jnp.int32, (BLOCK, HEAD_DIM), 0) + base_ref[0]
    lanes = lax.broadcasted_iota(jnp.int32, (BLOCK, HEAD_DIM), 1)
    angles = rows.astype(jnp.float32) * inv_ref[...]
    cosine = jnp.cos(angles)
    sine = jnp.sin(angles)
    sine = jnp.where(lanes < HEAD_DIM // 2, -sine, sine)
    cos_ref[...] = cosine
    sin_ref[...] = sine
    loads[1].wait()
    loads[2].wait()
    for h in range(KV_HEADS):
        cols = slice(h * HEAD_DIM, (h + 1) * HEAD_DIM)
        turned = turn(own_ref[:, cols], cosine, sine)
        own_ref[:, cols] = turned
        plain = v_ref[:, cols]
        for high in range(2):
            for low in range(8):
                t = (high * 8 + low) * 8
                send_ref[low, 0, h // 2, high, h % 2] = turned[t : t + 8]
                send_ref[low, 1, h // 2, high, h % 2] = plain[t : t + 8]


def bundle_kernel(count_ref, cos_ref, sin_ref, q_ref, k_ref, v_ref, out_ref):
    for g in range(GROUP):
        cols = slice(g * HEAD_DIM, (g + 1) * HEAD_DIM)
        out_ref[:, cols] = turn(q_ref[:, cols], cos_ref[...], sin_ref[...])
    out_ref[:, GROUP * HEAD_DIM : (GROUP + 1) * HEAD_DIM] = k_ref[...]
    out_ref[:, (GROUP + 1) * HEAD_DIM :] = v_ref[...]


def plan_kernel(token_ref, anc_ref, picks_ref, slots_ref, count_ref):
    n = DEVICES
    f32, bf, i32 = jnp.float32, jnp.bfloat16, jnp.int32
    across = (((1,), (1,)), ((), ()))
    anc = anc_ref[...]
    col = token_ref[:, 0:1]
    lane = lax.broadcasted_iota(i32, (n, n), 1)
    sub = lax.broadcasted_iota(i32, (n, n), 0)
    row = jnp.sum(jnp.where(sub == lane, col, 0), axis=0, keepdims=True)
    depth = jnp.sum((anc >= 0).astype(i32), axis=0, keepdims=True)
    holds = jnp.zeros((n, n), f32)
    for j in range(SLOTS):
        entry = jnp.where(j < depth - 1, anc[j : j + 1], -1)
        holds = jnp.where(entry == col, 1.0, holds)
    block_at = (col == lane).astype(f32).astype(bf)
    plane8 = lax.broadcasted_iota(i32, (PLANES, n), 0)
    lane8 = lax.broadcasted_iota(i32, (PLANES, n), 1)
    in_plane = (lane8 // (n // PLANES) == plane8).astype(f32).astype(bf)
    blocks = jnp.dot(in_plane, block_at, preferred_element_type=f32)
    need = lax.dot_general(
        blocks.astype(bf), holds.astype(bf), across, preferred_element_type=f32
    )
    needed = (need > 0.5).astype(f32)
    upto = (sub <= lane).astype(f32).astype(bf)
    ranks = jnp.dot(needed.astype(bf), upto, preferred_element_type=f32)
    count_ref[...] = jnp.max(ranks, axis=(0, 1), keepdims=True).astype(i32)
    ranks = ranks - 1.0
    wanted = lax.broadcasted_iota(i32, (CAP, n), 0).astype(f32)
    span = lax.broadcasted_iota(i32, (CAP, n), 1).astype(f32)
    for z in range(PLANES):
        hit = (ranks[z : z + 1] == wanted) & (needed[z : z + 1] > 0.5)
        picks_ref[:, z : z + 1] = jnp.sum(
            jnp.where(hit, span, 0.0), axis=1, keepdims=True
        ).astype(i32)
    z, c, xh = lax.axis_index("z"), lax.axis_index("c"), lax.axis_index("xh")
    mine = z * 32 + c * 16 + (plane8 // 2) * 4 + xh * 2 + plane8 % 2
    own_block = jnp.dot(
        (lane8 == mine).astype(f32).astype(bf), block_at, preferred_element_type=f32
    )
    path = lax.dot_general(
        own_block.astype(bf), anc.astype(f32).astype(bf), across, preferred_element_type=f32
    ).astype(i32)
    my_rank = jnp.sum(jnp.where(plane8 == z, ranks, 0.0), axis=0, keepdims=True)
    for j in range(SLOTS):
        slot = jnp.sum(
            jnp.where(path[:, j : j + 1] == row, my_rank, 0.0), axis=1, keepdims=True
        ).astype(i32)
        slots_ref[:, j : j + 1] = jnp.clip(slot, 0, CAP - 1)
    slots_ref[:, SLOTS:] = jnp.sum((path >= 0).astype(i32), axis=1, keepdims=True) - 1


def pack_kernel(picks_ref, src_ref, *out_refs):
    z = lax.axis_index("z")
    for d in range(PLANES):
        plane = lax.rem(z + d, PLANES)

        def one(k, carry):
            out_refs[d][k] = src_ref[picks_ref[k, plane]]
            return carry

        lax.fori_loop(0, CAP, one, 0, unroll=True)


def pick_kernel(idx_ref, src_ref, out_ref):
    def one(d, carry):
        for j in range(SLOTS):
            out_ref[d, j] = src_ref[idx_ref[d, j]]
        return carry

    lax.fori_loop(0, out_ref.shape[0], one, 0)


def attention(x_ref, k_ref, v_ref, alive, period, out_ref):
    k_ref[0:BLOCK] = x_ref[:, GROUP * HEAD_DIM : (GROUP + 1) * HEAD_DIM]
    v_ref[0:BLOCK, 0:HEAD_DIM] = x_ref[:, (GROUP + 1) * HEAD_DIM :]
    v_ref[:, HEAD_DIM:] = jnp.ones((k_ref.shape[0], HEAD_DIM), jnp.bfloat16)
    column = lax.broadcasted_iota(jnp.int32, (1, SLOTS * BLOCK), 1)
    bias = jnp.where((column // period) % SLOTS < alive, 0.0, NEG)
    row = lax.broadcasted_iota(jnp.int32, (BLOCK, BLOCK), 0)
    col = lax.broadcasted_iota(jnp.int32, (BLOCK, BLOCK), 1)
    for g in range(GROUP):
        cols = slice(g * HEAD_DIM, (g + 1) * HEAD_DIM)
        scores = lax.dot_general(
            x_ref[:, cols], k_ref[...], (((1,), (1,)), ((), ())), preferred_element_type=jnp.float32
        )
        near = jnp.where(col <= row, scores[:, :BLOCK], NEG)
        scores = jnp.concatenate([near, scores[:, BLOCK:] + bias], axis=1)
        top = jnp.max(scores, axis=1, keepdims=True)
        weights = jnp.exp2((scores - top) * EXP2_SCALE).astype(jnp.bfloat16)
        mixed = jnp.dot(weights, v_ref[...], preferred_element_type=jnp.float32)
        out_ref[:, cols] = (mixed[:, :HEAD_DIM] / mixed[:, HEAD_DIM:]).astype(jnp.bfloat16)


def own_member():
    return lax.axis_index("y") * 2 + lax.axis_index("xl")


def fill(k_ref, v_ref, at, slots_ref, m, here, there):
    def copy(dst_ref, parts):
        for j in range(SLOTS):
            slot = slots_ref[m, j]
            place = at + j * HALF
            for part in parts:
                size = part.shape[1]
                dst_ref[place : place + size, 0:HEAD_DIM] = part[slot]
                place += size

    core = lax.axis_index("c")

    @pl.when(core == 0)
    def _():
        copy(k_ref, here)
        copy(v_ref, there)

    @pl.when(core != 0)
    def _():
        copy(k_ref, there)
        copy(v_ref, here)


def dead_slots(alive):
    column = lax.broadcasted_iota(jnp.int32, (1, SLOTS * HALF), 1)
    return jnp.where(column // HALF < alive, 0.0, NEG)


def scored(x_ref, g, k_ref):
    q = x_ref[:, g * HEAD_DIM : (g + 1) * HEAD_DIM]
    return lax.dot_general(
        q, k_ref[...], (((1,), (1,)), ((), ())), preferred_element_type=jnp.float32
    )


def first_kernel(slots_ref, x_ref, *refs):
    here, there = refs[:GROUPS], refs[GROUPS : 2 * GROUPS]
    mix_ref, top_ref, sum_ref, k_ref, v_ref = refs[2 * GROUPS :]
    v_ref[:, HEAD_DIM:] = jnp.ones((BLOCK + SLOTS * HALF, HEAD_DIM), jnp.bfloat16)
    row = lax.broadcasted_iota(jnp.int32, (BLOCK, BLOCK), 0)
    col = lax.broadcasted_iota(jnp.int32, (BLOCK, BLOCK), 1)
    causal = col <= row

    def one(m, carry):
        fill(k_ref, v_ref, BLOCK, slots_ref, m, here, there)
        k_ref[0:BLOCK] = x_ref[m, :, GROUP * HEAD_DIM : (GROUP + 1) * HEAD_DIM]
        v_ref[0:BLOCK, 0:HEAD_DIM] = x_ref[m, :, (GROUP + 1) * HEAD_DIM :]
        bias = dead_slots(slots_ref[m, SLOTS])
        for g in range(GROUP):
            scores = scored(x_ref.at[m], g, k_ref)
            near = jnp.where(causal, scores[:, :BLOCK], NEG)
            scores = jnp.concatenate([near, scores[:, BLOCK:] + bias], axis=1)
            top = jnp.max(scores, axis=1, keepdims=True)
            weights = jnp.exp2((scores - top) * EXP2_SCALE).astype(jnp.bfloat16)
            mixed = jnp.dot(weights, v_ref[...], preferred_element_type=jnp.float32)
            mix_ref[m, g] = mixed[:, :HEAD_DIM]
            sum_ref[m, g] = mixed[:, HEAD_DIM : HEAD_DIM + 1]
            top_ref[m, g] = top
        return carry

    lax.fori_loop(0, KV_HEADS, one, 0)


def second_kernel(mask, slots_ref, x_ref, mix_ref, top_ref, sum_ref, *refs):
    here, there = refs[:GROUPS], refs[GROUPS : 2 * GROUPS]
    out_refs, (k_ref, v_ref, done_ref) = refs[2 * GROUPS : -3], refs[-3:]
    v_ref[:, HEAD_DIM:] = jnp.ones((SLOTS * HALF, HEAD_DIM), jnp.bfloat16)

    def one(n, carry):
        m = own_member() ^ mask ^ n
        fill(k_ref, v_ref, 0, slots_ref, m, here, there)
        bias = dead_slots(slots_ref[m, SLOTS])
        for g in range(GROUP):
            scores = scored(x_ref.at[m], g, k_ref) + bias
            before = top_ref[m, g]
            top = jnp.maximum(before, jnp.max(scores, axis=1, keepdims=True))
            weights = jnp.exp2((scores - top) * EXP2_SCALE).astype(jnp.bfloat16)
            mixed = jnp.dot(weights, v_ref[...], preferred_element_type=jnp.float32)
            keep = jnp.exp2((before - top) * EXP2_SCALE)
            total = mixed[:, HEAD_DIM:] + keep * sum_ref[m, g]
            mixed = mixed[:, :HEAD_DIM] + keep * mix_ref[m, g]
            cols = slice(g * HEAD_DIM, (g + 1) * HEAD_DIM)
            done_ref[n, :, cols] = (mixed / total).astype(jnp.bfloat16)
        return carry

    lax.fori_loop(0, len(out_refs), one, 0)
    for n, out_ref in enumerate(out_refs):
        out_ref[...] = done_ref[n]


def head_kernel(alive_ref, x_ref, far_k_ref, far_v_ref, out_ref, k_ref, v_ref):
    k_ref[BLOCK:] = far_k_ref[...]
    v_ref[BLOCK:, 0:HEAD_DIM] = far_v_ref[...]
    attention(x_ref, k_ref, v_ref, alive_ref[0], HALF, out_ref)


def join_kernel(*refs):
    out_ref, sems = refs[-2], refs[-1]
    width = GROUP * HEAD_DIM
    copies = []
    for step in range(KV_HEADS):
        at = pl.multiple_of((own_member() ^ step) * width, width)
        copies.append(
            pltpu.make_async_copy(refs[step], out_ref.at[:, pl.ds(at, width)], sems.at[step])
        )
    for copy in copies:
        copy.start()
    for copy in copies:
        copy.wait()


def quick(picks, slots, chunks, members):
    bf = jnp.bfloat16
    packs = pl.pallas_call(
        pack_kernel,
        out_shape=[jax.ShapeDtypeStruct((CAP, 8, HEAD_DIM), bf)] * PLANES,
        in_specs=[SMEM, VMEM],
        compiler_params=room(8),
    )(picks, chunks)
    swap = [(0, 1), (1, 0)]
    got = {0: packs[0]}
    for shifts in SHIFTS:
        for d in shifts:
            if d:
                pairs = [(i, (i + d) % PLANES) for i in range(PLANES)]
                got[d] = lax.ppermute(packs[d], "z", pairs)
    f32 = jnp.float32
    near = [
        jnp.stack([got[d] for d in shifts], axis=1).reshape(CAP, 8 * len(shifts), HEAD_DIM)
        for shifts in SHIFTS
    ]
    far, near_there = [], []
    for part in near:
        far.append(lax.ppermute(part, "xh", swap))
        near_there.append(lax.ppermute(part, "c", swap))
    keys = BLOCK + SLOTS * HALF
    running = pl.pallas_call(
        first_kernel,
        out_shape=(
            jax.ShapeDtypeStruct((KV_HEADS, GROUP, BLOCK, HEAD_DIM), f32),
            jax.ShapeDtypeStruct((KV_HEADS, GROUP, BLOCK, 1), f32),
            jax.ShapeDtypeStruct((KV_HEADS, GROUP, BLOCK, 1), f32),
        ),
        in_specs=[SMEM] + [VMEM] * (1 + 2 * GROUPS),
        out_specs=[VMEM] * 3,
        scratch_shapes=[pltpu.VMEM((keys, HEAD_DIM), bf), pltpu.VMEM((keys, 2 * HEAD_DIM), bf)],
        compiler_params=room(24),
        cost_estimate=pl.CostEstimate(flops=1 << 31, bytes_accessed=4 << 20, transcendentals=2 << 20),
    )(slots, members, *near, *near_there)
    far, running = lax.optimization_barrier((far, running))
    far_there = [lax.ppermute(part, "c", swap) for part in far]
    outs = {}
    keys = SLOTS * HALF
    shape = (BLOCK, GROUP * HEAD_DIM)
    for mask in (4, 0):
        results = pl.pallas_call(
            functools.partial(second_kernel, mask),
            out_shape=[jax.ShapeDtypeStruct(shape, bf)] * 4,
            in_specs=[SMEM] + [VMEM] * (4 + 2 * GROUPS),
            out_specs=[VMEM] * 4,
            scratch_shapes=[
                pltpu.VMEM((keys, HEAD_DIM), bf),
                pltpu.VMEM((keys, 2 * HEAD_DIM), bf),
                pltpu.VMEM((4,) + shape, bf),
            ],
            compiler_params=room(24),
            cost_estimate=pl.CostEstimate(
                flops=1 << 30, bytes_accessed=1 << 21, transcendentals=1 << 20
            ),
        )(slots, members, *running, *far, *far_there)
        for n, out in enumerate(results):
            step = mask ^ n
            pairs = [(m, m ^ step) for m in range(KV_HEADS)]
            outs[step] = lax.ppermute(out, HEAD_AXES, pairs) if step else out
    return [outs[step] for step in range(KV_HEADS)]


def join(outs, *unused):
    return pl.pallas_call(
        join_kernel,
        out_shape=jax.ShapeDtypeStruct((BLOCK, HEADS * HEAD_DIM), jnp.bfloat16),
        in_specs=[VMEM] * KV_HEADS,
        out_specs=HBM,
        scratch_shapes=[pltpu.SemaphoreType.DMA((KV_HEADS,))],
        compiler_params=pltpu.CompilerParams(vmem_limit_bytes=67043328),
    )(*outs)


def general(outs, chunks, bundle, token_block, ancestors):
    bf = jnp.bfloat16
    span_blocks = token_block.reshape(DEVICES, BLOCK)[:, 0]
    ids = jnp.arange(DEVICES, dtype=jnp.int32)
    span_of = jnp.sum(jnp.where(span_blocks[:, None] == ids[None, :], ids[:, None], 0), axis=0)
    lineage = ancestors[span_blocks]
    depth = jnp.sum((lineage >= 0).astype(jnp.int32), axis=1)
    spans = span_of[jnp.maximum(lineage, 0)]
    alive = lax.dynamic_slice_in_dim(depth - 1, lax.axis_index(AXES), 1)
    packed = pl.pallas_call(
        pick_kernel,
        out_shape=jax.ShapeDtypeStruct((DEVICES, SLOTS, 8, HEAD_DIM), bf),
        in_specs=[SMEM, VMEM],
    )(spans, chunks)
    got = lax.all_to_all(packed.reshape(DEVICES, SLOTS * 8, HEAD_DIM), AXES, 0, 0, tiled=True)
    got = got.reshape(8, 2, 4, 2, 2, SLOTS, 8, HEAD_DIM).transpose(1, 2, 4, 3, 5, 0, 6, 7)
    got = got.reshape(2, KV_HEADS, SLOTS * BLOCK, HEAD_DIM)
    far_k = pl.BlockSpec((None, None, SLOTS * BLOCK, HEAD_DIM), lambda h: (0, h, 0, 0))
    far_v = pl.BlockSpec((None, None, SLOTS * BLOCK, HEAD_DIM), lambda h: (1, h, 0, 0))
    return pl.pallas_call(
        head_kernel,
        grid=(KV_HEADS,),
        out_shape=jax.ShapeDtypeStruct((BLOCK, HEADS * HEAD_DIM), bf),
        in_specs=[SMEM, pl.BlockSpec((None, BLOCK, PACK), lambda h: (h, 0, 0)), far_k, far_v],
        out_specs=pl.BlockSpec((BLOCK, GROUP * HEAD_DIM), lambda h: (0, h)),
        scratch_shapes=KV_SCRATCH,
    )(alive, bundle, got, got)


def shards(queries, keys, values, ancestors, token_block, positions):
    bf, f32, i32 = jnp.bfloat16, jnp.float32, jnp.int32
    send, cosine, sine, own_k = pl.pallas_call(
        spread_kernel,
        out_shape=(
            jax.ShapeDtypeStruct((8, 2, 4, 2, 2, 8, HEAD_DIM), bf),
            jax.ShapeDtypeStruct((BLOCK, HEAD_DIM), f32),
            jax.ShapeDtypeStruct((BLOCK, HEAD_DIM), f32),
            jax.ShapeDtypeStruct((BLOCK, KV_HEADS * HEAD_DIM), bf),
        ),
        in_specs=[HBM, VMEM, HBM, HBM],
        scratch_shapes=[
            pltpu.VMEM((BLOCK, KV_HEADS * HEAD_DIM), bf),
            pltpu.SMEM((BLOCK,), i32),
            pltpu.SemaphoreType.DMA((3,)),
        ],
    )(positions, jnp.asarray(inverse_row()), keys, values)
    chunks = lax.all_to_all(send.reshape(DEVICES, 8, HEAD_DIM), AXES, 0, 0, tiled=True)
    table = pl.BlockSpec((BLOCK, HEAD_DIM), lambda h: (0, 0))
    head = pl.BlockSpec((BLOCK, HEAD_DIM), lambda h: (0, h))
    picks, slots, count = pl.pallas_call(
        plan_kernel,
        out_shape=(
            jax.ShapeDtypeStruct((CAP, PLANES), i32),
            jax.ShapeDtypeStruct((8, ANC_MAX), i32),
            jax.ShapeDtypeStruct((1, 1), i32),
        ),
        in_specs=[VMEM, VMEM],
        compiler_params=room(8),
        cost_estimate=pl.CostEstimate(flops=4 << 20, bytes_accessed=4 << 20, transcendentals=0),
    )(token_block.reshape(DEVICES, BLOCK), ancestors.T)
    bundle = pl.pallas_call(
        bundle_kernel,
        grid=(KV_HEADS,),
        out_shape=jax.ShapeDtypeStruct((KV_HEADS, BLOCK, PACK), bf),
        in_specs=[VMEM_ONE, table, table, pl.BlockSpec((BLOCK, GROUP * HEAD_DIM), lambda h: (0, h)), head, head],
        out_specs=pl.BlockSpec((None, BLOCK, PACK), lambda h: (h, 0, 0)),
        compiler_params=room(8),
        cost_estimate=pl.CostEstimate(flops=4 << 20, bytes_accessed=4 << 20, transcendentals=0),
    )(count, cosine, sine, queries, own_k, values)
    members = lax.all_to_all(bundle, HEAD_AXES, 0, 0, tiled=True)
    fits = count[0, 0] <= CAP
    outs = quick(picks, slots, chunks, members)
    return lax.cond(fits, join, general, outs, chunks, bundle, token_block, ancestors)


def solution(mesh):
    fine = Mesh(mesh.devices.reshape(8, 2, 4, 2, 2), AXES)
    rows = P(AXES, None)

    return jax.shard_map(
        shards,
        mesh=fine,
        in_specs=(rows, rows, rows, P(), P(), P()),
        out_specs=rows,
        check_vma=False,
    )
```

```python
import functools

import jax
import jax.numpy as jnp
import numpy as np
from jax import lax
from jax.experimental import pallas as pl
from jax.experimental.pallas import tpu as pltpu
from jax.sharding import Mesh
from jax.sharding import PartitionSpec as P


HEADS = 32
KV_HEADS = 8
GROUP = HEADS // KV_HEADS
HEAD_DIM = 128
BLOCK = 128
ANC_MAX = 8
SLOTS = ANC_MAX - 1
DEVICES = 256
PLANES = 8
CAP = 34
HALF = BLOCK // 2
SHIFTS = ((0, 1, 7, 2), (6, 3, 5, 4))
GROUPS = len(SHIFTS)
KV_SCRATCH = [
    pltpu.VMEM((ANC_MAX * BLOCK, HEAD_DIM), jnp.bfloat16),
    pltpu.VMEM((ANC_MAX * BLOCK, 2 * HEAD_DIM), jnp.bfloat16),
]
PACK = (GROUP + 2) * HEAD_DIM
ROTARY_BASE = 500000.0
AXES = ("z", "c", "y", "xh", "xl")
HEAD_AXES = ("y", "xl")
NEG = -1e30
EXP2_SCALE = float(HEAD_DIM**-0.5 * np.log2(np.e))

HBM = pl.BlockSpec(memory_space=pltpu.HBM)
SMEM = pl.BlockSpec(memory_space=pltpu.SMEM)
VMEM = pl.BlockSpec(memory_space=pltpu.VMEM)
VMEM_ONE = pl.BlockSpec((1, 1), lambda h: (0, 0))


def room(mib):
    return pltpu.CompilerParams(vmem_limit_bytes=mib << 20)


def inverse_row():
    half = HEAD_DIM // 2
    inv = (ROTARY_BASE ** (-2.0 * np.arange(half, dtype=np.float64) / HEAD_DIM)).astype(np.float32)
    return np.concatenate([inv, inv])[None, :]


def turn(x, cosine, sine):
    x = x.astype(jnp.float32)
    return (x * cosine + pltpu.roll(x, HEAD_DIM // 2, 1) * sine).astype(jnp.bfloat16)


def device_index():
    z, c, y, xh, xl = [lax.axis_index(name) for name in AXES]
    return (((z * 2 + c) * 4 + y) * 2 + xh) * 2 + xl


def spread_kernel(
    pos_ref, inv_ref, k_hbm, v_hbm, send_ref, cos_ref, sin_ref, own_ref, v_ref, base_ref, sems
):
    start = pl.multiple_of(device_index() * BLOCK, BLOCK)
    loads = [
        pltpu.make_async_copy(pos_ref.at[pl.ds(start, BLOCK)], base_ref, sems.at[0]),
        pltpu.make_async_copy(k_hbm, own_ref, sems.at[1]),
        pltpu.make_async_copy(v_hbm, v_ref, sems.at[2]),
    ]
    for load in loads:
        load.start()
    loads[0].wait()
    rows = lax.broadcasted_iota(jnp.int32, (BLOCK, HEAD_DIM), 0) + base_ref[0]
    lanes = lax.broadcasted_iota(jnp.int32, (BLOCK, HEAD_DIM), 1)
    angles = rows.astype(jnp.float32) * inv_ref[...]
    cosine = jnp.cos(angles)
    sine = jnp.sin(angles)
    sine = jnp.where(lanes < HEAD_DIM // 2, -sine, sine)
    cos_ref[...] = cosine
    sin_ref[...] = sine
    loads[1].wait()
    loads[2].wait()
    for h in range(KV_HEADS):
        cols = slice(h * HEAD_DIM, (h + 1) * HEAD_DIM)
        turned = turn(own_ref[:, cols], cosine, sine)
        own_ref[:, cols] = turned
        plain = v_ref[:, cols]
        for high in range(2):
            for low in range(8):
                t = (high * 8 + low) * 8
                send_ref[low, 0, h // 2, high, h % 2] = turned[t : t + 8]
                send_ref[low, 1, h // 2, high, h % 2] = plain[t : t + 8]


def bundle_kernel(count_ref, cos_ref, sin_ref, q_ref, k_ref, v_ref, out_ref):
    for g in range(GROUP):
        cols = slice(g * HEAD_DIM, (g + 1) * HEAD_DIM)
        out_ref[:, cols] = turn(q_ref[:, cols], cos_ref[...], sin_ref[...])
    out_ref[:, GROUP * HEAD_DIM : (GROUP + 1) * HEAD_DIM] = k_ref[...]
    out_ref[:, (GROUP + 1) * HEAD_DIM :] = v_ref[...]


def plan_kernel(token_ref, anc_ref, picks_ref, slots_ref, count_ref):
    n = DEVICES
    f32, bf, i32 = jnp.float32, jnp.bfloat16, jnp.int32
    across = (((1,), (1,)), ((), ()))
    anc = anc_ref[...]
    col = token_ref[:, 0:1]
    lane = lax.broadcasted_iota(i32, (n, n), 1)
    sub = lax.broadcasted_iota(i32, (n, n), 0)
    row = jnp.sum(jnp.where(sub == lane, col, 0), axis=0, keepdims=True)
    depth = jnp.sum((anc >= 0).astype(i32), axis=0, keepdims=True)
    holds = jnp.zeros((n, n), f32)
    for j in range(SLOTS):
        entry = jnp.where(j < depth - 1, anc[j : j + 1], -1)
        holds = jnp.where(entry == col, 1.0, holds)
    block_at = (col == lane).astype(f32).astype(bf)
    plane8 = lax.broadcasted_iota(i32, (PLANES, n), 0)
    lane8 = lax.broadcasted_iota(i32, (PLANES, n), 1)
    in_plane = (lane8 // (n // PLANES) == plane8).astype(f32).astype(bf)
    blocks = jnp.dot(in_plane, block_at, preferred_element_type=f32)
    need = lax.dot_general(
        blocks.astype(bf), holds.astype(bf), across, preferred_element_type=f32
    )
    needed = (need > 0.5).astype(f32)
    upto = (sub <= lane).astype(f32).astype(bf)
    ranks = jnp.dot(needed.astype(bf), upto, preferred_element_type=f32)
    count_ref[...] = jnp.max(ranks, axis=(0, 1), keepdims=True).astype(i32)
    ranks = ranks - 1.0
    wanted = lax.broadcasted_iota(i32, (CAP, n), 0).astype(f32)
    span = lax.broadcasted_iota(i32, (CAP, n), 1).astype(f32)
    for z in range(PLANES):
        hit = (ranks[z : z + 1] == wanted) & (needed[z : z + 1] > 0.5)
        picks_ref[:, z : z + 1] = jnp.sum(
            jnp.where(hit, span, 0.0), axis=1, keepdims=True
        ).astype(i32)
    z, c, xh = lax.axis_index("z"), lax.axis_index("c"), lax.axis_index("xh")
    mine = z * 32 + c * 16 + (plane8 // 2) * 4 + xh * 2 + plane8 % 2
    own_block = jnp.dot(
        (lane8 == mine).astype(f32).astype(bf), block_at, preferred_element_type=f32
    )
    path = lax.dot_general(
        own_block.astype(bf), anc.astype(f32).astype(bf), across, preferred_element_type=f32
    ).astype(i32)
    my_rank = jnp.sum(jnp.where(plane8 == z, ranks, 0.0), axis=0, keepdims=True)
    for j in range(SLOTS):
        slot = jnp.sum(
            jnp.where(path[:, j : j + 1] == row, my_rank, 0.0), axis=1, keepdims=True
        ).astype(i32)
        slots_ref[:, j : j + 1] = jnp.clip(slot, 0, CAP - 1)
    slots_ref[:, SLOTS:] = jnp.sum((path >= 0).astype(i32), axis=1, keepdims=True) - 1


def pack_kernel(picks_ref, src_ref, *out_refs):
    z = lax.axis_index("z")
    for d in range(PLANES):
        plane = lax.rem(z + d, PLANES)

        def one(k, carry):
            out_refs[d][k] = src_ref[picks_ref[k, plane]]
            return carry

        lax.fori_loop(0, CAP, one, 0, unroll=True)


def pick_kernel(idx_ref, src_ref, out_ref):
    def one(d, carry):
        for j in range(SLOTS):
            out_ref[d, j] = src_ref[idx_ref[d, j]]
        return carry

    lax.fori_loop(0, out_ref.shape[0], one, 0)


def attention(x_ref, k_ref, v_ref, alive, period, out_ref):
    k_ref[0:BLOCK] = x_ref[:, GROUP * HEAD_DIM : (GROUP + 1) * HEAD_DIM]
    v_ref[0:BLOCK, 0:HEAD_DIM] = x_ref[:, (GROUP + 1) * HEAD_DIM :]
    column = lax.broadcasted_iota(jnp.int32, (1, SLOTS * BLOCK), 1)
    bias = jnp.where((column // period) % SLOTS < alive, 0.0, NEG)
    row = lax.broadcasted_iota(jnp.int32, (BLOCK, BLOCK), 0)
    col = lax.broadcasted_iota(jnp.int32, (BLOCK, BLOCK), 1)
    causal = col <= row
    cols = [slice(g * HEAD_DIM, (g + 1) * HEAD_DIM) for g in range(GROUP)]
    scores = [
        lax.dot_general(
            x_ref[:, at], k_ref[...], (((1,), (1,)), ((), ())), preferred_element_type=jnp.float32
        )
        for at in cols
    ]
    scores = [
        jnp.concatenate([jnp.where(causal, s[:, :BLOCK], NEG), s[:, BLOCK:] + bias], axis=1)
        for s in scores
    ]
    tops = [jnp.max(s, axis=1, keepdims=True) for s in scores]
    weights = [
        jnp.exp2((s - top) * EXP2_SCALE).astype(jnp.bfloat16) for s, top in zip(scores, tops)
    ]
    for at, w in zip(cols, weights):
        mixed = jnp.dot(w, v_ref[...], preferred_element_type=jnp.float32)
        out_ref[:, at] = (mixed[:, :HEAD_DIM] / mixed[:, HEAD_DIM:]).astype(jnp.bfloat16)


def own_member():
    return lax.axis_index("y") * 2 + lax.axis_index("xl")


def fill(k_ref, v_ref, slots_ref, m, here, there):
    def copy(dst_ref, parts):
        for j in range(SLOTS):
            slot = slots_ref[m, j]
            at = (j + 1) * BLOCK
            for part in parts:
                size = part.shape[1]
                dst_ref[at : at + size, 0:HEAD_DIM] = part[slot]
                at += size

    core = lax.axis_index("c")

    @pl.when(core == 0)
    def _():
        copy(k_ref, here)
        copy(v_ref, there)

    @pl.when(core != 0)
    def _():
        copy(k_ref, there)
        copy(v_ref, here)


def span_kernel(mask, slots_ref, x_ref, *refs):
    here, there = refs[: 2 * GROUPS], refs[2 * GROUPS : 4 * GROUPS]
    out_refs, (k_ref, v_ref, done_ref) = refs[4 * GROUPS : -3], refs[-3:]
    v_ref[:, HEAD_DIM:] = jnp.ones((ANC_MAX * BLOCK, HEAD_DIM), jnp.bfloat16)

    def one(n, carry):
        m = own_member() ^ mask ^ n
        fill(k_ref, v_ref, slots_ref, m, here, there)
        attention(x_ref.at[m], k_ref, v_ref, slots_ref[m, SLOTS], BLOCK, done_ref.at[n])
        return carry

    lax.fori_loop(0, len(out_refs), one, 0)
    for n, out_ref in enumerate(out_refs):
        out_ref[...] = done_ref[n]


def head_kernel(alive_ref, x_ref, far_k_ref, far_v_ref, out_ref, k_ref, v_ref):
    v_ref[:, HEAD_DIM:] = jnp.ones((ANC_MAX * BLOCK, HEAD_DIM), jnp.bfloat16)
    k_ref[BLOCK:] = far_k_ref[...]
    v_ref[BLOCK:, 0:HEAD_DIM] = far_v_ref[...]
    attention(x_ref, k_ref, v_ref, alive_ref[0], HALF, out_ref)


def join_kernel(*refs):
    out_ref, sems = refs[-2], refs[-1]
    width = GROUP * HEAD_DIM
    copies = []
    for step in range(KV_HEADS):
        at = pl.multiple_of((own_member() ^ step) * width, width)
        copies.append(
            pltpu.make_async_copy(refs[step], out_ref.at[:, pl.ds(at, width)], sems.at[step])
        )
    for copy in copies:
        copy.start()
    for copy in copies:
        copy.wait()


def quick(picks, slots, chunks, members):
    bf = jnp.bfloat16
    packs = pl.pallas_call(
        pack_kernel,
        out_shape=[jax.ShapeDtypeStruct((CAP, 8, HEAD_DIM), bf)] * PLANES,
        in_specs=[SMEM, VMEM],
        compiler_params=room(8),
    )(picks, chunks)
    swap = [(0, 1), (1, 0)]
    got = {0: packs[0]}
    for shifts in SHIFTS:
        for d in shifts:
            if d:
                pairs = [(i, (i + d) % PLANES) for i in range(PLANES)]
                got[d] = lax.ppermute(packs[d], "z", pairs)
    near = [
        jnp.stack([got[d] for d in shifts], axis=1).reshape(CAP, 8 * len(shifts), HEAD_DIM)
        for shifts in SHIFTS
    ]
    far, near_there = [], []
    for part in near:
        far.append(lax.ppermute(part, "xh", swap))
        near_there.append(lax.ppermute(part, "c", swap))
    here = near + far
    there = near_there + [lax.ppermute(part, "c", swap) for part in far]
    outs = {}
    shape = (BLOCK, GROUP * HEAD_DIM)
    for mask in (4, 0):
        results = pl.pallas_call(
            functools.partial(span_kernel, mask),
            out_shape=[jax.ShapeDtypeStruct(shape, bf)] * 4,
            in_specs=[SMEM] + [VMEM] * (1 + 4 * GROUPS),
            out_specs=[VMEM] * 4,
            scratch_shapes=KV_SCRATCH + [pltpu.VMEM((4,) + shape, bf)],
            compiler_params=room(24),
            cost_estimate=pl.CostEstimate(
                flops=1 << 30, bytes_accessed=1 << 21, transcendentals=1 << 20
            ),
        )(slots, members, *here, *there)
        for n, out in enumerate(results):
            step = mask ^ n
            pairs = [(m, m ^ step) for m in range(KV_HEADS)]
            outs[step] = lax.ppermute(out, HEAD_AXES, pairs) if step else out
    return [outs[step] for step in range(KV_HEADS)]


def join(outs, *unused):
    return pl.pallas_call(
        join_kernel,
        out_shape=jax.ShapeDtypeStruct((BLOCK, HEADS * HEAD_DIM), jnp.bfloat16),
        in_specs=[VMEM] * KV_HEADS,
        out_specs=HBM,
        scratch_shapes=[pltpu.SemaphoreType.DMA((KV_HEADS,))],
        compiler_params=pltpu.CompilerParams(vmem_limit_bytes=67043328),
    )(*outs)


def general(outs, chunks, bundle, token_block, ancestors):
    bf = jnp.bfloat16
    span_blocks = token_block.reshape(DEVICES, BLOCK)[:, 0]
    ids = jnp.arange(DEVICES, dtype=jnp.int32)
    span_of = jnp.sum(jnp.where(span_blocks[:, None] == ids[None, :], ids[:, None], 0), axis=0)
    lineage = ancestors[span_blocks]
    depth = jnp.sum((lineage >= 0).astype(jnp.int32), axis=1)
    spans = span_of[jnp.maximum(lineage, 0)]
    alive = lax.dynamic_slice_in_dim(depth - 1, lax.axis_index(AXES), 1)
    packed = pl.pallas_call(
        pick_kernel,
        out_shape=jax.ShapeDtypeStruct((DEVICES, SLOTS, 8, HEAD_DIM), bf),
        in_specs=[SMEM, VMEM],
    )(spans, chunks)
    got = lax.all_to_all(packed.reshape(DEVICES, SLOTS * 8, HEAD_DIM), AXES, 0, 0, tiled=True)
    got = got.reshape(8, 2, 4, 2, 2, SLOTS, 8, HEAD_DIM).transpose(1, 2, 4, 3, 5, 0, 6, 7)
    got = got.reshape(2, KV_HEADS, SLOTS * BLOCK, HEAD_DIM)
    far_k = pl.BlockSpec((None, None, SLOTS * BLOCK, HEAD_DIM), lambda h: (0, h, 0, 0))
    far_v = pl.BlockSpec((None, None, SLOTS * BLOCK, HEAD_DIM), lambda h: (1, h, 0, 0))
    return pl.pallas_call(
        head_kernel,
        grid=(KV_HEADS,),
        out_shape=jax.ShapeDtypeStruct((BLOCK, HEADS * HEAD_DIM), bf),
        in_specs=[SMEM, pl.BlockSpec((None, BLOCK, PACK), lambda h: (h, 0, 0)), far_k, far_v],
        out_specs=pl.BlockSpec((BLOCK, GROUP * HEAD_DIM), lambda h: (0, h)),
        scratch_shapes=KV_SCRATCH,
    )(alive, bundle, got, got)


def shards(queries, keys, values, ancestors, token_block, positions):
    bf, f32, i32 = jnp.bfloat16, jnp.float32, jnp.int32
    send, cosine, sine, own_k = pl.pallas_call(
        spread_kernel,
        out_shape=(
            jax.ShapeDtypeStruct((8, 2, 4, 2, 2, 8, HEAD_DIM), bf),
            jax.ShapeDtypeStruct((BLOCK, HEAD_DIM), f32),
            jax.ShapeDtypeStruct((BLOCK, HEAD_DIM), f32),
            jax.ShapeDtypeStruct((BLOCK, KV_HEADS * HEAD_DIM), bf),
        ),
        in_specs=[HBM, VMEM, HBM, HBM],
        scratch_shapes=[
            pltpu.VMEM((BLOCK, KV_HEADS * HEAD_DIM), bf),
            pltpu.SMEM((BLOCK,), i32),
            pltpu.SemaphoreType.DMA((3,)),
        ],
    )(positions, jnp.asarray(inverse_row()), keys, values)
    chunks = lax.all_to_all(send.reshape(DEVICES, 8, HEAD_DIM), AXES, 0, 0, tiled=True)
    table = pl.BlockSpec((BLOCK, HEAD_DIM), lambda h: (0, 0))
    head = pl.BlockSpec((BLOCK, HEAD_DIM), lambda h: (0, h))
    picks, slots, count = pl.pallas_call(
        plan_kernel,
        out_shape=(
            jax.ShapeDtypeStruct((CAP, PLANES), i32),
            jax.ShapeDtypeStruct((8, ANC_MAX), i32),
            jax.ShapeDtypeStruct((1, 1), i32),
        ),
        in_specs=[VMEM, VMEM],
        compiler_params=room(8),
        cost_estimate=pl.CostEstimate(flops=4 << 20, bytes_accessed=4 << 20, transcendentals=0),
    )(token_block.reshape(DEVICES, BLOCK), ancestors.T)
    bundle = pl.pallas_call(
        bundle_kernel,
        grid=(KV_HEADS,),
        out_shape=jax.ShapeDtypeStruct((KV_HEADS, BLOCK, PACK), bf),
        in_specs=[VMEM_ONE, table, table, pl.BlockSpec((BLOCK, GROUP * HEAD_DIM), lambda h: (0, h)), head, head],
        out_specs=pl.BlockSpec((None, BLOCK, PACK), lambda h: (h, 0, 0)),
        compiler_params=room(8),
        cost_estimate=pl.CostEstimate(flops=4 << 20, bytes_accessed=4 << 20, transcendentals=0),
    )(count, cosine, sine, queries, own_k, values)
    members = lax.all_to_all(bundle, HEAD_AXES, 0, 0, tiled=True)
    fits = count[0, 0] <= CAP
    outs = quick(picks, slots, chunks, members)
    return lax.cond(fits, join, general, outs, chunks, bundle, token_block, ancestors)


def solution(mesh):
    fine = Mesh(mesh.devices.reshape(8, 2, 4, 2, 2), AXES)
    rows = P(AXES, None)

    return jax.shard_map(
        shards,
        mesh=fine,
        in_specs=(rows, rows, rows, P(), P(), P()),
        out_specs=rows,
        check_vma=False,
    )
```

```python
import functools

import jax
import jax.numpy as jnp
import numpy as np
from jax import lax
from jax.experimental import pallas as pl
from jax.experimental.pallas import tpu as pltpu
from jax.sharding import Mesh
from jax.sharding import PartitionSpec as P


HEADS = 32
KV_HEADS = 8
GROUP = HEADS // KV_HEADS
HEAD_DIM = 128
BLOCK = 128
ANC_MAX = 8
SLOTS = ANC_MAX - 1
DEVICES = 256
PLANES = 8
CAP = 34
HALF = BLOCK // 2
REACH = 3
GROUPS = 2
KV_SCRATCH = [
    pltpu.VMEM((ANC_MAX * BLOCK, HEAD_DIM), jnp.bfloat16),
    pltpu.VMEM((ANC_MAX * BLOCK, 2 * HEAD_DIM), jnp.bfloat16),
]
PACK = (GROUP + 2) * HEAD_DIM
ROTARY_BASE = 500000.0
AXES = ("z", "c", "y", "xh", "xl")
HEAD_AXES = ("y", "xl")
NEG = -1e30
EXP2_SCALE = float(HEAD_DIM**-0.5 * np.log2(np.e))

HBM = pl.BlockSpec(memory_space=pltpu.HBM)
SMEM = pl.BlockSpec(memory_space=pltpu.SMEM)
VMEM = pl.BlockSpec(memory_space=pltpu.VMEM)
VMEM_ONE = pl.BlockSpec((1, 1), lambda h: (0, 0))


def room(mib):
    return pltpu.CompilerParams(vmem_limit_bytes=mib << 20)


def inverse_row():
    half = HEAD_DIM // 2
    inv = (ROTARY_BASE ** (-2.0 * np.arange(half, dtype=np.float64) / HEAD_DIM)).astype(np.float32)
    return np.concatenate([inv, inv])[None, :]


def turn(x, cosine, sine):
    x = x.astype(jnp.float32)
    return (x * cosine + pltpu.roll(x, HEAD_DIM // 2, 1) * sine).astype(jnp.bfloat16)


def device_index():
    z, c, y, xh, xl = [lax.axis_index(name) for name in AXES]
    return (((z * 2 + c) * 4 + y) * 2 + xh) * 2 + xl


def spread_kernel(
    pos_ref, inv_ref, k_hbm, v_hbm, send_ref, cos_ref, sin_ref, own_ref, v_ref, base_ref, sems
):
    start = pl.multiple_of(device_index() * BLOCK, BLOCK)
    loads = [
        pltpu.make_async_copy(pos_ref.at[pl.ds(start, BLOCK)], base_ref, sems.at[0]),
        pltpu.make_async_copy(k_hbm, own_ref, sems.at[1]),
        pltpu.make_async_copy(v_hbm, v_ref, sems.at[2]),
    ]
    for load in loads:
        load.start()
    loads[0].wait()
    rows = lax.broadcasted_iota(jnp.int32, (BLOCK, HEAD_DIM), 0) + base_ref[0]
    lanes = lax.broadcasted_iota(jnp.int32, (BLOCK, HEAD_DIM), 1)
    angles = rows.astype(jnp.float32) * inv_ref[...]
    cosine = jnp.cos(angles)
    sine = jnp.sin(angles)
    sine = jnp.where(lanes < HEAD_DIM // 2, -sine, sine)
    cos_ref[...] = cosine
    sin_ref[...] = sine
    loads[1].wait()
    loads[2].wait()
    for h in range(KV_HEADS):
        cols = slice(h * HEAD_DIM, (h + 1) * HEAD_DIM)
        turned = turn(own_ref[:, cols], cosine, sine)
        own_ref[:, cols] = turned
        plain = v_ref[:, cols]
        for high in range(2):
            for low in range(8):
                t = (high * 8 + low) * 8
                send_ref[low, 0, h // 2, high, h % 2] = turned[t : t + 8]
                send_ref[low, 1, h // 2, high, h % 2] = plain[t : t + 8]


def bundle_kernel(count_ref, cos_ref, sin_ref, q_ref, k_ref, v_ref, out_ref):
    for g in range(GROUP):
        cols = slice(g * HEAD_DIM, (g + 1) * HEAD_DIM)
        out_ref[:, cols] = turn(q_ref[:, cols], cos_ref[...], sin_ref[...])
    out_ref[:, GROUP * HEAD_DIM : (GROUP + 1) * HEAD_DIM] = k_ref[...]
    out_ref[:, (GROUP + 1) * HEAD_DIM :] = v_ref[...]


def plan_kernel(token_ref, anc_ref, picks_ref, slots_ref, count_ref):
    n = DEVICES
    f32, bf, i32 = jnp.float32, jnp.bfloat16, jnp.int32
    across = (((1,), (1,)), ((), ()))
    anc = anc_ref[...]
    col = token_ref[:, 0:1]
    lane = lax.broadcasted_iota(i32, (n, n), 1)
    sub = lax.broadcasted_iota(i32, (n, n), 0)
    row = jnp.sum(jnp.where(sub == lane, col, 0), axis=0, keepdims=True)
    depth = jnp.sum((anc >= 0).astype(i32), axis=0, keepdims=True)
    holds = jnp.zeros((n, n), f32)
    for j in range(SLOTS):
        entry = jnp.where(j < depth - 1, anc[j : j + 1], -1)
        holds = jnp.where(entry == col, 1.0, holds)
    block_at = (col == lane).astype(f32).astype(bf)
    plane8 = lax.broadcasted_iota(i32, (PLANES, n), 0)
    lane8 = lax.broadcasted_iota(i32, (PLANES, n), 1)
    in_plane = (lane8 // (n // PLANES) == plane8).astype(f32).astype(bf)
    blocks = jnp.dot(in_plane, block_at, preferred_element_type=f32)
    need = lax.dot_general(
        blocks.astype(bf), holds.astype(bf), across, preferred_element_type=f32
    )
    needed = (need > 0.5).astype(f32)
    upto = (sub <= lane).astype(f32).astype(bf)
    ranks = jnp.dot(needed.astype(bf), upto, preferred_element_type=f32)
    count_ref[...] = jnp.max(ranks, axis=(0, 1), keepdims=True).astype(i32)
    ranks = ranks - 1.0
    wanted = lax.broadcasted_iota(i32, (CAP, n), 0).astype(f32)
    span = lax.broadcasted_iota(i32, (CAP, n), 1).astype(f32)
    for z in range(PLANES):
        hit = (ranks[z : z + 1] == wanted) & (needed[z : z + 1] > 0.5)
        picks_ref[:, z : z + 1] = jnp.sum(
            jnp.where(hit, span, 0.0), axis=1, keepdims=True
        ).astype(i32)
    z, c, xh = lax.axis_index("z"), lax.axis_index("c"), lax.axis_index("xh")
    mine = z * 32 + c * 16 + (plane8 // 2) * 4 + xh * 2 + plane8 % 2
    own_block = jnp.dot(
        (lane8 == mine).astype(f32).astype(bf), block_at, preferred_element_type=f32
    )
    path = lax.dot_general(
        own_block.astype(bf), anc.astype(f32).astype(bf), across, preferred_element_type=f32
    ).astype(i32)
    my_rank = jnp.sum(jnp.where(plane8 == z, ranks, 0.0), axis=0, keepdims=True)
    for j in range(SLOTS):
        slot = jnp.sum(
            jnp.where(path[:, j : j + 1] == row, my_rank, 0.0), axis=1, keepdims=True
        ).astype(i32)
        slots_ref[:, j : j + 1] = jnp.clip(slot, 0, CAP - 1)
    slots_ref[:, SLOTS:] = jnp.sum((path >= 0).astype(i32), axis=1, keepdims=True) - 1


def pack_kernel(picks_ref, src_ref, own_ref, mid_ref, keep_ref, give_ref):
    z = lax.axis_index("z")
    side = 1 - 2 * lax.axis_index("c")
    targets = [(own_ref, None, z), (mid_ref, None, z + PLANES // 2)]
    for j in range(REACH):
        targets.append((keep_ref, j, z + side * (j + 1)))
        targets.append((give_ref, j, z - side * (j + 1)))
    for out_ref, j, target in targets:
        plane = lax.rem(target + PLANES, PLANES)
        out_ref = out_ref if j is None else out_ref.at[j]

        def one(k, carry):
            out_ref[k] = src_ref[picks_ref[k, plane]]
            return carry

        lax.fori_loop(0, CAP, one, 0, unroll=True)


def pick_kernel(idx_ref, src_ref, out_ref):
    def one(d, carry):
        for j in range(SLOTS):
            out_ref[d, j] = src_ref[idx_ref[d, j]]
        return carry

    lax.fori_loop(0, out_ref.shape[0], one, 0)


def attention(x_ref, k_ref, v_ref, alive, period, out_ref):
    k_ref[0:BLOCK] = x_ref[:, GROUP * HEAD_DIM : (GROUP + 1) * HEAD_DIM]
    v_ref[0:BLOCK, 0:HEAD_DIM] = x_ref[:, (GROUP + 1) * HEAD_DIM :]
    column = lax.broadcasted_iota(jnp.int32, (1, SLOTS * BLOCK), 1)
    bias = jnp.where((column // period) % SLOTS < alive, 0.0, NEG)
    row = lax.broadcasted_iota(jnp.int32, (BLOCK, BLOCK), 0)
    col = lax.broadcasted_iota(jnp.int32, (BLOCK, BLOCK), 1)
    causal = col <= row
    cols = [slice(g * HEAD_DIM, (g + 1) * HEAD_DIM) for g in range(GROUP)]
    scores = [
        lax.dot_general(
            x_ref[:, at], k_ref[...], (((1,), (1,)), ((), ())), preferred_element_type=jnp.float32
        )
        for at in cols
    ]
    scores = [
        jnp.concatenate([jnp.where(causal, s[:, :BLOCK], NEG), s[:, BLOCK:] + bias], axis=1)
        for s in scores
    ]
    tops = [jnp.max(s, axis=1, keepdims=True) for s in scores]
    weights = [
        jnp.exp2((s - top) * EXP2_SCALE).astype(jnp.bfloat16) for s, top in zip(scores, tops)
    ]
    for at, w in zip(cols, weights):
        mixed = jnp.dot(w, v_ref[...], preferred_element_type=jnp.float32)
        out_ref[:, at] = (mixed[:, :HEAD_DIM] / mixed[:, HEAD_DIM:]).astype(jnp.bfloat16)


def own_member():
    return lax.axis_index("y") * 2 + lax.axis_index("xl")


SAME_KIND = ((0, 0, 0, 24, 0), (0, 1, 0, 16, 24), (1, 0, 24, 16, 40), (1, 1, 16, 8, 56))
OTHER_KIND = (
    (1, 0, 0, 8, 0),
    (0, 0, 24, 16, 8),
    (0, 1, 16, 8, 24),
    (1, 1, 8, 8, 32),
    (1, 0, 8, 16, 40),
    (1, 1, 0, 8, 56),
)


def fill(k_ref, v_ref, slots_ref, m, here, there):
    def copy(dst_ref, plan):
        for j in range(SLOTS):
            slot = slots_ref[m, j]
            for half in range(2):
                at = (j + 1) * BLOCK + half * HALF
                for other, group, row, rows, to in plan:
                    part = (there if other else here)[half * GROUPS + group]
                    dst_ref[at + to : at + to + rows, 0:HEAD_DIM] = part[slot, row : row + rows]

    core = lax.axis_index("c")

    @pl.when(core == 0)
    def _():
        copy(k_ref, SAME_KIND)
        copy(v_ref, OTHER_KIND)

    @pl.when(core != 0)
    def _():
        copy(k_ref, OTHER_KIND)
        copy(v_ref, SAME_KIND)


def span_kernel(first, slots_ref, x_ref, *refs):
    here, there = refs[: 2 * GROUPS], refs[2 * GROUPS : 4 * GROUPS]
    out_refs, (k_ref, v_ref, done_ref) = refs[4 * GROUPS : -3], refs[-3:]
    v_ref[:, HEAD_DIM:] = jnp.ones((ANC_MAX * BLOCK, HEAD_DIM), jnp.bfloat16)

    def one(n, carry):
        m = own_member() ^ (n + first)
        fill(k_ref, v_ref, slots_ref, m, here, there)
        attention(x_ref.at[m], k_ref, v_ref, slots_ref[m, SLOTS], BLOCK, done_ref.at[n])
        return carry

    lax.fori_loop(0, len(out_refs), one, 0)
    for n, out_ref in enumerate(out_refs):
        out_ref[...] = done_ref[n]


def head_kernel(alive_ref, x_ref, far_k_ref, far_v_ref, out_ref, k_ref, v_ref):
    v_ref[:, HEAD_DIM:] = jnp.ones((ANC_MAX * BLOCK, HEAD_DIM), jnp.bfloat16)
    k_ref[BLOCK:] = far_k_ref[...]
    v_ref[BLOCK:, 0:HEAD_DIM] = far_v_ref[...]
    attention(x_ref, k_ref, v_ref, alive_ref[0], HALF, out_ref)


def join_kernel(*refs):
    out_ref, held_ref, sems = refs[-3:]
    width = GROUP * HEAD_DIM
    loads, stores = [], []
    for step in range(KV_HEADS):
        at = pl.multiple_of((own_member() ^ step) * width, width)
        held = held_ref.at[step]
        loads.append(pltpu.make_async_copy(refs[step], held, sems.at[0, step]))
        stores.append(pltpu.make_async_copy(held, out_ref.at[:, pl.ds(at, width)], sems.at[1, step]))
    for load in loads:
        load.start()
    for load, store in zip(loads, stores):
        load.wait()
        store.start()
    for store in stores:
        store.wait()


def quick(picks, slots, chunks, members):
    bf = jnp.bfloat16
    piece = (CAP, 8, HEAD_DIM)
    own, mid, keep, give = pl.pallas_call(
        pack_kernel,
        out_shape=[
            jax.ShapeDtypeStruct(piece, bf),
            jax.ShapeDtypeStruct(piece, bf),
            jax.ShapeDtypeStruct((REACH,) + piece, bf),
            jax.ShapeDtypeStruct((REACH,) + piece, bf),
        ],
        in_specs=[SMEM, VMEM],
        compiler_params=room(8),
    )(picks, chunks)
    swap = [(0, 1), (1, 0)]
    taken = lax.ppermute(give, "c", swap)
    mid = lax.ppermute(mid, "z", [(i, (i + 4) % PLANES) for i in range(PLANES)])
    came = []
    for j in range(REACH):
        pairs = [
            (z * 2 + c, (z + (1 - 2 * c) * (j + 1)) % PLANES * 2 + c)
            for z in range(PLANES)
            for c in range(2)
        ]
        came.append(lax.ppermute(jnp.stack([keep[j], taken[j]]), ("z", "c"), pairs))

    def rows(parts):
        return jnp.stack(parts, axis=1).reshape(CAP, 8 * len(parts), HEAD_DIM)

    near = [
        rows([own, came[0][0], came[1][0], came[0][1], came[1][1]]),
        rows([came[2][0], mid, came[2][1]]),
    ]
    far, near_there = [], []
    for part in near:
        far.append(lax.ppermute(part, "xh", swap))
        near_there.append(lax.ppermute(part, "c", swap))
    here = near + far
    there = near_there + [lax.ppermute(part, "c", swap) for part in far]
    outs = {}
    shape = (BLOCK, GROUP * HEAD_DIM)
    for first, count in ((4, 4), (1, 3), (0, 1)):
        results = pl.pallas_call(
            functools.partial(span_kernel, first),
            out_shape=[jax.ShapeDtypeStruct(shape, bf)] * count,
            in_specs=[SMEM] + [VMEM] * (1 + 4 * GROUPS),
            out_specs=[VMEM] * count,
            scratch_shapes=KV_SCRATCH + [pltpu.VMEM((count,) + shape, bf)],
            compiler_params=room(24),
            cost_estimate=pl.CostEstimate(
                flops=1 << 30, bytes_accessed=1 << 21, transcendentals=1 << 20
            ),
        )(slots, members, *here, *there)
        for n, out in enumerate(results):
            step = first + n
            pairs = [(m, m ^ step) for m in range(KV_HEADS)]
            outs[step] = lax.ppermute(out, HEAD_AXES, pairs) if step else out
    return [outs[step] for step in range(KV_HEADS)]


def join(outs, *unused):
    return pl.pallas_call(
        join_kernel,
        out_shape=jax.ShapeDtypeStruct((BLOCK, HEADS * HEAD_DIM), jnp.bfloat16),
        in_specs=[HBM] * KV_HEADS,
        out_specs=HBM,
        scratch_shapes=[
            pltpu.VMEM((KV_HEADS, BLOCK, GROUP * HEAD_DIM), jnp.bfloat16),
            pltpu.SemaphoreType.DMA((2, KV_HEADS)),
        ],
        compiler_params=pltpu.CompilerParams(vmem_limit_bytes=67043328),
    )(*outs)


def general(outs, chunks, bundle, token_block, ancestors):
    bf = jnp.bfloat16
    span_blocks = token_block.reshape(DEVICES, BLOCK)[:, 0]
    ids = jnp.arange(DEVICES, dtype=jnp.int32)
    span_of = jnp.sum(jnp.where(span_blocks[:, None] == ids[None, :], ids[:, None], 0), axis=0)
    lineage = ancestors[span_blocks]
    depth = jnp.sum((lineage >= 0).astype(jnp.int32), axis=1)
    spans = span_of[jnp.maximum(lineage, 0)]
    alive = lax.dynamic_slice_in_dim(depth - 1, lax.axis_index(AXES), 1)
    packed = pl.pallas_call(
        pick_kernel,
        out_shape=jax.ShapeDtypeStruct((DEVICES, SLOTS, 8, HEAD_DIM), bf),
        in_specs=[SMEM, VMEM],
    )(spans, chunks)
    got = lax.all_to_all(packed.reshape(DEVICES, SLOTS * 8, HEAD_DIM), AXES, 0, 0, tiled=True)
    got = got.reshape(8, 2, 4, 2, 2, SLOTS, 8, HEAD_DIM).transpose(1, 2, 4, 3, 5, 0, 6, 7)
    got = got.reshape(2, KV_HEADS, SLOTS * BLOCK, HEAD_DIM)
    far_k = pl.BlockSpec((None, None, SLOTS * BLOCK, HEAD_DIM), lambda h: (0, h, 0, 0))
    far_v = pl.BlockSpec((None, None, SLOTS * BLOCK, HEAD_DIM), lambda h: (1, h, 0, 0))
    return pl.pallas_call(
        head_kernel,
        grid=(KV_HEADS,),
        out_shape=jax.ShapeDtypeStruct((BLOCK, HEADS * HEAD_DIM), bf),
        in_specs=[SMEM, pl.BlockSpec((None, BLOCK, PACK), lambda h: (h, 0, 0)), far_k, far_v],
        out_specs=pl.BlockSpec((BLOCK, GROUP * HEAD_DIM), lambda h: (0, h)),
        scratch_shapes=KV_SCRATCH,
    )(alive, bundle, got, got)


def shards(queries, keys, values, ancestors, token_block, positions):
    bf, f32, i32 = jnp.bfloat16, jnp.float32, jnp.int32
    send, cosine, sine, own_k = pl.pallas_call(
        spread_kernel,
        out_shape=(
            jax.ShapeDtypeStruct((8, 2, 4, 2, 2, 8, HEAD_DIM), bf),
            jax.ShapeDtypeStruct((BLOCK, HEAD_DIM), f32),
            jax.ShapeDtypeStruct((BLOCK, HEAD_DIM), f32),
            jax.ShapeDtypeStruct((BLOCK, KV_HEADS * HEAD_DIM), bf),
        ),
        in_specs=[HBM, VMEM, HBM, HBM],
        scratch_shapes=[
            pltpu.VMEM((BLOCK, KV_HEADS * HEAD_DIM), bf),
            pltpu.SMEM((BLOCK,), i32),
            pltpu.SemaphoreType.DMA((3,)),
        ],
    )(positions, jnp.asarray(inverse_row()), keys, values)
    chunks = lax.all_to_all(send.reshape(DEVICES, 8, HEAD_DIM), AXES, 0, 0, tiled=True)
    table = pl.BlockSpec((BLOCK, HEAD_DIM), lambda h: (0, 0))
    head = pl.BlockSpec((BLOCK, HEAD_DIM), lambda h: (0, h))
    picks, slots, count = pl.pallas_call(
        plan_kernel,
        out_shape=(
            jax.ShapeDtypeStruct((CAP, PLANES), i32),
            jax.ShapeDtypeStruct((8, ANC_MAX), i32),
            jax.ShapeDtypeStruct((1, 1), i32),
        ),
        in_specs=[VMEM, VMEM],
        compiler_params=room(8),
        cost_estimate=pl.CostEstimate(flops=4 << 20, bytes_accessed=4 << 20, transcendentals=0),
    )(token_block.reshape(DEVICES, BLOCK), ancestors.T)
    bundle = pl.pallas_call(
        bundle_kernel,
        grid=(KV_HEADS,),
        out_shape=jax.ShapeDtypeStruct((KV_HEADS, BLOCK, PACK), bf),
        in_specs=[VMEM_ONE, table, table, pl.BlockSpec((BLOCK, GROUP * HEAD_DIM), lambda h: (0, h)), head, head],
        out_specs=pl.BlockSpec((None, BLOCK, PACK), lambda h: (h, 0, 0)),
        compiler_params=room(8),
        cost_estimate=pl.CostEstimate(flops=4 << 20, bytes_accessed=4 << 20, transcendentals=0),
    )(count, cosine, sine, queries, own_k, values)
    members = lax.all_to_all(bundle, HEAD_AXES, 0, 0, tiled=True)
    fits = count[0, 0] <= CAP
    outs = quick(picks, slots, chunks, members)
    return lax.cond(fits, join, general, outs, chunks, bundle, token_block, ancestors)


def solution(mesh):
    fine = Mesh(mesh.devices.reshape(8, 2, 4, 2, 2), AXES)
    rows = P(AXES, None)

    return jax.shard_map(
        shards,
        mesh=fine,
        in_specs=(rows, rows, rows, P(), P(), P()),
        out_specs=rows,
        check_vma=False,
    )
```

```python
import functools

import jax
import jax.numpy as jnp
import numpy as np
from jax import lax
from jax.experimental import pallas as pl
from jax.experimental.pallas import tpu as pltpu
from jax.sharding import Mesh
from jax.sharding import PartitionSpec as P


HEADS = 32
KV_HEADS = 8
GROUP = HEADS // KV_HEADS
HEAD_DIM = 128
BLOCK = 128
ANC_MAX = 8
SLOTS = ANC_MAX - 1
DEVICES = 256
PLANES = 8
CAP = 34
HALF = BLOCK // 2
REACH = 3
GROUPS = 2
KV_SCRATCH = [
    pltpu.VMEM((ANC_MAX * BLOCK, HEAD_DIM), jnp.bfloat16),
    pltpu.VMEM((ANC_MAX * BLOCK, 2 * HEAD_DIM), jnp.bfloat16),
]
PACK = (GROUP + 2) * HEAD_DIM
ROTARY_BASE = 500000.0
AXES = ("z", "c", "y", "xh", "xl")
HEAD_AXES = ("y", "xl")
NEG = -1e30
EXP2_SCALE = float(HEAD_DIM**-0.5 * np.log2(np.e))

HBM = pl.BlockSpec(memory_space=pltpu.HBM)
SMEM = pl.BlockSpec(memory_space=pltpu.SMEM)
VMEM = pl.BlockSpec(memory_space=pltpu.VMEM)


def room(mib):
    return pltpu.CompilerParams(vmem_limit_bytes=mib << 20)


def inverse_row():
    half = HEAD_DIM // 2
    inv = (ROTARY_BASE ** (-2.0 * np.arange(half, dtype=np.float64) / HEAD_DIM)).astype(np.float32)
    return np.concatenate([inv, inv])[None, :]


def turn(x, cosine, sine):
    x = x.astype(jnp.float32)
    return (x * cosine + pltpu.roll(x, HEAD_DIM // 2, 1) * sine).astype(jnp.bfloat16)


def device_index():
    z, c, y, xh, xl = [lax.axis_index(name) for name in AXES]
    return (((z * 2 + c) * 4 + y) * 2 + xh) * 2 + xl


def spread_kernel(
    pos_ref, inv_ref, k_hbm, v_hbm, send_ref, cos_ref, sin_ref, own_ref, v_ref, base_ref, sems
):
    start = pl.multiple_of(device_index() * BLOCK, BLOCK)
    loads = [
        pltpu.make_async_copy(pos_ref.at[pl.ds(start, BLOCK)], base_ref, sems.at[0]),
        pltpu.make_async_copy(k_hbm, own_ref, sems.at[1]),
        pltpu.make_async_copy(v_hbm, v_ref, sems.at[2]),
    ]
    for load in loads:
        load.start()
    loads[0].wait()
    rows = lax.broadcasted_iota(jnp.int32, (BLOCK, HEAD_DIM), 0) + base_ref[0]
    lanes = lax.broadcasted_iota(jnp.int32, (BLOCK, HEAD_DIM), 1)
    angles = rows.astype(jnp.float32) * inv_ref[...]
    cosine = jnp.cos(angles)
    sine = jnp.sin(angles)
    sine = jnp.where(lanes < HEAD_DIM // 2, -sine, sine)
    cos_ref[...] = cosine
    sin_ref[...] = sine
    loads[1].wait()
    loads[2].wait()
    for h in range(KV_HEADS):
        cols = slice(h * HEAD_DIM, (h + 1) * HEAD_DIM)
        turned = turn(own_ref[:, cols], cosine, sine)
        own_ref[:, cols] = turned
        plain = v_ref[:, cols]
        for high in range(2):
            for low in range(8):
                t = (high * 8 + low) * 8
                xl = h % 2 ^ high
                send_ref[low, 0, h // 2, high, xl] = turned[t : t + 8]
                send_ref[low, 1, h // 2, high, xl] = plain[t : t + 8]


def bundle_kernel(xh_ref, count_ref, cos_ref, sin_ref, q_ref, k_ref, v_ref, out_ref):
    for g in range(GROUP):
        cols = slice(g * HEAD_DIM, (g + 1) * HEAD_DIM)
        out_ref[:, cols] = turn(q_ref[:, cols], cos_ref[...], sin_ref[...])
    out_ref[:, GROUP * HEAD_DIM : (GROUP + 1) * HEAD_DIM] = k_ref[...]
    out_ref[:, (GROUP + 1) * HEAD_DIM :] = v_ref[...]


def plan_kernel(token_ref, anc_ref, picks_ref, slots_ref, count_ref):
    n = DEVICES
    f32, bf, i32 = jnp.float32, jnp.bfloat16, jnp.int32
    across = (((1,), (1,)), ((), ()))
    anc = anc_ref[...]
    col = token_ref[:, 0:1]
    lane = lax.broadcasted_iota(i32, (n, n), 1)
    sub = lax.broadcasted_iota(i32, (n, n), 0)
    row = jnp.sum(jnp.where(sub == lane, col, 0), axis=0, keepdims=True)
    depth = jnp.sum((anc >= 0).astype(i32), axis=0, keepdims=True)
    holds = jnp.zeros((n, n), f32)
    for j in range(SLOTS):
        entry = jnp.where(j < depth - 1, anc[j : j + 1], -1)
        holds = jnp.where(entry == col, 1.0, holds)
    block_at = (col == lane).astype(f32).astype(bf)
    plane8 = lax.broadcasted_iota(i32, (PLANES, n), 0)
    lane8 = lax.broadcasted_iota(i32, (PLANES, n), 1)
    in_plane = (lane8 // (n // PLANES) == plane8).astype(f32).astype(bf)
    blocks = jnp.dot(in_plane, block_at, preferred_element_type=f32)
    need = lax.dot_general(
        blocks.astype(bf), holds.astype(bf), across, preferred_element_type=f32
    )
    needed = (need > 0.5).astype(f32)
    upto = (sub <= lane).astype(f32).astype(bf)
    ranks = jnp.dot(needed.astype(bf), upto, preferred_element_type=f32)
    count_ref[...] = jnp.max(ranks, axis=(0, 1), keepdims=True).astype(i32)
    ranks = ranks - 1.0
    wanted = lax.broadcasted_iota(i32, (CAP, n), 0).astype(f32)
    span = lax.broadcasted_iota(i32, (CAP, n), 1).astype(f32)
    for z in range(PLANES):
        hit = (ranks[z : z + 1] == wanted) & (needed[z : z + 1] > 0.5)
        picks_ref[:, z : z + 1] = jnp.sum(
            jnp.where(hit, span, 0.0), axis=1, keepdims=True
        ).astype(i32)
    z, c, xh = lax.axis_index("z"), lax.axis_index("c"), lax.axis_index("xh")
    mine = z * 32 + c * 16 + (plane8 // 2) * 4 + xh * 2 + plane8 % 2
    own_block = jnp.dot(
        (lane8 == mine).astype(f32).astype(bf), block_at, preferred_element_type=f32
    )
    path = lax.dot_general(
        own_block.astype(bf), anc.astype(f32).astype(bf), across, preferred_element_type=f32
    ).astype(i32)
    my_rank = jnp.sum(jnp.where(plane8 == z, ranks, 0.0), axis=0, keepdims=True)
    for j in range(SLOTS):
        slot = jnp.sum(
            jnp.where(path[:, j : j + 1] == row, my_rank, 0.0), axis=1, keepdims=True
        ).astype(i32)
        slots_ref[:, j : j + 1] = jnp.clip(slot, 0, CAP - 1)
    slots_ref[:, SLOTS:] = jnp.sum((path >= 0).astype(i32), axis=1, keepdims=True) - 1


def pack_kernel(picks_ref, src_ref, own_ref, mid_ref, keep_ref, give_ref):
    z = lax.axis_index("z")
    side = 1 - 2 * lax.axis_index("c")
    targets = [(own_ref, None, z), (mid_ref, None, z + PLANES // 2)]
    for j in range(REACH):
        targets.append((keep_ref, j, z + side * (j + 1)))
        targets.append((give_ref, j, z - side * (j + 1)))
    for out_ref, j, target in targets:
        plane = lax.rem(target + PLANES, PLANES)
        out_ref = out_ref if j is None else out_ref.at[j]

        def one(k, carry):
            out_ref[k] = src_ref[picks_ref[k, plane]]
            return carry

        lax.fori_loop(0, CAP, one, 0, unroll=True)


def pick_kernel(idx_ref, src_ref, out_ref):
    def one(d, carry):
        for j in range(SLOTS):
            out_ref[d, j] = src_ref[idx_ref[d, j]]
        return carry

    lax.fori_loop(0, out_ref.shape[0], one, 0)


def attention(x_ref, k_ref, v_ref, alive, period, out_ref):
    k_ref[0:BLOCK] = x_ref[:, GROUP * HEAD_DIM : (GROUP + 1) * HEAD_DIM]
    v_ref[0:BLOCK, 0:HEAD_DIM] = x_ref[:, (GROUP + 1) * HEAD_DIM :]
    column = lax.broadcasted_iota(jnp.int32, (1, SLOTS * BLOCK), 1)
    bias = jnp.where((column // period) % SLOTS < alive, 0.0, NEG)
    row = lax.broadcasted_iota(jnp.int32, (BLOCK, BLOCK), 0)
    col = lax.broadcasted_iota(jnp.int32, (BLOCK, BLOCK), 1)
    causal = col <= row
    cols = [slice(g * HEAD_DIM, (g + 1) * HEAD_DIM) for g in range(GROUP)]
    scores = [
        lax.dot_general(
            x_ref[:, at], k_ref[...], (((1,), (1,)), ((), ())), preferred_element_type=jnp.float32
        )
        for at in cols
    ]
    scores = [
        jnp.concatenate([jnp.where(causal, s[:, :BLOCK], NEG), s[:, BLOCK:] + bias], axis=1)
        for s in scores
    ]
    tops = [jnp.max(s, axis=1, keepdims=True) for s in scores]
    weights = [
        jnp.exp2((s - top) * EXP2_SCALE).astype(jnp.bfloat16) for s, top in zip(scores, tops)
    ]
    for at, w in zip(cols, weights):
        mixed = jnp.dot(w, v_ref[...], preferred_element_type=jnp.float32)
        out_ref[:, at] = (mixed[:, :HEAD_DIM] / mixed[:, HEAD_DIM:]).astype(jnp.bfloat16)


def own_member():
    return lax.axis_index("y") * 2 + lax.axis_index("xl")


SAME_KIND = ((0, 0, 0, 24, 0), (0, 1, 0, 16, 24), (1, 0, 24, 16, 40), (1, 1, 16, 8, 56))
OTHER_KIND = (
    (1, 0, 0, 8, 0),
    (0, 0, 24, 16, 8),
    (0, 1, 16, 8, 24),
    (1, 1, 8, 8, 32),
    (1, 0, 8, 16, 40),
    (1, 1, 0, 8, 56),
)


def fill(k_ref, v_ref, slots_ref, m, here, there):
    def copy(dst_ref, plan):
        for j in range(SLOTS):
            slot = slots_ref[m, j]
            for half in range(2):
                at = (j + 1) * BLOCK + half * HALF
                for other, group, row, rows, to in plan:
                    part = (there if other else here)[half * GROUPS + group]
                    dst_ref[at + to : at + to + rows, 0:HEAD_DIM] = part[slot, row : row + rows]

    core = lax.axis_index("c")

    @pl.when(core == 0)
    def _():
        copy(k_ref, SAME_KIND)
        copy(v_ref, OTHER_KIND)

    @pl.when(core != 0)
    def _():
        copy(k_ref, OTHER_KIND)
        copy(v_ref, SAME_KIND)


def span_kernel(first, slots_ref, x_ref, *refs):
    here, there = refs[: 2 * GROUPS], refs[2 * GROUPS : 4 * GROUPS]
    out_refs, (k_ref, v_ref, done_ref) = refs[4 * GROUPS : -3], refs[-3:]
    v_ref[:, HEAD_DIM:] = jnp.ones((ANC_MAX * BLOCK, HEAD_DIM), jnp.bfloat16)

    def one(n, carry):
        m = own_member() ^ (n + first)
        fill(k_ref, v_ref, slots_ref, m, here, there)
        attention(x_ref.at[m], k_ref, v_ref, slots_ref[m, SLOTS], BLOCK, done_ref.at[n])
        return carry

    lax.fori_loop(0, len(out_refs), one, 0)
    for n, out_ref in enumerate(out_refs):
        out_ref[...] = done_ref[n]


def head_kernel(alive_ref, x_ref, far_k_ref, far_v_ref, out_ref, k_ref, v_ref):
    v_ref[:, HEAD_DIM:] = jnp.ones((ANC_MAX * BLOCK, HEAD_DIM), jnp.bfloat16)
    k_ref[BLOCK:] = far_k_ref[...]
    v_ref[BLOCK:, 0:HEAD_DIM] = far_v_ref[...]
    attention(x_ref, k_ref, v_ref, alive_ref[0], HALF, out_ref)


def join_kernel(*refs):
    out_ref, held_ref, sems = refs[-3:]
    width = GROUP * HEAD_DIM
    loads, stores = [], []
    for step in range(KV_HEADS):
        at = pl.multiple_of((own_member() ^ step ^ lax.axis_index("xh")) * width, width)
        held = held_ref.at[step]
        loads.append(pltpu.make_async_copy(refs[step], held, sems.at[0, step]))
        stores.append(pltpu.make_async_copy(held, out_ref.at[:, pl.ds(at, width)], sems.at[1, step]))
    for load in loads:
        load.start()
    for load, store in zip(loads, stores):
        load.wait()
        store.start()
    for store in stores:
        store.wait()


def quick(picks, slots, chunks, members):
    bf = jnp.bfloat16
    piece = (CAP, 8, HEAD_DIM)
    own, mid, keep, give = pl.pallas_call(
        pack_kernel,
        out_shape=[
            jax.ShapeDtypeStruct(piece, bf),
            jax.ShapeDtypeStruct(piece, bf),
            jax.ShapeDtypeStruct((REACH,) + piece, bf),
            jax.ShapeDtypeStruct((REACH,) + piece, bf),
        ],
        in_specs=[SMEM, VMEM],
        compiler_params=room(8),
    )(picks, chunks)
    swap = [(0, 1), (1, 0)]
    taken = lax.ppermute(give, "c", swap)
    mid = lax.ppermute(mid, "z", [(i, (i + 4) % PLANES) for i in range(PLANES)])
    came = []
    for j in range(REACH):
        pairs = [
            (z * 2 + c, (z + (1 - 2 * c) * (j + 1)) % PLANES * 2 + c)
            for z in range(PLANES)
            for c in range(2)
        ]
        came.append(lax.ppermute(jnp.stack([keep[j], taken[j]]), ("z", "c"), pairs))

    def rows(parts):
        return jnp.stack(parts, axis=1).reshape(CAP, 8 * len(parts), HEAD_DIM)

    near = [
        rows([own, came[0][0], came[1][0], came[0][1], came[1][1]]),
        rows([came[2][0], mid, came[2][1]]),
    ]
    far, near_there = [], []
    for part in near:
        far.append(lax.ppermute(part, ("xh", "xl"), [(x, 3 - x) for x in range(4)]))
        near_there.append(lax.ppermute(part, "c", swap))
    far[1], members = lax.optimization_barrier((far[1], members))
    here = near + far
    there = near_there + [lax.ppermute(part, "c", swap) for part in far]
    outs = {}
    shape = (BLOCK, GROUP * HEAD_DIM)
    for first, count in ((4, 4), (1, 3), (0, 1)):
        results = pl.pallas_call(
            functools.partial(span_kernel, first),
            out_shape=[jax.ShapeDtypeStruct(shape, bf)] * count,
            in_specs=[SMEM] + [VMEM] * (1 + 4 * GROUPS),
            out_specs=[VMEM] * count,
            scratch_shapes=KV_SCRATCH + [pltpu.VMEM((count,) + shape, bf)],
            compiler_params=room(24),
            cost_estimate=pl.CostEstimate(
                flops=1 << 30, bytes_accessed=1 << 21, transcendentals=1 << 20
            ),
        )(slots, members, *here, *there)
        for n, out in enumerate(results):
            step = first + n
            pairs = [(m, m ^ step) for m in range(KV_HEADS)]
            outs[step] = lax.ppermute(out, HEAD_AXES, pairs) if step else out
    return [outs[step] for step in range(KV_HEADS)]


def join(outs, *unused):
    return pl.pallas_call(
        join_kernel,
        out_shape=jax.ShapeDtypeStruct((BLOCK, HEADS * HEAD_DIM), jnp.bfloat16),
        in_specs=[HBM] * KV_HEADS,
        out_specs=HBM,
        scratch_shapes=[
            pltpu.VMEM((KV_HEADS, BLOCK, GROUP * HEAD_DIM), jnp.bfloat16),
            pltpu.SemaphoreType.DMA((2, KV_HEADS)),
        ],
        compiler_params=pltpu.CompilerParams(vmem_limit_bytes=67043328),
    )(*outs)


def general(outs, chunks, bundle, token_block, ancestors):
    bf = jnp.bfloat16
    span_blocks = token_block.reshape(DEVICES, BLOCK)[:, 0]
    ids = jnp.arange(DEVICES, dtype=jnp.int32)
    span_of = jnp.sum(jnp.where(span_blocks[:, None] == ids[None, :], ids[:, None], 0), axis=0)
    lineage = ancestors[span_blocks]
    depth = jnp.sum((lineage >= 0).astype(jnp.int32), axis=1)
    spans = span_of[jnp.maximum(lineage, 0)]
    alive = lax.dynamic_slice_in_dim(depth - 1, lax.axis_index(AXES), 1)
    packed = pl.pallas_call(
        pick_kernel,
        out_shape=jax.ShapeDtypeStruct((DEVICES, SLOTS, 8, HEAD_DIM), bf),
        in_specs=[SMEM, VMEM],
    )(spans, chunks)
    got = lax.all_to_all(packed.reshape(DEVICES, SLOTS * 8, HEAD_DIM), AXES, 0, 0, tiled=True)
    got = got.reshape(8, 2, 4, 2, 2, SLOTS, 8, HEAD_DIM)
    got = jnp.stack([got[:, :, :, 0], got[:, :, :, 1, ::-1]], axis=3)
    got = got.transpose(1, 2, 4, 3, 5, 0, 6, 7)
    got = got.reshape(2, KV_HEADS, SLOTS * BLOCK, HEAD_DIM)
    pairs = bundle.reshape(KV_HEADS // 2, 2, BLOCK, PACK)
    pairs = jnp.where(lax.axis_index("xh") == 0, pairs, pairs[:, ::-1])
    bundle = pairs.reshape(bundle.shape)
    far_k = pl.BlockSpec((None, None, SLOTS * BLOCK, HEAD_DIM), lambda h: (0, h, 0, 0))
    far_v = pl.BlockSpec((None, None, SLOTS * BLOCK, HEAD_DIM), lambda h: (1, h, 0, 0))
    return pl.pallas_call(
        head_kernel,
        grid=(KV_HEADS,),
        out_shape=jax.ShapeDtypeStruct((BLOCK, HEADS * HEAD_DIM), bf),
        in_specs=[SMEM, pl.BlockSpec((None, BLOCK, PACK), lambda h: (h, 0, 0)), far_k, far_v],
        out_specs=pl.BlockSpec((BLOCK, GROUP * HEAD_DIM), lambda h: (0, h)),
        scratch_shapes=KV_SCRATCH,
    )(alive, bundle, got, got)


def shards(queries, keys, values, ancestors, token_block, positions):
    bf, f32, i32 = jnp.bfloat16, jnp.float32, jnp.int32
    send, cosine, sine, own_k = pl.pallas_call(
        spread_kernel,
        out_shape=(
            jax.ShapeDtypeStruct((8, 2, 4, 2, 2, 8, HEAD_DIM), bf),
            jax.ShapeDtypeStruct((BLOCK, HEAD_DIM), f32),
            jax.ShapeDtypeStruct((BLOCK, HEAD_DIM), f32),
            jax.ShapeDtypeStruct((BLOCK, KV_HEADS * HEAD_DIM), bf),
        ),
        in_specs=[HBM, VMEM, HBM, HBM],
        scratch_shapes=[
            pltpu.VMEM((BLOCK, KV_HEADS * HEAD_DIM), bf),
            pltpu.SMEM((BLOCK,), i32),
            pltpu.SemaphoreType.DMA((3,)),
        ],
    )(positions, jnp.asarray(inverse_row()), keys, values)
    chunks = lax.all_to_all(send.reshape(DEVICES, 8, HEAD_DIM), AXES, 0, 0, tiled=True)
    table = pl.BlockSpec((BLOCK, HEAD_DIM), lambda h, xh: (0, 0))
    head = pl.BlockSpec((BLOCK, HEAD_DIM), lambda h, xh: (0, h))
    one = pl.BlockSpec((1, 1), lambda h, xh: (0, 0))
    heads = pl.BlockSpec((BLOCK, GROUP * HEAD_DIM), lambda h, xh: (0, h))
    picks, slots, count = pl.pallas_call(
        plan_kernel,
        out_shape=(
            jax.ShapeDtypeStruct((CAP, PLANES), i32),
            jax.ShapeDtypeStruct((8, ANC_MAX), i32),
            jax.ShapeDtypeStruct((1, 1), i32),
        ),
        in_specs=[VMEM, VMEM],
        compiler_params=room(8),
        cost_estimate=pl.CostEstimate(flops=4 << 20, bytes_accessed=4 << 20, transcendentals=0),
    )(token_block.reshape(DEVICES, BLOCK), ancestors.T)
    bundle = pl.pallas_call(
        bundle_kernel,
        grid_spec=pltpu.PrefetchScalarGridSpec(
            num_scalar_prefetch=1,
            grid=(KV_HEADS,),
            in_specs=[one, table, table, heads, head, head],
            out_specs=pl.BlockSpec((None, BLOCK, PACK), lambda h, xh: (h ^ xh[0], 0, 0)),
        ),
        out_shape=jax.ShapeDtypeStruct((KV_HEADS, BLOCK, PACK), bf),
        compiler_params=room(8),
        cost_estimate=pl.CostEstimate(flops=4 << 20, bytes_accessed=4 << 20, transcendentals=0),
    )(lax.axis_index("xh").astype(i32)[None], count, cosine, sine, queries, own_k, values)
    members = lax.all_to_all(bundle, HEAD_AXES, 0, 0, tiled=True)
    fits = count[0, 0] <= CAP
    outs = quick(picks, slots, chunks, members)
    return lax.cond(fits, join, general, outs, chunks, bundle, token_block, ancestors)


def solution(mesh):
    fine = Mesh(mesh.devices.reshape(8, 2, 4, 2, 2), AXES)
    rows = P(AXES, None)

    return jax.shard_map(
        shards,
        mesh=fine,
        in_specs=(rows, rows, rows, P(), P(), P()),
        out_specs=rows,
        check_vma=False,
    )
```
